32 devices in a mesh: dp: 16 (over z, y, x), tile: 2 (over core).
Axes of the slice: x: 2, y: 2, z: 4, core: 2. Of those that a mesh axis runs over, the one named last changes fastest.
Arguments:
- patches: bfloat16 [64, 256, 16], P('dp', 'tile'), may hold values from -6 to 6
- bucket: int32 [64], P('dp'), may hold values from 0 to 2
- keep_order: int32 [64, 256], P('dp'), may hold values from 0 to 255, each once within a row
- timesteps: int32 [64], P('dp'), may hold values from 0 to 999
- labels: int32 [64], P('dp'), may hold values from 0 to 999
- patch_weight: bfloat16 [16, 1152], replicated, may hold values from -1.5 to 1.5
- patch_bias: bfloat16 [1152], replicated, may hold values from -1.75 to 1.75
- class_table: bfloat16 [1000, 1152], replicated, may hold values from -6 to 6
- ada_weight: bfloat16 [1152, 6912], P(None, 'tile'), may hold values from -0.1875 to 0.1875
- ada_bias: bfloat16 [6912], P('tile'), may hold values from -1.75 to 1.75
- qkv_weight: bfloat16 [1152, 3456], replicated, may hold values from -0.1875 to 0.1875
- query_bias: bfloat16 [1152], replicated, may hold values from -1.75 to 1.75
- value_bias: bfloat16 [1152], replicated, may hold values from -1.75 to 1.75
- proj_weight: bfloat16 [1152, 1152], replicated, may hold values from -0.5 to 0.5
- proj_bias: bfloat16 [1152], replicated, may hold values from -1.75 to 1.75
- up_weight: bfloat16 [1152, 4608], replicated, may hold values from -0.1875 to 0.1875
- up_bias: bfloat16 [4608], replicated, may hold values from -1.75 to 1.75
- down_weight: bfloat16 [4608, 1152], replicated, may hold values from -0.09375 to 0.09375
- down_bias: bfloat16 [1152], replicated, may hold values from -1.75 to 1.75
- final_weight: bfloat16 [1152, 16], replicated, may hold values from -0.1875 to 0.1875
- final_bias: bfloat16 [16], replicated, may hold values from -1.75 to 1.75
- out_grad: bfloat16 [64, 256, 16], P('dp', 'tile'), may hold values from -6 to 6
Outputs:
- denoised: float32 [64, 256, 16], P('dp', 'tile')
- patch_grad: float32 [64, 256, 16], P('dp', 'tile')
- patch_weight_grad: float32 [16, 1152], replicated
- patch_bias_grad: float32 [1152], replicated
- class_table_grad: float32 [1000, 1152], replicated
- ada_weight_grad: float32 [1152, 6912], P('dp', 'tile')
- ada_bias_grad: float32 [6912], replicated
- qkv_weight_grad: float32 [1152, 3456], P('dp', 'tile')
- query_bias_grad: float32 [1152], replicated
- value_bias_grad: float32 [1152], replicated
- proj_weight_grad: float32 [1152, 1152], P('dp', 'tile')
- proj_bias_grad: float32 [1152], replicated
- up_weight_grad: float32 [1152, 4608], P('dp', 'tile')
- up_bias_grad: float32 [4608], replicated
- down_weight_grad: float32 [4608, 1152], P('dp', 'tile')
- down_bias_grad: float32 [1152], replicated
- final_weight_grad: float32 [1152, 16], replicated
- final_bias_grad: float32 [16], replicated
- token_counts: float32 [2], replicated
The draws below stay inside these ranges and needn't reach their ends.
Inputs may be any that keep to these rules, and one draw needn't show every extreme that they name: `bucket`: 0, 1, 2 stand for token grids of 16 x 16, 12 x 20 and 20 x 12. `keep_order`: each row holds every slot number once.
All inputs are finite; a program needn't handle non-finite values.
Results may differ from the reference program's by a relative error of at most 0.015.
Values sent between devices are 32-bit elements; how exact they have to be, the bound alone decides.
No kernel may reach another device: no remote copies, remote signals or barrier semaphores. Data moves between devices by JAX's collectives and lax.ppermute only.
A program may use at most 384 MiB of HBM per device.

```python
import math
import jax
import jax.numpy as jnp
from jax import lax

D = 1152
HEADS = 16
FF = 4608
CLASSES = 1000
PATCH_DIM = 16
SLOTS = 256
IMAGES = 64


def with_ends(values, rng, least, high):
    shape = values.shape
    place = [jax.random.randint(jax.random.fold_in(rng, axis), (), 0, shape[axis]) for axis in range(len(shape))]
    values = values.at[tuple(place)].set(least)
    longest = shape.index(max(shape))
    place[longest] = (place[longest] + 1) % shape[longest]
    return values.at[tuple(place)].set(high)


def block_levels(own_key, shape, cuts, low, high):
    factor_of = 1.0
    for dim, blocks in cuts:
        heights = jax.random.uniform(jax.random.fold_in(jax.random.fold_in(own_key, 6), dim), (blocks,), jnp.float32, low / len(cuts), high / len(cuts))
        factor_of = factor_of * jnp.repeat(jnp.exp(heights), shape[dim] // blocks).reshape((-1,) + (1,) * (len(shape) - 1 - dim))
    return factor_of


def gaussian(rng, extent, spread, reach, pieces=(), kind=jnp.bfloat16):
    gain = block_levels(rng, extent, pieces, -0.22, 0.18) if pieces else 1.0
    drawn = jax.random.normal(rng, extent, jnp.float32) * spread * gain
    return jnp.minimum(jnp.maximum(drawn, -reach), reach).astype(kind)


def setup_inputs(seed: int = 0) -> dict:
    key_list = jax.random.split(jax.random.key(seed), 23)
    return {
        "patches": gaussian(key_list[0], (IMAGES, SLOTS, PATCH_DIM), 1.0, 6.0, ((0, 16), (1, 2))),
        "bucket": with_ends(jax.random.randint(key_list[1], (IMAGES,), 0, 3), jax.random.fold_in(key_list[1], 1), 0, 2).astype(jnp.int32),
        "keep_order": jax.vmap(lambda own: jax.random.permutation(own, SLOTS))(jax.random.split(key_list[2], IMAGES)).reshape((IMAGES, SLOTS)).astype(jnp.int32),
        "timesteps": with_ends(jax.random.randint(key_list[3], (IMAGES,), 0, 1000), jax.random.fold_in(key_list[3], 1), 0, 999).astype(jnp.int32),
        "labels": with_ends(jax.random.randint(key_list[4], (IMAGES,), 0, CLASSES), jax.random.fold_in(key_list[4], 1), 0, CLASSES - 1).astype(jnp.int32),
        "patch_weight": gaussian(key_list[5], (PATCH_DIM, D), PATCH_DIM ** -0.5, 1.5),
        "patch_bias": gaussian(key_list[6], (D,), 0.3, 1.75),
        "class_table": gaussian(key_list[7], (CLASSES, D), 1.0, 6.0),
        "ada_weight": gaussian(key_list[8], (D, 6 * D), D ** -0.5, 0.1875, ((1, 2),)),
        "ada_bias": gaussian(key_list[9], (6 * D,), 0.3, 1.75, ((0, 2),)),
        "qkv_weight": gaussian(key_list[10], (D, 3 * D), D ** -0.5, 0.1875),
        "query_bias": gaussian(key_list[11], (D,), 0.3, 1.75),
        "value_bias": gaussian(key_list[12], (D,), 0.3, 1.75),
        "proj_weight": gaussian(key_list[13], (D, D), (D // 8) ** -0.5, 0.5),
        "proj_bias": gaussian(key_list[14], (D,), 0.3, 1.75),
        "up_weight": gaussian(key_list[15], (D, FF), D ** -0.5, 0.1875),
        "up_bias": gaussian(key_list[16], (FF,), 0.3, 1.75),
        "down_weight": gaussian(key_list[17], (FF, D), FF ** -0.5, 0.09375),
        "down_bias": gaussian(key_list[18], (D,), 0.3, 1.75),
        "final_weight": gaussian(key_list[19], (D, PATCH_DIM), D ** -0.5, 0.1875),
        "final_bias": gaussian(key_list[20], (PATCH_DIM,), 0.3, 1.75),
        "out_grad": gaussian(key_list[21], (IMAGES, SLOTS, PATCH_DIM), 1.0, 6.0, ((0, 16), (1, 2))),
    }


@jax.custom_vjp
def low(v):
    return lax.optimization_barrier(v.astype(jnp.bfloat16)).astype(jnp.float32)

@jax.custom_vjp
def low_back(v):
    return v

def low_keep(v):
    return (low(v), None)

def low_pass(kept, grad):
    return (grad,)

def back_keep(v):
    return (v, None)

def back_low(kept, grad):
    return (low(grad),)
low.defvjp(low_keep, low_pass)
low_back.defvjp(back_keep, back_low)
epsilon = 1e-06
highest = lax.Precision.HIGHEST

def layer_norm(values):
    center = values - lax.optimization_barrier(jnp.mean(values, axis=-1, keepdims=True))
    return center * lax.rsqrt(lax.optimization_barrier(jnp.mean(center * center, axis=-1, keepdims=True)) + epsilon)

def gelu_tanh(values):
    return 0.5 * values * (1.0 + jnp.tanh(0.7978845608028654 * (values + 0.044715 * values * values * values)))

def geometry(bucket, slot_ids, tile_slots):
    half_rows = jnp.where(bucket == 0, 8, jnp.where(bucket == 1, 6, 10)).astype(jnp.int32)[:, None]
    columns = jnp.where(bucket == 0, 16, jnp.where(bucket == 1, 20, 12)).astype(jnp.int32)[:, None]
    tile_ids = (slot_ids // tile_slots)[None, :]
    local_ids = (slot_ids % tile_slots)[None, :]
    is_valid = local_ids < half_rows * columns
    return (is_valid, tile_ids * half_rows + local_ids // columns, local_ids % columns)

def axis_embed(positions, half_width):
    quarter = half_width // 2
    omega = jnp.exp(-math.log(10000.0) * jnp.arange(quarter, dtype=jnp.float32) / quarter)
    angles = positions.astype(jnp.float32)[..., None] * omega
    return jnp.concatenate([jnp.sin(angles), jnp.cos(angles)], axis=-1)

def position_embed(rowpos, colpos, model_width):
    return jnp.concatenate([axis_embed(rowpos, model_width // 2), axis_embed(colpos, model_width // 2)], axis=-1)

def time_embed(timesteps, model_width):
    half_width = model_width // 2
    freqs = jnp.exp(-math.log(10000.0) * jnp.arange(half_width, dtype=jnp.float32) / half_width)
    angles = timesteps.astype(jnp.float32)[:, None] * freqs
    return jnp.concatenate([jnp.cos(angles), jnp.sin(angles)], axis=-1)

def keep_mask(keep_order, is_valid):
    slot_total = keep_order.shape[1]
    slot_ids = jnp.arange(slot_total, dtype=jnp.int32)
    placed = lax.optimization_barrier(jnp.sum(jnp.where(keep_order[:, :, None] == slot_ids[None, None, :], slot_ids[None, :, None], 0), axis=1)).astype(jnp.int32)
    earlier = (placed[:, :, None] < placed[:, None, :]) & is_valid[:, :, None]
    rank_of = lax.optimization_barrier(jnp.sum(earlier.astype(jnp.int32), axis=1)).astype(jnp.int32)
    keep_limit = (lax.optimization_barrier(jnp.sum(is_valid.astype(jnp.int32), axis=1)) // 2).astype(jnp.int32)
    return (is_valid & (rank_of < keep_limit[:, None]), rank_of, keep_limit)

def group_forward(weights, pixels, bucket, keep_order, timesteps, labels):
    patch_weight, patch_bias, class_table, ada_weight, ada_bias, qkv_weight, query_bias, value_bias, proj_weight, proj_bias, up_weight, up_bias, down_weight, down_bias, final_weight, final_bias = weights
    model_width = patch_weight.shape[1]
    slot_ids = jnp.arange(SLOTS, dtype=jnp.int32)
    is_valid, rowpos, colpos = geometry(bucket, slot_ids, SLOTS // 2)
    kept, _, _ = keep_mask(keep_order, is_valid)
    embedded = low_back(jnp.einsum('isp,pd->isd', pixels, patch_weight, precision=highest) + patch_bias + position_embed(rowpos, colpos, model_width))
    condition = time_embed(timesteps, model_width) + jnp.take(class_table, labels, axis=0)
    modulation = low_back(jnp.dot(low(jax.nn.silu(condition)), ada_weight, precision=highest) + ada_bias)
    shift_a, scale_a, gate_a, shift_m, scale_m, gate_m = [portion[:, None, :] for portion in jnp.split(modulation, 6, axis=1)]
    attn_in = low(layer_norm(embedded) * (1.0 + scale_a) + shift_a)
    queries = low(low_back(jnp.einsum('isd,de->ise', attn_in, qkv_weight[:, :model_width], precision=highest) + query_bias))
    keys = low(low_back(jnp.einsum('isd,de->ise', attn_in, qkv_weight[:, model_width:2 * model_width], precision=highest)))
    values = low(low_back(jnp.einsum('isd,de->ise', attn_in, qkv_weight[:, 2 * model_width:], precision=highest) + value_bias))
    group_size, slot_total = embedded.shape[:2]
    head_size = model_width // HEADS
    query_heads = queries.reshape(group_size, slot_total, HEADS, head_size)
    key_heads = keys.reshape(group_size, slot_total, HEADS, head_size)
    value_heads = values.reshape(group_size, slot_total, HEADS, head_size)
    scores = low_back(jnp.einsum('gqhd,gkhd->ghqk', query_heads, key_heads, precision=highest) * head_size ** (-0.5))
    scores = jnp.where(kept[:, None, None, :], scores, -jnp.inf)
    maximum = lax.optimization_barrier(jnp.max(scores, axis=-1, keepdims=True))
    powers = jnp.exp(scores - maximum)
    probabilities = low(powers / lax.optimization_barrier(jnp.sum(powers, axis=-1, keepdims=True)))
    mixed = low(low_back(jnp.einsum('ghqk,gkhd->gqhd', probabilities, value_heads, precision=highest).reshape(group_size, slot_total, model_width)))
    attn_out = low_back(jnp.einsum('isd,de->ise', mixed, proj_weight, precision=highest) + proj_bias)
    middle = embedded + gate_a * attn_out
    mlp_in = low(layer_norm(middle) * (1.0 + scale_m) + shift_m)
    pre_act = low_back(jnp.einsum('isd,df->isf', mlp_in, up_weight, precision=highest) + up_bias)
    activated = low(gelu_tanh(pre_act))
    mlp_out = low_back(jnp.einsum('isf,fd->isd', activated, down_weight, precision=highest) + down_bias)
    block_out = middle + gate_m * mlp_out
    merged = jnp.where(kept[:, :, None], block_out, embedded)
    final_in = low(layer_norm(merged))
    return (jnp.einsum('isd,dp->isp', final_in, final_weight, precision=highest) + final_bias) * is_valid[:, :, None]

def reference(patches, bucket, keep_order, timesteps, labels, patch_weight, patch_bias, class_table, ada_weight, ada_bias, qkv_weight, query_bias, value_bias, proj_weight, proj_bias, up_weight, up_bias, down_weight, down_bias, final_weight, final_bias, out_grad):
    weights = tuple((entry.astype(jnp.float32) for entry in (patch_weight, patch_bias, class_table, ada_weight, ada_bias, qkv_weight, query_bias, value_bias, proj_weight, proj_bias, up_weight, up_bias, down_weight, down_bias, final_weight, final_bias)))
    group_size = math.gcd(IMAGES, 16)

    def shaped(tensor):
        return tensor.reshape((IMAGES // group_size, group_size) + tensor.shape[1:])

    def forward(params, pixels):

        def one_group(inputs):
            return group_forward(params, *inputs)
        result = lax.map(jax.checkpoint(one_group), (shaped(pixels), shaped(bucket), shaped(keep_order), shaped(timesteps), shaped(labels)))
        return result.reshape(IMAGES, SLOTS, PATCH_DIM)
    denoised, pullback = jax.vjp(forward, weights, patches.astype(jnp.float32))
    grad_weights, patch_grad = pullback(out_grad.astype(jnp.float32))
    patch_weight_grad, patch_bias_grad, class_table_grad, ada_weight_grad, ada_bias_grad, qkv_weight_grad, query_bias_grad, value_bias_grad, proj_weight_grad, proj_bias_grad, up_weight_grad, up_bias_grad, down_weight_grad, down_bias_grad, final_weight_grad, final_bias_grad = grad_weights
    is_valid, _, _ = geometry(bucket, jnp.arange(SLOTS, dtype=jnp.int32), SLOTS // 2)
    valid_count = lax.optimization_barrier(jnp.sum(is_valid.astype(jnp.int32), axis=1))
    kept_total = jnp.sum((valid_count // 2).astype(jnp.float32))
    valid_total = jnp.sum(valid_count.astype(jnp.float32))
    token_counts = jnp.stack([kept_total, valid_total])
    return (denoised, patch_grad, patch_weight_grad, patch_bias_grad, class_table_grad, ada_weight_grad, ada_bias_grad, qkv_weight_grad, query_bias_grad, value_bias_grad, proj_weight_grad, proj_bias_grad, up_weight_grad, up_bias_grad, down_weight_grad, down_bias_grad, final_weight_grad, final_bias_grad, token_counts)
```

```python
import math

import jax
import jax.numpy as jnp
import numpy as np
from jax import lax
from jax.sharding import PartitionSpec as P

HEADS = 16
GRID_MAX = 32
epsilon = 1e-06
highest = lax.Precision.HIGHEST
f32 = jnp.float32
bf16 = jnp.bfloat16


def mm(spec, left, right):
    return jnp.einsum(spec, left, right, preferred_element_type=f32)


def norm_stats(values):
    center = values - jnp.mean(values, axis=-1, keepdims=True)
    rstd = lax.rsqrt(jnp.mean(center * center, axis=-1, keepdims=True) + epsilon)
    return center * rstd, rstd


def norm_back(normed, rstd, grad):
    return rstd * (
        grad
        - jnp.mean(grad, axis=-1, keepdims=True)
        - normed * jnp.mean(grad * normed, axis=-1, keepdims=True)
    )


def gelu_parts(u):
    inner = 0.7978845608028654 * (u + 0.044715 * u * u * u)
    th = jnp.tanh(inner)
    value = 0.5 * u * (1.0 + th)
    slope = 0.5 * (1.0 + th) + 0.5 * u * (1.0 - th * th) * 0.7978845608028654 * (
        1.0 + 3.0 * 0.044715 * u * u
    )
    return value, slope


def split_heads(tensor):
    return tensor.reshape(tensor.shape[0], tensor.shape[1], HEADS, tensor.shape[2] // HEADS)


def three_way(table):
    parts = []
    rest = table
    for _ in range(3):
        piece = rest.astype(bf16)
        parts.append(piece)
        rest = rest - piece.astype(f32)
    return parts


def axis_table(width):
    quarter = width // 2
    omega = jnp.exp(-math.log(10000.0) * jnp.arange(quarter, dtype=f32) / quarter)
    angles = jnp.arange(GRID_MAX, dtype=f32)[:, None] * omega[None, :]
    return jnp.concatenate([jnp.sin(angles), jnp.cos(angles)], axis=-1)


def time_embed(timesteps, model_width):
    half = model_width // 2
    freqs = jnp.exp(-math.log(10000.0) * jnp.arange(half, dtype=f32) / half)
    angles = timesteps.astype(f32)[:, None] * freqs
    return jnp.concatenate([jnp.cos(angles), jnp.sin(angles)], axis=-1)


def swap_tiles(value):
    return lax.ppermute(value, "tile", [(0, 1), (1, 0)])


def flip_bit(value, bit, count):
    return lax.ppermute(value, "dp", [(d, d ^ (1 << bit)) for d in range(count)])


def relative_masks(order):
    bits = len(order)
    masks = []
    for rel in range(1 << bits):
        mask = 0
        for stage in range(bits):
            if (rel >> (bits - 1 - stage)) & 1:
                mask |= 1 << order[stage]
        masks.append(mask)
    return masks


class Halving:
    def __init__(self, blocks, order, count):
        self.blocks = blocks
        self.order = order
        self.count = count
        index = lax.axis_index("dp")
        self.ids = [index ^ mask for mask in relative_masks(order)]
        self.received = []

    def gather(self, low, high):
        return jnp.stack(
            [
                lax.dynamic_index_in_dim(self.blocks, self.ids[k], 0, keepdims=False)
                for k in range(low, high)
            ]
        )

    def step(self):
        stage = len(self.received)
        low = 1 << (len(self.order) - 1 - stage)
        message = self.gather(low, 2 * low)
        for piece in self.received:
            message = message + piece[low : 2 * low]
        self.received.append(flip_bit(message, self.order[stage], self.count))

    def result(self):
        while len(self.received) < len(self.order):
            self.step()
        total = self.gather(0, 1)
        for piece in self.received:
            total = total + piece[0:1]
        return total[0]


def all_sum(value, bits, count):
    value = value + swap_tiles(value)
    for bit in range(bits):
        value = value + flip_bit(value, bit, count)
    return value


def all_collect(value, bits, count):
    value = value[None]
    for bit in range(bits):
        value = jnp.concatenate([value, flip_bit(value, bit, count)], axis=0)
    return value


def body(
    patches,
    bucket,
    keep_order,
    timesteps,
    labels,
    patch_weight,
    patch_bias,
    class_table,
    ada_weight,
    ada_bias,
    qkv_weight,
    query_bias,
    value_bias,
    proj_weight,
    proj_bias,
    up_weight,
    up_bias,
    down_weight,
    down_bias,
    final_weight,
    final_bias,
    out_grad,
):
    images, tile_slots, patch_width = patches.shape
    slot_total = keep_order.shape[1]
    width = patch_weight.shape[1]
    hidden = up_weight.shape[1]
    class_count = class_table.shape[0]
    count = lax.axis_size("dp")
    bits = count.bit_length() - 1
    tile = lax.axis_index("tile")
    own = images // 2
    half_slots = slot_total // 2
    first = tile * own

    def mine(value):
        return lax.dynamic_slice_in_dim(value, first, own, 0)

    def others(value):
        return lax.dynamic_slice_in_dim(value, own - first, own, 0)

    unit = (bucket[0] >= 0).astype(f32)

    pair = jnp.concatenate([patches, out_grad], axis=2).astype(f32)
    slots_data = jnp.concatenate([mine(pair), swap_tiles(others(pair)) * unit], axis=1).astype(bf16)
    near = jnp.arange(slot_total, dtype=jnp.int32)
    slot_ids = (near + tile * tile_slots) % slot_total

    condition = time_embed(timesteps, width) + jnp.take(class_table, labels, axis=0).astype(f32)
    cond_act = jax.nn.silu(condition).astype(bf16)
    mod_half = mm("id,de->ie", cond_act, ada_weight) + ada_bias.astype(f32)
    mod_mine, mod_recv = mine(mod_half), swap_tiles(others(mod_half))
    modulation = jnp.where(
        tile == 0,
        jnp.concatenate([mod_mine, mod_recv], axis=1),
        jnp.concatenate([mod_recv, mod_mine], axis=1),
    )
    shift_a, scale_a, gate_a, shift_m, scale_m, gate_m = [
        portion[:, None, :] for portion in jnp.split(modulation, 6, axis=1)
    ]

    my_bucket, my_order = mine(bucket), mine(keep_order)
    half_rows = jnp.where(my_bucket == 0, 8, jnp.where(my_bucket == 1, 6, 10))[:, None]
    columns = jnp.where(my_bucket == 0, 16, jnp.where(my_bucket == 1, 20, 12))[:, None]
    area = half_rows * columns
    order_valid = (my_order % tile_slots) < area
    upper = (near[:, None] < near[None, :]).astype(bf16)
    rank = mm("ij,jk->ik", order_valid.astype(bf16), upper).astype(jnp.int32)
    limit = area
    place = jnp.where(rank < limit, rank, rank - limit + half_slots)
    hit = (place[:, None, :] == near[None, :, None]) & order_valid[:, None, :]
    row_slot = jnp.sum(jnp.where(hit, my_order[:, None, :] + 1, 0), axis=2) - 1
    live = row_slot >= 0
    select = (row_slot[:, :, None] == slot_ids[None, None, :]).astype(bf16)
    row_data = mm("irs,isc->irc", select, slots_data).astype(bf16)
    row_patches, row_grads = row_data[:, :, :patch_width], row_data[:, :, patch_width:]
    local = row_slot % tile_slots
    grid_row = (row_slot // tile_slots) * half_rows + local // columns
    grid_col = local % columns
    marks = jnp.arange(GRID_MAX, dtype=jnp.int32)
    mark_row = (grid_row[:, :, None] == marks).astype(bf16)
    mark_col = (grid_col[:, :, None] == marks).astype(bf16)
    table = three_way(axis_table(width // 2))
    blank = jnp.zeros((GRID_MAX, width // 2), bf16)
    wide = jnp.concatenate(
        [patch_weight]
        + [jnp.concatenate([piece, blank], axis=1) for piece in table]
        + [jnp.concatenate([blank, piece], axis=1) for piece in table],
        axis=0,
    )
    features = jnp.concatenate([row_patches] + [mark_row] * 3 + [mark_col] * 3, axis=2)
    embedded = mm("irk,kd->ird", features, wide) + patch_bias.astype(f32)
    key_live = live[:, :half_slots]

    kept_x = embedded[:, :half_slots]
    normed_a, rstd_a = norm_stats(kept_x)
    attn_in = (normed_a * (1.0 + scale_a) + shift_a).astype(bf16)
    qkv_bias = jnp.concatenate([query_bias, jnp.zeros_like(query_bias), value_bias]).astype(f32)
    qkv = (mm("isd,de->ise", attn_in, qkv_weight) + qkv_bias).astype(bf16)
    queries, keys, values = [split_heads(part) for part in jnp.split(qkv, 3, axis=2)]
    scaling = (width // HEADS) ** (-0.5)
    scores = mm("gqhd,gkhd->ghqk", queries, keys) * scaling
    scores = jnp.where(key_live[:, None, None, :], scores, -1e30)
    powers = jnp.exp(scores - jnp.max(scores, axis=-1, keepdims=True))
    probs = powers / jnp.sum(powers, axis=-1, keepdims=True)
    probs_low = probs.astype(bf16)
    mixed = mm("ghqk,gkhd->gqhd", probs_low, values).reshape(kept_x.shape).astype(bf16)
    attn_out = mm("iqd,de->iqe", mixed, proj_weight) + proj_bias.astype(f32)
    middle = kept_x + gate_a * attn_out
    normed_m, rstd_m = norm_stats(middle)
    mlp_in = (normed_m * (1.0 + scale_m) + shift_m).astype(bf16)
    pre_act = mm("iqd,df->iqf", mlp_in, up_weight) + up_bias.astype(f32)
    act_value, act_slope = gelu_parts(pre_act)
    activated = act_value.astype(bf16)
    mlp_out = mm("iqf,fd->iqd", activated, down_weight) + down_bias.astype(f32)
    block_out = middle + gate_m * mlp_out
    merged = jnp.concatenate([block_out, embedded[:, half_slots:]], axis=1)
    normed_f, rstd_f = norm_stats(merged)
    final_in = normed_f.astype(bf16)
    row_denoised = mm("isd,dp->isp", final_in, final_weight) + final_bias.astype(f32)

    final_weight_grad = mm("isd,isp->dp", final_in, row_grads)
    final_bias_grad = jnp.sum(row_grads.astype(f32), axis=(0, 1))
    d_final = mm("isp,dp->isd", row_grads, final_weight)
    d_merged = norm_back(normed_f, rstd_f, d_final)
    d_block = d_merged[:, :half_slots]
    d_mlp = (gate_m * d_block).astype(bf16)
    d_gate_m = jnp.sum(d_block * mlp_out, axis=1)

    def exchange(left, right):
        rows, lw, rw = left.shape[0] * left.shape[1], left.shape[2], right.shape[2] // 2
        left, right = left.reshape(rows, lw), right.reshape(rows, 2 * rw)
        keep = lax.dynamic_slice_in_dim(right, tile * rw, rw, 1)
        give = lax.dynamic_slice_in_dim(right, (1 - tile) * rw, rw, 1)
        got_left = swap_tiles(left.astype(f32)) * unit
        got_right = swap_tiles(give.astype(f32)) * unit
        both_left = jnp.concatenate([left, got_left.astype(bf16)], axis=0)
        both_right = jnp.concatenate([keep, got_right.astype(bf16)], axis=0)
        return both_left, both_right

    orders = (list(range(bits)), [1, 0] + list(range(2, bits)))

    def scatter(left, right, axis, cut):
        both_left, both_right = exchange(left, right)
        grad = mm("kd,kc->dc", both_left, both_right)
        grad = grad.reshape(count, grad.shape[0] // count, grad.shape[1])
        size = grad.shape[axis]
        return [
            Halving(lax.slice_in_dim(grad, 0, cut, axis=axis), orders[0], count),
            Halving(lax.slice_in_dim(grad, cut, size, axis=axis), orders[1], count),
        ]

    down_chain = scatter(activated, d_mlp, 1, hidden // count // 2)
    down_bias_grad = jnp.sum(d_mlp.astype(f32), axis=(0, 1))
    d_activated = mm("iqd,fd->iqf", d_mlp, down_weight)
    d_pre = (d_activated * act_slope).astype(bf16)
    up_chain = scatter(mlp_in, d_pre, 2, hidden // 4)
    up_bias_grad = jnp.sum(d_pre.astype(f32), axis=(0, 1))
    d_mlp_in = mm("iqf,df->iqd", d_pre, up_weight)
    d_shift_m = jnp.sum(d_mlp_in, axis=1)
    d_scale_m = jnp.sum(d_mlp_in * normed_m, axis=1)
    d_middle = d_block + norm_back(normed_m, rstd_m, d_mlp_in * (1.0 + scale_m))
    d_attn = (gate_a * d_middle).astype(bf16)
    d_gate_a = jnp.sum(d_middle * attn_out, axis=1)
    proj_chain = scatter(mixed, d_attn, 1, (width // count + 1) // 2)
    proj_bias_grad = jnp.sum(d_attn.astype(f32), axis=(0, 1))
    d_mixed = split_heads(mm("iqe,de->iqd", d_attn, proj_weight).astype(bf16))
    d_probs = mm("gqhd,gkhd->ghqk", d_mixed, values)
    row_delta = jnp.sum(probs * d_probs, axis=-1, keepdims=True)
    d_scores = (probs * (d_probs - row_delta)).astype(bf16)
    d_query = mm("ghqk,gkhd->gqhd", d_scores, keys) * scaling
    d_key = mm("ghqk,gqhd->gkhd", d_scores, queries) * scaling
    d_value = mm("ghqk,gqhd->gkhd", probs_low, d_mixed)
    d_qkv = jnp.concatenate(
        [part.reshape(kept_x.shape) for part in (d_query, d_key, d_value)], axis=2
    ).astype(bf16)
    qkv_chain = scatter(attn_in, d_qkv, 2, 896)
    qkv_bias_sums = jnp.sum(d_qkv.astype(f32), axis=(0, 1))
    d_attn_in = mm("ice,de->icd", d_qkv, qkv_weight)
    d_shift_a = jnp.sum(d_attn_in, axis=1)
    d_scale_a = jnp.sum(d_attn_in * normed_a, axis=1)
    d_kept = d_middle + norm_back(normed_a, rstd_a, d_attn_in * (1.0 + scale_a))
    d_low = jnp.concatenate([d_kept, d_merged[:, half_slots:]], axis=1).astype(bf16)
    row_patch_grad = mm("isd,pd->isp", d_low, patch_weight)
    patch_weight_grad = mm("isp,isd->pd", row_patches, d_low)
    patch_bias_grad = jnp.sum(d_low.astype(f32), axis=(0, 1))

    back = jnp.concatenate([row_denoised, row_patch_grad], axis=2)
    slot_out = jnp.einsum("irs,irc->isc", select.astype(f32), back, precision=highest)
    near_part, far_part = slot_out[:, :tile_slots], swap_tiles(slot_out[:, tile_slots:])
    slot_mine = jnp.where(
        tile == 0,
        jnp.concatenate([near_part, far_part], axis=0),
        jnp.concatenate([far_part, near_part], axis=0),
    )
    denoised, patch_grad = slot_mine[:, :, :patch_width], slot_mine[:, :, patch_width:]

    d_mod = jnp.concatenate(
        [d_shift_a, d_scale_a, d_gate_a, d_shift_m, d_scale_m, d_gate_m], axis=1
    )
    mod_width = d_mod.shape[1] // 2
    keep = lax.dynamic_slice_in_dim(d_mod, tile * mod_width, mod_width, 1)
    give = lax.dynamic_slice_in_dim(d_mod, (1 - tile) * mod_width, mod_width, 1)
    got = swap_tiles(give) * unit
    d_mod_half = jnp.where(
        tile == 0, jnp.concatenate([keep, got], axis=0), jnp.concatenate([got, keep], axis=0)
    ).astype(bf16)
    d_cond_act = mm("ie,de->id", d_mod_half, ada_weight)
    gate = jax.nn.sigmoid(condition)
    d_cond_part = d_cond_act * (gate * (1.0 + condition * (1.0 - gate)))
    d_condition = d_cond_part + swap_tiles(d_cond_part)

    small = [
        patch_weight_grad,
        patch_bias_grad,
        qkv_bias_sums[:width],
        qkv_bias_sums[2 * width :],
        proj_bias_grad,
        up_bias_grad,
        down_bias_grad,
        final_weight_grad,
        final_bias_grad,
    ]
    area_all = jnp.where(bucket == 0, 128, 120)
    counts_local = jnp.stack([jnp.sum(area_all), jnp.sum(2 * area_all)]).astype(f32) * 0.5
    flat = jnp.concatenate([leaf.reshape(-1) for leaf in small] + [counts_local])
    flat = jnp.pad(flat, (0, (-flat.shape[0]) % 1024)).reshape(-1, 128)
    summed = all_sum(flat, bits, count).reshape(-1)
    sums = []
    offset = 0
    for leaf in small + [counts_local]:
        sums.append(summed[offset : offset + leaf.size].reshape(leaf.shape))
        offset += leaf.size

    packed = jnp.concatenate(
        [
            d_mod_half.astype(f32),
            d_condition,
            cond_act.astype(f32),
            jnp.broadcast_to(labels.astype(f32)[:, None], (images, 128)),
        ],
        axis=1,
    )
    every = (all_collect(packed, bits, count) * unit).reshape(count * images, -1)
    all_mod = every[:, :mod_width].astype(bf16)
    all_cond = every[:, mod_width : mod_width + width]
    all_act = every[:, mod_width + width : mod_width + 2 * width]
    all_label = every[:, mod_width + 2 * width].astype(jnp.int32)
    block = width // count
    act_rows = lax.dynamic_slice_in_dim(all_act, lax.axis_index("dp") * block, block, 1).astype(bf16)
    ada_final = mm("nd,ne->de", act_rows, all_mod)
    ada_half = jnp.sum(all_mod.astype(f32), axis=0)
    ada_other = swap_tiles(ada_half)
    ada_bias_sum = jnp.where(
        tile == 0,
        jnp.concatenate([ada_half, ada_other]),
        jnp.concatenate([ada_other, ada_half]),
    )
    one_hot = (all_label[:, None] == jnp.arange(class_count, dtype=jnp.int32)[None, :]).astype(f32)
    class_table_sum = jnp.einsum("nc,nd->cd", one_hot, all_cond, precision=highest)

    down_final = jnp.concatenate([chain.result() for chain in down_chain], axis=0)
    up_final = jnp.concatenate([chain.result() for chain in up_chain], axis=1)
    proj_final = jnp.concatenate([chain.result() for chain in proj_chain], axis=0)
    qkv_final = jnp.concatenate([chain.result() for chain in qkv_chain], axis=1)
    (
        patch_weight_sum,
        patch_bias_sum,
        query_bias_sum,
        value_bias_sum,
        proj_bias_sum,
        up_bias_sum,
        down_bias_sum,
        final_weight_sum,
        final_bias_sum,
        token_counts,
    ) = sums
    return (
        denoised,
        patch_grad,
        patch_weight_sum,
        patch_bias_sum,
        class_table_sum,
        ada_final,
        ada_bias_sum,
        qkv_final,
        query_bias_sum,
        value_bias_sum,
        proj_final,
        proj_bias_sum,
        up_final,
        up_bias_sum,
        down_final,
        down_bias_sum,
        final_weight_sum,
        final_bias_sum,
        token_counts,
    )


def solution(mesh):
    in_specs = (
        P("dp", "tile", None),
        P("dp"),
        P("dp", None),
        P("dp"),
        P("dp"),
        P(),
        P(),
        P(),
        P(None, "tile"),
        P("tile"),
        P(),
        P(),
        P(),
        P(),
        P(),
        P(),
        P(),
        P(),
        P(),
        P(),
        P(),
        P("dp", "tile", None),
    )
    out_specs = (
        P("dp", "tile", None),
        P("dp", "tile", None),
        P(),
        P(),
        P(),
        P("dp", "tile"),
        P(),
        P("dp", "tile"),
        P(),
        P(),
        P("dp", "tile"),
        P(),
        P("dp", "tile"),
        P(),
        P("dp", "tile"),
        P(),
        P(),
        P(),
        P(),
    )
    return jax.shard_map(body, mesh=mesh, in_specs=in_specs, out_specs=out_specs, check_vma=False)
```

```python
import math

import jax
import jax.numpy as jnp
import numpy as np
from jax import lax
from jax.experimental import pallas as pl
from jax.experimental.pallas import tpu as pltpu
from jax.sharding import PartitionSpec as P

HEADS = 16
GRID_MAX = 32
epsilon = 1e-06
highest = lax.Precision.HIGHEST
f32 = jnp.float32
bf16 = jnp.bfloat16


def mm(spec, left, right):
    return jnp.einsum(spec, left, right, preferred_element_type=f32)


def norm_stats(values):
    center = values - jnp.mean(values, axis=-1, keepdims=True)
    rstd = lax.rsqrt(jnp.mean(center * center, axis=-1, keepdims=True) + epsilon)
    return center * rstd, rstd


def norm_back(normed, rstd, grad):
    return rstd * (
        grad
        - jnp.mean(grad, axis=-1, keepdims=True)
        - normed * jnp.mean(grad * normed, axis=-1, keepdims=True)
    )


def gelu_parts(u):
    inner = 0.7978845608028654 * (u + 0.044715 * u * u * u)
    th = jnp.tanh(inner)
    value = 0.5 * u * (1.0 + th)
    slope = 0.5 * (1.0 + th) + 0.5 * u * (1.0 - th * th) * 0.7978845608028654 * (
        1.0 + 3.0 * 0.044715 * u * u
    )
    return value, slope


def split_heads(tensor):
    return tensor.reshape(tensor.shape[0], tensor.shape[1], HEADS, tensor.shape[2] // HEADS)


def three_way(table):
    parts = []
    rest = table
    for _ in range(3):
        piece = rest.astype(bf16)
        parts.append(piece)
        rest = rest - piece.astype(f32)
    return parts


def axis_table(width):
    quarter = width // 2
    omega = jnp.exp(-math.log(10000.0) * jnp.arange(quarter, dtype=f32) / quarter)
    angles = jnp.arange(GRID_MAX, dtype=f32)[:, None] * omega[None, :]
    return jnp.concatenate([jnp.sin(angles), jnp.cos(angles)], axis=-1)


def time_embed(timesteps, model_width):
    half = model_width // 2
    freqs = jnp.exp(-math.log(10000.0) * jnp.arange(half, dtype=f32) / half)
    angles = timesteps.astype(f32)[:, None] * freqs
    return jnp.concatenate([jnp.cos(angles), jnp.sin(angles)], axis=-1)


def swap_tiles(value):
    return lax.ppermute(value, "tile", [(0, 1), (1, 0)])


def flip_bit(value, bit, count):
    return lax.ppermute(value, "dp", [(d, d ^ (1 << bit)) for d in range(count)])


def flip_stage(value, stage, orders, count):
    pairs = []
    for d in range(count):
        for t, order in enumerate(orders):
            pairs.append((2 * d + t, 2 * (d ^ (1 << order[stage])) + t))
    return lax.ppermute(value, ("dp", "tile"), pairs)


def relative_masks(order):
    bits = len(order)
    masks = []
    for rel in range(1 << bits):
        mask = 0
        for stage in range(bits):
            if (rel >> (bits - 1 - stage)) & 1:
                mask |= 1 << order[stage]
        masks.append(mask)
    return masks


def packed_rows(rows, cols):
    return (cols // 128) * rows + ((rows + 1) // 2 if cols % 128 else 0)


def pack_kernel(ids_ref, grad_ref, out_ref):
    rows, cols = grad_ref.shape[1:]
    full, rest = divmod(cols, 128)
    for c in range(full):
        out_ref[0, c * rows : (c + 1) * rows, :] = grad_ref[0, :, c * 128 : (c + 1) * 128]
    if rest:
        top = (rows + 1) // 2
        start = full * rows
        out_ref[0, start : start + top, :rest] = grad_ref[0, :top, full * 128 :]
        out_ref[0, start : start + rows - top, rest:] = grad_ref[0, top:, full * 128 :]


def pack(grad, ids, low, high):
    _, rows, cols = grad.shape
    long = packed_rows(rows, cols)
    number = high - low
    return pl.pallas_call(
        pack_kernel,
        out_shape=jax.ShapeDtypeStruct((number, long, 128), f32),
        grid_spec=pltpu.PrefetchScalarGridSpec(
            num_scalar_prefetch=1,
            grid=(number,),
            in_specs=[pl.BlockSpec((1, rows, cols), lambda k, ids: (ids[low + k], 0, 0))],
            out_specs=pl.BlockSpec((1, long, 128), lambda k, ids: (k, 0, 0)),
        ),
        cost_estimate=pl.CostEstimate(
            flops=0, bytes_accessed=8 * number * rows * cols, transcendentals=0
        ),
        name="pack",
    )(ids, grad)


def unpack(block, rows, cols):
    full, rest = divmod(cols, 128)
    wide = block[: full * rows].reshape(full, rows, 128).transpose(1, 0, 2)
    wide = wide.reshape(rows, full * 128)
    if not rest:
        return wide
    top = (rows + 1) // 2
    tail = block[full * rows :]
    last = jnp.concatenate([tail[:, :rest], tail[: rows - top, rest:]], axis=0)
    return jnp.concatenate([wide, last], axis=1)


class Halving:
    def __init__(self, grad, ids, orders, count):
        self.grad = grad
        self.shape = grad.shape[1:]
        self.ids = ids
        self.orders = orders
        self.count = count
        self.stages = len(orders[0])
        self.first = pack(grad, ids, count // 2, count)
        self.received = []

    def step(self):
        stage = len(self.received)
        if stage == 0:
            message = self.first
            self.keep = pack(self.grad, self.ids, 0, self.count // 2)
        else:
            low = 1 << (self.stages - 1 - stage)
            message = self.keep[low : 2 * low]
            for piece in self.received:
                message = message + piece[low : 2 * low]
        self.received.append(flip_stage(message, stage, self.orders, self.count))

    def result(self):
        while len(self.received) < self.stages:
            self.step()
        total = self.keep[0]
        for piece in self.received:
            total = total + piece[0]
        return unpack(total, *self.shape)


def all_sum(value, bits, count):
    value = value + swap_tiles(value)
    for bit in range(bits):
        value = value + flip_bit(value, bit, count)
    return value


def all_collect(value, bits, count):
    value = value[None]
    for bit in range(bits):
        value = jnp.concatenate([value, flip_bit(value, bit, count)], axis=0)
    return value


def body(
    patches,
    bucket,
    keep_order,
    timesteps,
    labels,
    patch_weight,
    patch_bias,
    class_table,
    ada_weight,
    ada_bias,
    qkv_weight,
    query_bias,
    value_bias,
    proj_weight,
    proj_bias,
    up_weight,
    up_bias,
    down_weight,
    down_bias,
    final_weight,
    final_bias,
    out_grad,
):
    images, tile_slots, patch_width = patches.shape
    slot_total = keep_order.shape[1]
    width = patch_weight.shape[1]
    hidden = up_weight.shape[1]
    class_count = class_table.shape[0]
    count = lax.axis_size("dp")
    bits = count.bit_length() - 1
    tile = lax.axis_index("tile")
    own = images // 2
    half_slots = slot_total // 2
    first = tile * own

    def mine(value):
        return lax.dynamic_slice_in_dim(value, first, own, 0)

    def others(value):
        return lax.dynamic_slice_in_dim(value, own - first, own, 0)

    unit = (bucket[0] >= 0).astype(f32)

    pair = jnp.concatenate([patches, out_grad], axis=2).astype(f32)
    slots_data = jnp.concatenate([mine(pair), swap_tiles(others(pair)) * unit], axis=1).astype(bf16)
    near = jnp.arange(slot_total, dtype=jnp.int32)
    slot_ids = (near + tile * tile_slots) % slot_total

    condition = time_embed(timesteps, width) + jnp.take(class_table, labels, axis=0).astype(f32)
    cond_act = jax.nn.silu(condition).astype(bf16)
    mod_half = mm("id,de->ie", cond_act, ada_weight) + ada_bias.astype(f32)
    mod_mine, mod_recv = mine(mod_half), swap_tiles(others(mod_half))
    modulation = jnp.where(
        tile == 0,
        jnp.concatenate([mod_mine, mod_recv], axis=1),
        jnp.concatenate([mod_recv, mod_mine], axis=1),
    )
    shift_a, scale_a, gate_a, shift_m, scale_m, gate_m = [
        portion[:, None, :] for portion in jnp.split(modulation, 6, axis=1)
    ]

    my_bucket, my_order = mine(bucket), mine(keep_order)
    half_rows = jnp.where(my_bucket == 0, 8, jnp.where(my_bucket == 1, 6, 10))[:, None]
    columns = jnp.where(my_bucket == 0, 16, jnp.where(my_bucket == 1, 20, 12))[:, None]
    area = half_rows * columns
    order_valid = (my_order % tile_slots) < area
    upper = (near[:, None] < near[None, :]).astype(bf16)
    rank = mm("ij,jk->ik", order_valid.astype(bf16), upper).astype(jnp.int32)
    limit = area
    place = jnp.where(rank < limit, rank, rank - limit + half_slots)
    hit = (place[:, None, :] == near[None, :, None]) & order_valid[:, None, :]
    row_slot = jnp.sum(jnp.where(hit, my_order[:, None, :] + 1, 0), axis=2) - 1
    live = row_slot >= 0
    select = (row_slot[:, :, None] == slot_ids[None, None, :]).astype(bf16)
    row_data = mm("irs,isc->irc", select, slots_data).astype(bf16)
    row_patches, row_grads = row_data[:, :, :patch_width], row_data[:, :, patch_width:]
    local = row_slot % tile_slots
    grid_row = (row_slot // tile_slots) * half_rows + local // columns
    grid_col = local % columns
    marks = jnp.arange(GRID_MAX, dtype=jnp.int32)
    mark_row = (grid_row[:, :, None] == marks).astype(bf16)
    mark_col = (grid_col[:, :, None] == marks).astype(bf16)
    table = three_way(axis_table(width // 2))
    blank = jnp.zeros((GRID_MAX, width // 2), bf16)
    wide = jnp.concatenate(
        [patch_weight]
        + [jnp.concatenate([piece, blank], axis=1) for piece in table]
        + [jnp.concatenate([blank, piece], axis=1) for piece in table],
        axis=0,
    )
    features = jnp.concatenate([row_patches] + [mark_row] * 3 + [mark_col] * 3, axis=2)
    embedded = mm("irk,kd->ird", features, wide) + patch_bias.astype(f32)
    key_live = live[:, :half_slots]

    kept_x = embedded[:, :half_slots]
    normed_a, rstd_a = norm_stats(kept_x)
    attn_in = (normed_a * (1.0 + scale_a) + shift_a).astype(bf16)
    qkv_bias = jnp.concatenate([query_bias, jnp.zeros_like(query_bias), value_bias]).astype(f32)
    qkv = (mm("isd,de->ise", attn_in, qkv_weight) + qkv_bias).astype(bf16)
    queries, keys, values = [split_heads(part) for part in jnp.split(qkv, 3, axis=2)]
    scaling = (width // HEADS) ** (-0.5)
    scores = mm("gqhd,gkhd->ghqk", queries, keys) * scaling
    scores = jnp.where(key_live[:, None, None, :], scores, -1e30)
    powers = jnp.exp(scores - jnp.max(scores, axis=-1, keepdims=True))
    probs = powers / jnp.sum(powers, axis=-1, keepdims=True)
    probs_low = probs.astype(bf16)
    mixed = mm("ghqk,gkhd->gqhd", probs_low, values).reshape(kept_x.shape).astype(bf16)
    attn_out = mm("iqd,de->iqe", mixed, proj_weight) + proj_bias.astype(f32)
    middle = kept_x + gate_a * attn_out
    normed_m, rstd_m = norm_stats(middle)
    mlp_in = (normed_m * (1.0 + scale_m) + shift_m).astype(bf16)
    pre_act = mm("iqd,df->iqf", mlp_in, up_weight) + up_bias.astype(f32)
    act_value, act_slope = gelu_parts(pre_act)
    activated = act_value.astype(bf16)
    mlp_out = mm("iqf,fd->iqd", activated, down_weight) + down_bias.astype(f32)
    block_out = middle + gate_m * mlp_out
    merged = jnp.concatenate([block_out, embedded[:, half_slots:]], axis=1)
    normed_f, rstd_f = norm_stats(merged)
    final_in = normed_f.astype(bf16)
    row_denoised = mm("isd,dp->isp", final_in, final_weight) + final_bias.astype(f32)

    final_weight_grad = mm("isd,isp->dp", final_in, row_grads)
    final_bias_grad = jnp.sum(row_grads.astype(f32), axis=(0, 1))
    d_final = mm("isp,dp->isd", row_grads, final_weight)
    d_merged = norm_back(normed_f, rstd_f, d_final)
    d_block = d_merged[:, :half_slots]
    d_mlp = (gate_m * d_block).astype(bf16)
    d_gate_m = jnp.sum(d_block * mlp_out, axis=1)

    def exchange(left, right):
        rows, lw, rw = left.shape[0] * left.shape[1], left.shape[2], right.shape[2] // 2
        left, right = left.reshape(rows, lw), right.reshape(rows, 2 * rw)
        keep = lax.dynamic_slice_in_dim(right, tile * rw, rw, 1)
        give = lax.dynamic_slice_in_dim(right, (1 - tile) * rw, rw, 1)
        got_left = swap_tiles(left.astype(f32)) * unit
        got_right = swap_tiles(give.astype(f32)) * unit
        both_left = jnp.concatenate([left, got_left.astype(bf16)], axis=0)
        both_right = jnp.concatenate([keep, got_right.astype(bf16)], axis=0)
        return both_left, both_right

    orders = (list(range(bits)), [1, 0] + list(range(2, bits)))
    index = lax.axis_index("dp")
    masks = [jnp.array(relative_masks(order), jnp.int32) for order in orders]
    ids = jnp.where(tile == 0, masks[0], masks[1]) ^ index

    def scatter(left, right):
        both_left, both_right = exchange(left, right)
        grad = mm("kd,kc->dc", both_left, both_right)
        grad = grad.reshape(count, grad.shape[0] // count, grad.shape[1])
        return Halving(grad, ids, orders, count)

    def after(value, *others):
        return lax.optimization_barrier((value,) + others)[0]

    down_chain = scatter(activated, d_mlp)
    down_bias_grad = jnp.sum(d_mlp.astype(f32), axis=(0, 1))
    d_activated = mm("iqd,fd->iqf", d_mlp, down_weight)
    d_pre = (d_activated * act_slope).astype(bf16)
    up_chain = scatter(mlp_in, d_pre)
    up_bias_grad = jnp.sum(d_pre.astype(f32), axis=(0, 1))
    d_mlp_in = mm("iqf,df->iqd", after(d_pre, down_chain.first), up_weight)
    d_shift_m = jnp.sum(d_mlp_in, axis=1)
    d_scale_m = jnp.sum(d_mlp_in * normed_m, axis=1)
    d_middle = d_block + norm_back(normed_m, rstd_m, d_mlp_in * (1.0 + scale_m))
    d_attn = (gate_a * d_middle).astype(bf16)
    d_gate_a = jnp.sum(d_middle * attn_out, axis=1)
    proj_chain = scatter(mixed, d_attn)
    proj_bias_grad = jnp.sum(d_attn.astype(f32), axis=(0, 1))
    d_mixed = split_heads(
        mm("iqe,de->iqd", after(d_attn, up_chain.first), proj_weight).astype(bf16)
    )
    d_probs = mm("gqhd,gkhd->ghqk", d_mixed, values)
    row_delta = jnp.sum(probs * d_probs, axis=-1, keepdims=True)
    d_scores = (probs * (d_probs - row_delta)).astype(bf16)
    d_query = mm("ghqk,gkhd->gqhd", d_scores, keys) * scaling
    d_key = mm("ghqk,gqhd->gkhd", d_scores, queries) * scaling
    d_value = mm("ghqk,gqhd->gkhd", probs_low, d_mixed)
    d_qkv = jnp.concatenate(
        [part.reshape(kept_x.shape) for part in (d_query, d_key, d_value)], axis=2
    ).astype(bf16)
    qkv_chain = scatter(attn_in, d_qkv)
    qkv_bias_sums = jnp.sum(d_qkv.astype(f32), axis=(0, 1))
    d_attn_in = mm("ice,de->icd", d_qkv, qkv_weight)
    d_shift_a = jnp.sum(d_attn_in, axis=1)
    d_scale_a = jnp.sum(d_attn_in * normed_a, axis=1)
    d_kept = d_middle + norm_back(normed_a, rstd_a, d_attn_in * (1.0 + scale_a))
    d_low = jnp.concatenate([d_kept, d_merged[:, half_slots:]], axis=1).astype(bf16)
    row_patch_grad = mm("isd,pd->isp", d_low, patch_weight)
    patch_weight_grad = mm("isp,isd->pd", row_patches, d_low)
    patch_bias_grad = jnp.sum(d_low.astype(f32), axis=(0, 1))

    back = jnp.concatenate([row_denoised, row_patch_grad], axis=2)
    slot_out = jnp.einsum("irs,irc->isc", select.astype(f32), back, precision=highest)
    near_part, far_part = slot_out[:, :tile_slots], swap_tiles(slot_out[:, tile_slots:])
    slot_mine = jnp.where(
        tile == 0,
        jnp.concatenate([near_part, far_part], axis=0),
        jnp.concatenate([far_part, near_part], axis=0),
    )
    denoised, patch_grad = slot_mine[:, :, :patch_width], slot_mine[:, :, patch_width:]

    d_mod = jnp.concatenate(
        [d_shift_a, d_scale_a, d_gate_a, d_shift_m, d_scale_m, d_gate_m], axis=1
    )
    mod_width = d_mod.shape[1] // 2
    keep = lax.dynamic_slice_in_dim(d_mod, tile * mod_width, mod_width, 1)
    give = lax.dynamic_slice_in_dim(d_mod, (1 - tile) * mod_width, mod_width, 1)
    got = swap_tiles(give) * unit
    d_mod_half = jnp.where(
        tile == 0, jnp.concatenate([keep, got], axis=0), jnp.concatenate([got, keep], axis=0)
    ).astype(bf16)
    d_cond_act = mm("ie,de->id", d_mod_half, ada_weight)
    gate = jax.nn.sigmoid(condition)
    d_cond_part = d_cond_act * (gate * (1.0 + condition * (1.0 - gate)))
    d_condition = d_cond_part + swap_tiles(d_cond_part)

    small = [
        patch_weight_grad,
        patch_bias_grad,
        qkv_bias_sums[:width],
        qkv_bias_sums[2 * width :],
        proj_bias_grad,
        up_bias_grad,
        down_bias_grad,
        final_weight_grad,
        final_bias_grad,
    ]
    area_all = jnp.where(bucket == 0, 128, 120)
    counts_local = jnp.stack([jnp.sum(area_all), jnp.sum(2 * area_all)]).astype(f32) * 0.5
    flat = jnp.concatenate([leaf.reshape(-1) for leaf in small] + [counts_local])
    flat = jnp.pad(flat, (0, (-flat.shape[0]) % 1024)).reshape(-1, 128)
    summed = all_sum(flat, bits, count).reshape(-1)
    sums = []
    offset = 0
    for leaf in small + [counts_local]:
        sums.append(summed[offset : offset + leaf.size].reshape(leaf.shape))
        offset += leaf.size

    packed = jnp.concatenate(
        [
            d_mod_half.astype(f32),
            d_condition,
            cond_act.astype(f32),
            jnp.broadcast_to(labels.astype(f32)[:, None], (images, 128)),
        ],
        axis=1,
    )
    every = (all_collect(packed, bits, count) * unit).reshape(count * images, -1)
    all_mod = every[:, :mod_width].astype(bf16)
    all_cond = every[:, mod_width : mod_width + width]
    all_act = every[:, mod_width + width : mod_width + 2 * width]
    all_label = every[:, mod_width + 2 * width].astype(jnp.int32)
    block = width // count
    act_rows = lax.dynamic_slice_in_dim(all_act, lax.axis_index("dp") * block, block, 1).astype(bf16)
    ada_final = mm("nd,ne->de", act_rows, all_mod)
    ada_half = jnp.sum(all_mod.astype(f32), axis=0)
    ada_other = swap_tiles(ada_half)
    ada_bias_sum = jnp.where(
        tile == 0,
        jnp.concatenate([ada_half, ada_other]),
        jnp.concatenate([ada_other, ada_half]),
    )
    one_hot = (all_label[:, None] == jnp.arange(class_count, dtype=jnp.int32)[None, :]).astype(f32)
    class_table_sum = jnp.einsum("nc,nd->cd", one_hot, all_cond, precision=highest)

    down_final = down_chain.result()
    up_final = up_chain.result()
    proj_final = proj_chain.result()
    qkv_final = qkv_chain.result()
    (
        patch_weight_sum,
        patch_bias_sum,
        query_bias_sum,
        value_bias_sum,
        proj_bias_sum,
        up_bias_sum,
        down_bias_sum,
        final_weight_sum,
        final_bias_sum,
        token_counts,
    ) = sums
    return (
        denoised,
        patch_grad,
        patch_weight_sum,
        patch_bias_sum,
        class_table_sum,
        ada_final,
        ada_bias_sum,
        qkv_final,
        query_bias_sum,
        value_bias_sum,
        proj_final,
        proj_bias_sum,
        up_final,
        up_bias_sum,
        down_final,
        down_bias_sum,
        final_weight_sum,
        final_bias_sum,
        token_counts,
    )


def solution(mesh):
    in_specs = (
        P("dp", "tile", None),
        P("dp"),
        P("dp", None),
        P("dp"),
        P("dp"),
        P(),
        P(),
        P(),
        P(None, "tile"),
        P("tile"),
        P(),
        P(),
        P(),
        P(),
        P(),
        P(),
        P(),
        P(),
        P(),
        P(),
        P(),
        P("dp", "tile", None),
    )
    out_specs = (
        P("dp", "tile", None),
        P("dp", "tile", None),
        P(),
        P(),
        P(),
        P("dp", "tile"),
        P(),
        P("dp", "tile"),
        P(),
        P(),
        P("dp", "tile"),
        P(),
        P("dp", "tile"),
        P(),
        P("dp", "tile"),
        P(),
        P(),
        P(),
        P(),
    )
    return jax.shard_map(body, mesh=mesh, in_specs=in_specs, out_specs=out_specs, check_vma=False)
```

```python
import functools
import math

import jax
import jax.numpy as jnp
from jax import lax
from jax.experimental import pallas as pl
from jax.experimental.pallas import tpu as pltpu
from jax.sharding import PartitionSpec as P

HEADS = 16
GRID_MAX = 32
epsilon = 1e-06
highest = lax.Precision.HIGHEST
f32 = jnp.float32
bf16 = jnp.bfloat16


def mm(spec, left, right):
    return jnp.einsum(spec, left, right, preferred_element_type=f32)


def norm_stats(values):
    center = values - jnp.mean(values, axis=-1, keepdims=True)
    rstd = lax.rsqrt(jnp.mean(center * center, axis=-1, keepdims=True) + epsilon)
    return center * rstd, rstd


def norm_back(normed, rstd, grad):
    return rstd * (
        grad
        - jnp.mean(grad, axis=-1, keepdims=True)
        - normed * jnp.mean(grad * normed, axis=-1, keepdims=True)
    )


def gelu_parts(u):
    inner = 0.7978845608028654 * (u + 0.044715 * u * u * u)
    th = jnp.tanh(inner)
    value = 0.5 * u * (1.0 + th)
    slope = 0.5 * (1.0 + th) + 0.5 * u * (1.0 - th * th) * 0.7978845608028654 * (
        1.0 + 3.0 * 0.044715 * u * u
    )
    return value, slope


def split_heads(tensor):
    return tensor.reshape(tensor.shape[0], tensor.shape[1], HEADS, tensor.shape[2] // HEADS)


def three_way(table):
    parts = []
    rest = table
    for _ in range(3):
        piece = rest.astype(bf16)
        parts.append(piece)
        rest = rest - piece.astype(f32)
    return parts


def axis_table(width):
    quarter = width // 2
    omega = jnp.exp(-math.log(10000.0) * jnp.arange(quarter, dtype=f32) / quarter)
    angles = jnp.arange(GRID_MAX, dtype=f32)[:, None] * omega[None, :]
    return jnp.concatenate([jnp.sin(angles), jnp.cos(angles)], axis=-1)


def time_embed(timesteps, model_width):
    half = model_width // 2
    freqs = jnp.exp(-math.log(10000.0) * jnp.arange(half, dtype=f32) / half)
    angles = timesteps.astype(f32)[:, None] * freqs
    return jnp.concatenate([jnp.cos(angles), jnp.sin(angles)], axis=-1)


def time_columns(timesteps, first, number, model_width):
    half = model_width // 2
    column = first + jnp.arange(number, dtype=jnp.int32)
    freqs = jnp.exp(-math.log(10000.0) * (column % half).astype(f32) / half)
    angles = timesteps[:, None] * freqs
    return jnp.where(column < half, jnp.cos(angles), jnp.sin(angles))


def swap_tiles(value):
    return lax.ppermute(value, "tile", [(0, 1), (1, 0)])


def flip_stage(value, stage, orders, count):
    pairs = []
    for d in range(count):
        for t, order in enumerate(orders):
            pairs.append((2 * d + t, 2 * (d ^ (1 << order[stage])) + t))
    return lax.ppermute(value, ("dp", "tile"), pairs)


def relative_masks(order):
    bits = len(order)
    masks = []
    for rel in range(1 << bits):
        mask = 0
        for stage in range(bits):
            if (rel >> (bits - 1 - stage)) & 1:
                mask |= 1 << order[stage]
        masks.append(mask)
    return masks


def after(value, *others):
    return lax.optimization_barrier((value,) + others)[0]


CHUNK = 3
UNIT = 9
BOTH = {
    "x": (0, 1),
    "y": (1, 0),
    "1": (2, 2),
    "2": (3, 3),
}
PLAN = {
    "d0": "xy12",
    "d1": "xy12",
    "u0": "1xy2",
    "u1": "2xy1",
    "q0": "xy12",
    "q1": "xy12",
}
EVENTS = "d0 d1 u0 u1 d0 d1 q0 q1 d0 q0 s d1 u0 s q1 d0 u1 s q0 d1 s u0 q1 q0 u1 u0 u1 q1"


def unit_orders(plan):
    return tuple([BOTH[c][t] for c in plan] for t in (0, 1))


def dot_rows(left, right):
    return lax.dot_general(left, right, (((1,), (0,)), ((), ())), preferred_element_type=f32)


def row_kernel(part, ids_ref, left_ref, left_far_ref, right_ref, right_far_ref, out_ref):
    res = dot_rows(left_ref[0], right_ref[...])
    res = res + dot_rows(left_far_ref[0].astype(bf16), right_far_ref[...].astype(bf16))
    rows = out_ref.shape[2]
    for c in range(2):
        for h in range(4):
            out_ref[0, 4 * c + h] = res[h * rows : (h + 1) * rows, c * 128 : (c + 1) * 128]
    out_ref[0, 8, :, :64] = res[part * rows : (part + 1) * rows, 256:]
    out_ref[0, 8, :, 64:] = res[(part + 2) * rows : (part + 3) * rows, 256:]


def row_unit(ids, left, left_far, rights, part, low, number):
    _, rows, near = left.shape
    width = rights[0].shape[1]
    return pl.pallas_call(
        functools.partial(row_kernel, part),
        out_shape=jax.ShapeDtypeStruct((number, UNIT, rows // 4, 128), f32),
        grid_spec=pltpu.PrefetchScalarGridSpec(
            num_scalar_prefetch=1,
            grid=(number,),
            in_specs=[
                pl.BlockSpec((1, rows, near), lambda k, ids: (ids[low + k], 0, 0)),
                pl.BlockSpec((1, rows, near), lambda k, ids: (ids[low + k], 0, 0)),
                pl.BlockSpec((near, width), lambda k, ids: (0, 0)),
                pl.BlockSpec((near, width), lambda k, ids: (0, 0)),
            ],
            out_specs=pl.BlockSpec((1, UNIT, rows // 4, 128), lambda k, ids: (k, 0, 0, 0)),
        ),
        cost_estimate=pl.CostEstimate(
            flops=4 * number * rows * near * width,
            bytes_accessed=number * rows * (6 * near + 4 * width),
            transcendentals=0,
        ),
        name="row_unit",
    )(ids, left, left_far, *rights)


def column_kernel(border, first_tile, ids_ref, *refs):
    lefts, (right_ref, right_far_ref), (send_ref, keep_ref) = refs[:-5], refs[-5:-3], refs[-3:-1]
    stack_ref = refs[-1]
    number = len(lefts) // 2
    count, rows, near = lefts[0].shape
    half = count // 2 * rows
    step = pl.program_id(0)

    @pl.when(step == 0)
    def _():
        for i in range(number):
            for r in range(count):
                place = pl.ds(r * rows, rows)
                stack_ref[i, place, :near] = lefts[2 * i][ids_ref[r]]
                stack_ref[i, place, near:] = lefts[2 * i + 1][ids_ref[r]].astype(bf16)

    right = jnp.concatenate([right_ref[...], right_far_ref[...].astype(bf16)], axis=0)

    def write(kind):
        for ref, low in ((send_ref, half), (keep_ref, 0)):
            if kind == "first":
                res = dot_rows(stack_ref[0, low : low + half], right)
            elif kind == "last":
                res = dot_rows(stack_ref[1, low : low + half], right)
            else:
                start = (step * CHUNK + first_tile) * 128
                column = lax.broadcasted_iota(jnp.int32, (half, CHUNK * 128), 1) + start
                res = jnp.where(
                    column < border,
                    dot_rows(stack_ref[0, low : low + half], right),
                    dot_rows(stack_ref[1, low : low + half], right),
                )
            for r in range(count // 2):
                for c in range(CHUNK):
                    ref[r, c] = res[r * rows : (r + 1) * rows, c * 128 : (c + 1) * 128]

    if number == 1:
        write("first")
    else:
        begin = (step * CHUNK + first_tile) * 128
        end = begin + CHUNK * 128

        @pl.when(end <= border)
        def _():
            write("first")

        @pl.when(begin >= border)
        def _():
            write("last")

        @pl.when((end > border) & (begin < border))
        def _():
            write("mixed")


def column_unit(ids, lefts, right, right_far, part, border):
    count, rows, near = lefts[0].shape
    first_tile = part * UNIT
    first_chunk = first_tile // CHUNK
    whole = pl.BlockSpec((count, rows, near), lambda j, ids: (0, 0, 0))
    chunk = pl.BlockSpec((near, CHUNK * 128), lambda j, ids: (0, first_chunk + j))
    out = pl.BlockSpec((count // 2, CHUNK, rows, 128), lambda j, ids: (0, j, 0, 0))
    shape = jax.ShapeDtypeStruct((count // 2, UNIT, rows, 128), f32)
    number = len(lefts) // 2
    return pl.pallas_call(
        functools.partial(column_kernel, border, first_tile),
        out_shape=(shape, shape),
        grid_spec=pltpu.PrefetchScalarGridSpec(
            num_scalar_prefetch=1,
            grid=(UNIT // CHUNK,),
            in_specs=[whole] * len(lefts) + [chunk, chunk],
            out_specs=(out, out),
            scratch_shapes=[pltpu.VMEM((number, count * rows, 2 * near), bf16)],
        ),
        cost_estimate=pl.CostEstimate(
            flops=4 * count * rows * near * UNIT * 128,
            bytes_accessed=count * rows * (6 * near * number + 4 * UNIT * 128),
            transcendentals=0,
        ),
        name="column_unit",
    )(ids, *lefts, right, right_far)


class Halving:
    def __init__(self, send, keep, orders, count):
        self.flat = (-1, send.shape[1] * send.shape[2], 128)
        self.keep = keep
        self.message = send.reshape(self.flat)
        self.orders = orders
        self.count = count
        self.stages = len(orders[0])
        self.received = []

    def step(self, token):
        stage = len(self.received)
        if stage:
            if stage == 1:
                self.keep = self.keep().reshape(self.flat)
            low = 1 << (self.stages - 1 - stage)
            if token is not None:
                self.received[-1] = after(self.received[-1], token)
            message = self.keep[low : 2 * low]
            for piece in self.received:
                message = message + piece[low : 2 * low]
        else:
            message = self.message if token is None else after(self.message, token)
        self.received.append(flip_stage(message, stage, self.orders, self.count))
        return message

    def result(self):
        total = self.keep[0]
        for piece in self.received:
            total = total + piece[0]
        return total.reshape(UNIT, -1, 128)


def body(
    patches,
    bucket,
    keep_order,
    timesteps,
    labels,
    patch_weight,
    patch_bias,
    class_table,
    ada_weight,
    ada_bias,
    qkv_weight,
    query_bias,
    value_bias,
    proj_weight,
    proj_bias,
    up_weight,
    up_bias,
    down_weight,
    down_bias,
    final_weight,
    final_bias,
    out_grad,
):
    images, tile_slots, patch_width = patches.shape
    slot_total = keep_order.shape[1]
    width = patch_weight.shape[1]
    hidden = up_weight.shape[1]
    class_count = class_table.shape[0]
    count = lax.axis_size("dp")
    bits = count.bit_length() - 1
    tile = lax.axis_index("tile")
    own = images // 2
    half_slots = slot_total // 2
    first = tile * own

    def mine(value):
        return lax.dynamic_slice_in_dim(value, first, own, 0)

    def others(value):
        return lax.dynamic_slice_in_dim(value, own - first, own, 0)

    unit = (bucket[0] >= 0).astype(f32)

    pair = jnp.concatenate([patches, out_grad], axis=2).astype(f32)
    slots_data = jnp.concatenate([mine(pair), swap_tiles(others(pair)) * unit], axis=1).astype(bf16)
    near = jnp.arange(slot_total, dtype=jnp.int32)
    slot_ids = (near + tile * tile_slots) % slot_total

    condition = time_embed(timesteps, width) + jnp.take(class_table, labels, axis=0).astype(f32)
    cond_act = jax.nn.silu(condition).astype(bf16)
    mod_half = mm("id,de->ie", cond_act, ada_weight) + ada_bias.astype(f32)
    mod_mine, mod_recv = mine(mod_half), swap_tiles(others(mod_half))
    modulation = jnp.where(
        tile == 0,
        jnp.concatenate([mod_mine, mod_recv], axis=1),
        jnp.concatenate([mod_recv, mod_mine], axis=1),
    )
    shift_a, scale_a, gate_a, shift_m, scale_m, gate_m = [
        portion[:, None, :] for portion in jnp.split(modulation, 6, axis=1)
    ]

    my_bucket, my_order = mine(bucket), mine(keep_order)
    half_rows = jnp.where(my_bucket == 0, 8, jnp.where(my_bucket == 1, 6, 10))[:, None]
    columns = jnp.where(my_bucket == 0, 16, jnp.where(my_bucket == 1, 20, 12))[:, None]
    area = half_rows * columns
    order_valid = (my_order % tile_slots) < area
    upper = (near[:, None] < near[None, :]).astype(bf16)
    rank = mm("ij,jk->ik", order_valid.astype(bf16), upper).astype(jnp.int32)
    limit = area
    place = jnp.where(rank < limit, rank, rank - limit + half_slots)
    hit = (place[:, None, :] == near[None, :, None]) & order_valid[:, None, :]
    row_slot = jnp.sum(jnp.where(hit, my_order[:, None, :] + 1, 0), axis=2) - 1
    live = row_slot >= 0
    select = (row_slot[:, :, None] == slot_ids[None, None, :]).astype(bf16)
    row_data = mm("irs,isc->irc", select, slots_data).astype(bf16)
    row_patches, row_grads = row_data[:, :, :patch_width], row_data[:, :, patch_width:]
    local = row_slot % tile_slots
    grid_row = (row_slot // tile_slots) * half_rows + local // columns
    grid_col = local % columns
    marks = jnp.arange(GRID_MAX, dtype=jnp.int32)
    mark_row = (grid_row[:, :, None] == marks).astype(bf16)
    mark_col = (grid_col[:, :, None] == marks).astype(bf16)
    table = three_way(axis_table(width // 2))
    blank = jnp.zeros((GRID_MAX, width // 2), bf16)
    wide = jnp.concatenate(
        [patch_weight]
        + [jnp.concatenate([piece, blank], axis=1) for piece in table]
        + [jnp.concatenate([blank, piece], axis=1) for piece in table],
        axis=0,
    )
    features = jnp.concatenate([row_patches] + [mark_row] * 3 + [mark_col] * 3, axis=2)
    embedded = mm("irk,kd->ird", features, wide) + patch_bias.astype(f32)
    key_live = live[:, :half_slots]

    kept_x = embedded[:, :half_slots]
    normed_a, rstd_a = norm_stats(kept_x)
    attn_in = (normed_a * (1.0 + scale_a) + shift_a).astype(bf16)
    qkv_bias = jnp.concatenate([query_bias, jnp.zeros_like(query_bias), value_bias]).astype(f32)
    qkv = (mm("isd,de->ise", attn_in, qkv_weight) + qkv_bias).astype(bf16)
    queries, keys, values = [split_heads(part) for part in jnp.split(qkv, 3, axis=2)]
    scaling = (width // HEADS) ** (-0.5)
    scores = mm("gqhd,gkhd->ghqk", queries, keys) * scaling
    scores = jnp.where(key_live[:, None, None, :], scores, -1e30)
    powers = jnp.exp(scores - jnp.max(scores, axis=-1, keepdims=True))
    probs = powers / jnp.sum(powers, axis=-1, keepdims=True)
    probs_low = probs.astype(bf16)
    mixed = mm("ghqk,gkhd->gqhd", probs_low, values).reshape(kept_x.shape).astype(bf16)
    attn_out = mm("iqd,de->iqe", mixed, proj_weight) + proj_bias.astype(f32)
    middle = kept_x + gate_a * attn_out
    normed_m, rstd_m = norm_stats(middle)
    mlp_in = (normed_m * (1.0 + scale_m) + shift_m).astype(bf16)
    pre_act = mm("iqd,df->iqf", mlp_in, up_weight) + up_bias.astype(f32)
    act_value, act_slope = gelu_parts(pre_act)
    activated = act_value.astype(bf16)
    mlp_out = mm("iqf,fd->iqd", activated, down_weight) + down_bias.astype(f32)
    block_out = middle + gate_m * mlp_out
    merged = jnp.concatenate([block_out, embedded[:, half_slots:]], axis=1)
    normed_f, rstd_f = norm_stats(merged)
    final_in = normed_f.astype(bf16)
    row_denoised = mm("isd,dp->isp", final_in, final_weight) + final_bias.astype(f32)

    final_weight_grad = mm("isd,isp->dp", final_in, row_grads)
    final_bias_grad = jnp.sum(row_grads.astype(f32), axis=(0, 1))
    d_final = mm("isp,dp->isd", row_grads, final_weight)
    d_merged = norm_back(normed_f, rstd_f, d_final)
    d_block = d_merged[:, :half_slots]
    d_mlp = (gate_m * d_block).astype(bf16)
    d_gate_m = jnp.sum(d_block * mlp_out, axis=1)

    fast = count == 16 and (width // count) % 8 == 0 and images * slot_total == 1024
    index = lax.axis_index("dp")

    def unit_ids(orders):
        masks = [jnp.array(relative_masks(order), jnp.int32) for order in orders]
        return jnp.where(tile == 0, masks[0], masks[1]) ^ index

    def left_blocks(left):
        rows, size = left.shape[0] * left.shape[1], left.shape[2]
        blocks = left.reshape(rows, count, size // count).transpose(1, 2, 0)
        return blocks, swap_tiles(blocks.astype(f32))

    def right_half(right):
        rows, size = right.shape[0] * right.shape[1], right.shape[2] // 2
        right = right.reshape(rows, 2 * size)
        keep = lax.dynamic_slice_in_dim(right, tile * size, size, 1)
        give = lax.dynamic_slice_in_dim(right, (1 - tile) * size, size, 1)
        return keep, swap_tiles(give.astype(f32))

    def plain(left, right):
        (near_left, far_left), (near_right, far_right) = left, right
        far_left, far_right = (far_left * unit).astype(bf16), (far_right * unit).astype(bf16)
        grad = mm("brk,kc->brc", near_left, near_right) + mm("brk,kc->brc", far_left, far_right)
        grad = grad.reshape(-1, grad.shape[2])
        return lax.psum_scatter(grad, "dp", scatter_dimension=0, tiled=True)

    chains = {}

    def down_units(left, right):
        for part in (0, 1):
            orders = unit_orders(PLAN["d%d" % part])
            ids = unit_ids(orders)
            rights = [
                jnp.concatenate(
                    [item[:, 256 * part : 256 * part + 256], item[:, 512:]], axis=1
                )
                for item in right
            ]
            send = row_unit(ids, *left, rights, part, count // 2, count // 2)
            keep = functools.partial(row_unit, ids, *left, rights, part, 0, count // 2)
            chains["d%d" % part] = Halving(send, keep, orders, count)

    def column_units(name, lefts, right, border):
        for part in (0, 1):
            orders = unit_orders(PLAN[name + str(part)])
            own = lefts if part or border is None else lefts[:2]
            send, keep = column_unit(unit_ids(orders), own, *right, part, border)
            chains[name + str(part)] = Halving(send, lambda keep=keep: keep, orders, count)

    down_left, down_right = left_blocks(activated), right_half(d_mlp)
    if fast:
        down_units(down_left, down_right)
    else:
        down_final = plain(down_left, down_right)
    down_bias_grad = jnp.sum(d_mlp.astype(f32), axis=(0, 1))
    d_activated = mm("iqd,fd->iqf", d_mlp, down_weight)
    d_pre = (d_activated * act_slope).astype(bf16)
    up_left, up_right = left_blocks(mlp_in), right_half(d_pre)
    if fast:
        column_units("u", up_left, up_right, None)
    else:
        up_final = plain(up_left, up_right)
    up_bias_grad = jnp.sum(d_pre.astype(f32), axis=(0, 1))
    d_mlp_in = mm("iqf,df->iqd", d_pre, up_weight)
    d_shift_m = jnp.sum(d_mlp_in, axis=1)
    d_scale_m = jnp.sum(d_mlp_in * normed_m, axis=1)
    d_middle = d_block + norm_back(normed_m, rstd_m, d_mlp_in * (1.0 + scale_m))
    d_attn = (gate_a * d_middle).astype(bf16)
    d_gate_a = jnp.sum(d_middle * attn_out, axis=1)
    proj_left, proj_right = left_blocks(mixed), right_half(d_attn)
    proj_bias_grad = jnp.sum(d_attn.astype(f32), axis=(0, 1))
    d_mixed = split_heads(mm("iqe,de->iqd", d_attn, proj_weight).astype(bf16))
    d_probs = mm("gqhd,gkhd->ghqk", d_mixed, values)
    row_delta = jnp.sum(probs * d_probs, axis=-1, keepdims=True)
    d_scores = (probs * (d_probs - row_delta)).astype(bf16)
    d_query = mm("ghqk,gkhd->gqhd", d_scores, keys) * scaling
    d_key = mm("ghqk,gqhd->gkhd", d_scores, queries) * scaling
    d_value = mm("ghqk,gqhd->gkhd", probs_low, d_mixed)
    d_qkv = jnp.concatenate(
        [part.reshape(kept_x.shape) for part in (d_query, d_key, d_value)], axis=2
    ).astype(bf16)
    qkv_left, qkv_right = left_blocks(attn_in), right_half(d_qkv)
    border = qkv_right[0].shape[1]
    if fast:
        both_right = [jnp.concatenate(pair, axis=1) for pair in zip(qkv_right, proj_right)]
        column_units("q", qkv_left + proj_left, both_right, border)
    else:
        proj_final, qkv_final = plain(proj_left, proj_right), plain(qkv_left, qkv_right)
    qkv_bias_sums = jnp.sum(d_qkv.astype(f32), axis=(0, 1))
    d_attn_in = mm("ice,de->icd", d_qkv, qkv_weight)
    d_shift_a = jnp.sum(d_attn_in, axis=1)
    d_scale_a = jnp.sum(d_attn_in * normed_a, axis=1)
    d_kept = d_middle + norm_back(normed_a, rstd_a, d_attn_in * (1.0 + scale_a))
    d_low = jnp.concatenate([d_kept, d_merged[:, half_slots:]], axis=1).astype(bf16)
    row_patch_grad = mm("isd,pd->isp", d_low, patch_weight)
    patch_weight_grad = mm("isp,isd->pd", row_patches, d_low)
    patch_bias_grad = jnp.sum(d_low.astype(f32), axis=(0, 1))

    back = jnp.concatenate([row_denoised, row_patch_grad], axis=2)
    slot_out = jnp.einsum("irs,irc->isc", select.astype(f32), back, precision=highest)
    near_part, far_part = slot_out[:, :tile_slots], swap_tiles(slot_out[:, tile_slots:])
    slot_mine = jnp.where(
        tile == 0,
        jnp.concatenate([near_part, far_part], axis=0),
        jnp.concatenate([far_part, near_part], axis=0),
    )
    denoised, patch_grad = slot_mine[:, :, :patch_width], slot_mine[:, :, patch_width:]

    d_mod = jnp.concatenate(
        [d_shift_a, d_scale_a, d_gate_a, d_shift_m, d_scale_m, d_gate_m], axis=1
    )
    mod_width = d_mod.shape[1] // 2
    keep = lax.dynamic_slice_in_dim(d_mod, tile * mod_width, mod_width, 1)
    give = lax.dynamic_slice_in_dim(d_mod, (1 - tile) * mod_width, mod_width, 1)
    got = swap_tiles(give) * unit
    d_mod_half = jnp.where(
        tile == 0, jnp.concatenate([keep, got], axis=0), jnp.concatenate([got, keep], axis=0)
    ).astype(bf16)
    d_cond_act = mm("ie,de->id", d_mod_half, ada_weight)
    gate = jax.nn.sigmoid(condition)
    d_cond_part = d_cond_act * (gate * (1.0 + condition * (1.0 - gate)))
    d_condition = d_cond_part + swap_tiles(d_cond_part)

    small = [
        patch_weight_grad,
        patch_bias_grad,
        qkv_bias_sums[:width],
        qkv_bias_sums[2 * width :],
        proj_bias_grad,
        up_bias_grad,
        down_bias_grad,
        final_weight_grad,
        final_bias_grad,
    ]
    area_all = jnp.where(bucket == 0, 128, 120)
    counts_local = jnp.stack([jnp.sum(area_all), jnp.sum(2 * area_all)]).astype(f32) * 0.5
    flat = jnp.concatenate([leaf.reshape(-1) for leaf in small] + [counts_local])
    flat = jnp.pad(flat, (0, (-flat.shape[0]) % 2048)).reshape(2, -1, 128)
    flat_half = lax.dynamic_index_in_dim(flat, tile, 0, keepdims=False) + swap_tiles(
        lax.dynamic_index_in_dim(flat, 1 - tile, 0, keepdims=False)
    )
    lines = flat_half.shape[0]
    marks = jnp.stack([labels, timesteps], axis=1).astype(f32)
    packed = jnp.concatenate(
        [d_mod_half.astype(f32), d_condition, jnp.pad(marks, ((0, 0), (0, 126)))], axis=1
    )
    message = jnp.concatenate([flat_half, packed.reshape(-1, 128)], axis=0)
    tail = list(range(2, bits))[::-1]
    small_orders = (tail + [0, 1], tail + [1, 0])
    small_stage = 0

    def small_step(message, stage, token):
        if token is not None:
            message = after(message, token)
        got = flip_stage(message, stage, small_orders, count)
        return jnp.concatenate(
            [message[:lines] + got[:lines], message[lines:], got[lines:]], axis=0
        )

    token = None
    if fast:
        for event in EVENTS.split():
            if event == "s":
                message = small_step(message, small_stage, token)
                small_stage += 1
            else:
                token = chains[event].step(token)
    while small_stage < bits:
        message = small_step(message, small_stage, None)
        small_stage += 1

    every = (message[lines:] * unit).reshape(count * images, -1)
    all_mod = every[:, :mod_width].astype(bf16)
    all_cond = every[:, mod_width : mod_width + width]
    all_label = every[:, mod_width + width].astype(jnp.int32)
    all_time = every[:, mod_width + width + 1]
    one_hot = (all_label[:, None] == jnp.arange(class_count, dtype=jnp.int32)[None, :])
    block = width // count
    table_rows = lax.dynamic_slice_in_dim(class_table, index * block, block, 1)
    picked = mm("nc,cd->nd", one_hot.astype(bf16), table_rows)
    act_rows = time_columns(all_time, index * block, block, width) + picked
    act_rows = jax.nn.silu(act_rows).astype(bf16)
    ada_final = mm("nd,ne->de", act_rows, all_mod)
    ada_half = jnp.sum(all_mod.astype(f32), axis=0)
    ending = jnp.concatenate([message[:lines], ada_half.reshape(-1, 128)], axis=0)
    other = swap_tiles(ending)
    first_end = jnp.where(tile == 0, ending, other)
    second_end = jnp.where(tile == 0, other, ending)
    ada_bias_sum = jnp.concatenate(
        [first_end[lines:].reshape(-1), second_end[lines:].reshape(-1)]
    )
    summed = jnp.concatenate([first_end[:lines].reshape(-1), second_end[:lines].reshape(-1)])
    sums = []
    offset = 0
    for leaf in small + [counts_local]:
        sums.append(summed[offset : offset + leaf.size].reshape(leaf.shape))
        offset += leaf.size
    class_table_sum = jnp.einsum("nc,nd->cd", one_hot.astype(f32), all_cond, precision=highest)

    if fast:
        first_part, second_part = chains["d0"].result(), chains["d1"].result()
        wide = [
            item[:8].reshape(2, 4, -1, 128).transpose(1, 2, 0, 3).reshape(-1, 256)
            for item in (first_part, second_part)
        ]
        rest = jnp.concatenate(
            [
                first_part[8, :, :64],
                second_part[8, :, :64],
                first_part[8, :, 64:],
                second_part[8, :, 64:],
            ],
            axis=0,
        )
        down_final = jnp.concatenate(wide + [rest], axis=1)

        def columns_of(name):
            tiles = jnp.concatenate([chains[name + "0"].result(), chains[name + "1"].result()])
            return tiles.transpose(1, 0, 2).reshape(tiles.shape[1], -1)

        up_final = columns_of("u")
        joint = columns_of("q")
        qkv_final, proj_final = joint[:, :border], joint[:, border:]
    (
        patch_weight_sum,
        patch_bias_sum,
        query_bias_sum,
        value_bias_sum,
        proj_bias_sum,
        up_bias_sum,
        down_bias_sum,
        final_weight_sum,
        final_bias_sum,
        token_counts,
    ) = sums
    return (
        denoised,
        patch_grad,
        patch_weight_sum,
        patch_bias_sum,
        class_table_sum,
        ada_final,
        ada_bias_sum,
        qkv_final,
        query_bias_sum,
        value_bias_sum,
        proj_final,
        proj_bias_sum,
        up_final,
        up_bias_sum,
        down_final,
        down_bias_sum,
        final_weight_sum,
        final_bias_sum,
        token_counts,
    )


def solution(mesh):
    in_specs = (
        P("dp", "tile", None),
        P("dp"),
        P("dp", None),
        P("dp"),
        P("dp"),
        P(),
        P(),
        P(),
        P(None, "tile"),
        P("tile"),
        P(),
        P(),
        P(),
        P(),
        P(),
        P(),
        P(),
        P(),
        P(),
        P(),
        P(),
        P("dp", "tile", None),
    )
    out_specs = (
        P("dp", "tile", None),
        P("dp", "tile", None),
        P(),
        P(),
        P(),
        P("dp", "tile"),
        P(),
        P("dp", "tile"),
        P(),
        P(),
        P("dp", "tile"),
        P(),
        P("dp", "tile"),
        P(),
        P("dp", "tile"),
        P(),
        P(),
        P(),
        P(),
    )
    return jax.shard_map(body, mesh=mesh, in_specs=in_specs, out_specs=out_specs, check_vma=False)
```

```python
import functools
import math

import jax
import jax.numpy as jnp
from jax import lax
from jax.experimental import pallas as pl
from jax.experimental.pallas import tpu as pltpu
from jax.sharding import PartitionSpec as P

HEADS = 16
GRID_MAX = 32
epsilon = 1e-06
highest = lax.Precision.HIGHEST
f32 = jnp.float32
bf16 = jnp.bfloat16


def mm(spec, left, right):
    return jnp.einsum(spec, left, right, preferred_element_type=f32)


def norm_stats(values):
    center = values - jnp.mean(values, axis=-1, keepdims=True)
    rstd = lax.rsqrt(jnp.mean(center * center, axis=-1, keepdims=True) + epsilon)
    return center * rstd, rstd


def norm_back(normed, rstd, grad):
    return rstd * (
        grad
        - jnp.mean(grad, axis=-1, keepdims=True)
        - normed * jnp.mean(grad * normed, axis=-1, keepdims=True)
    )


def gelu_parts(u):
    inner = 0.7978845608028654 * (u + 0.044715 * u * u * u)
    th = jnp.tanh(inner)
    value = 0.5 * u * (1.0 + th)
    slope = 0.5 * (1.0 + th) + 0.5 * u * (1.0 - th * th) * 0.7978845608028654 * (
        1.0 + 3.0 * 0.044715 * u * u
    )
    return value, slope


def three_way(table):
    parts = []
    rest = table
    for _ in range(3):
        piece = rest.astype(bf16)
        parts.append(piece)
        rest = rest - piece.astype(f32)
    return parts


def axis_table(width):
    quarter = width // 2
    omega = jnp.exp(-math.log(10000.0) * jnp.arange(quarter, dtype=f32) / quarter)
    angles = jnp.arange(GRID_MAX, dtype=f32)[:, None] * omega[None, :]
    return jnp.concatenate([jnp.sin(angles), jnp.cos(angles)], axis=-1)


def time_embed(timesteps, model_width):
    half = model_width // 2
    freqs = jnp.exp(-math.log(10000.0) * jnp.arange(half, dtype=f32) / half)
    angles = timesteps.astype(f32)[:, None] * freqs
    return jnp.concatenate([jnp.cos(angles), jnp.sin(angles)], axis=-1)


def time_columns(timesteps, first, number, model_width):
    half = model_width // 2
    column = first + jnp.arange(number, dtype=jnp.int32)
    freqs = jnp.exp(-math.log(10000.0) * (column % half).astype(f32) / half)
    angles = timesteps[:, None] * freqs
    return jnp.where(column < half, jnp.cos(angles), jnp.sin(angles))


def swap_tiles(value):
    return lax.ppermute(value, "tile", [(0, 1), (1, 0)])


def flip_stage(value, stage, orders, count):
    pairs = []
    for d in range(count):
        for t, order in enumerate(orders):
            pairs.append((2 * d + t, 2 * (d ^ (1 << order[stage])) + t))
    return lax.ppermute(value, ("dp", "tile"), pairs)


def relative_masks(order):
    bits = len(order)
    masks = []
    for rel in range(1 << bits):
        mask = 0
        for stage in range(bits):
            if (rel >> (bits - 1 - stage)) & 1:
                mask |= 1 << order[stage]
        masks.append(mask)
    return masks


def after(value, *others):
    return lax.optimization_barrier((value,) + others)[0]


CHUNK = 3
UNIT = 9
BOTH = {
    "x": (0, 1),
    "y": (1, 0),
    "1": (2, 2),
    "2": (3, 3),
}
PLAN = {
    "d0": "x1y2",
    "d1": "1x2y",
    "u0": "xy12",
    "u1": "xy12",
    "q0": "xy12",
    "q1": "xy12",
}
ORDER = """
Kd0 d0 Kd1 d1 Cp Ct Ku0 u0 Ku1 C1 u1 C2 k0 d0 k1 u0 d1 u1 Cq Kq0 Kq1 u0 q1 C3 d0 d1 u0 q0 u1 C4
q1 s d1 u1 s u0 s q1 q0 u1 d0 d1 s q1 q0 q1 s C5 q0 d0 q0
"""


def unit_orders(plan):
    return tuple([BOTH[c][t] for c in plan] for t in (0, 1))


def dot_rows(left, right):
    return lax.dot_general(left, right, (((1,), (0,)), ((), ())), preferred_element_type=f32)


def halves_kernel(tile_ref, *refs):
    number = len(refs) - 2
    keep_ref, give_ref = refs[-2:]

    def write(own):
        start = 0
        for ref in refs[:number]:
            size = ref.shape[1] // 2
            place = slice(start, start + size)
            keep_ref[:, place] = ref[:, own * size : (own + 1) * size]
            give_ref[:, place] = ref[:, (1 - own) * size : (2 - own) * size].astype(f32)
            start += size
        if start < give_ref.shape[1]:
            rest = give_ref.shape[1] - start
            give_ref[:, start:] = jnp.zeros((give_ref.shape[0], rest), f32)

    for own in (0, 1):
        pl.when(tile_ref[0] == own)(functools.partial(write, own))


def halves(tile, *values):
    rows = values[0].shape[0]
    size = sum(value.shape[1] for value in values) // 2
    padded = -(-size // 128) * 128
    return pl.pallas_call(
        halves_kernel,
        out_shape=(
            jax.ShapeDtypeStruct((rows, size), bf16),
            jax.ShapeDtypeStruct((rows, padded), f32),
        ),
        grid_spec=pltpu.PrefetchScalarGridSpec(
            num_scalar_prefetch=1,
            grid=(1,),
            in_specs=[pl.BlockSpec(value.shape, lambda i, tile: (0, 0)) for value in values],
            out_specs=(
                pl.BlockSpec((rows, size), lambda i, tile: (0, 0)),
                pl.BlockSpec((rows, padded), lambda i, tile: (0, 0)),
            ),
        ),
        cost_estimate=pl.CostEstimate(flops=1, bytes_accessed=1, transcendentals=0),
        compiler_params=pltpu.CompilerParams(vmem_limit_bytes=12 * 2**20),
        name="halves",
    )(tile[None], *values)


def turned(value):
    size = value.shape[1]
    row = lax.broadcasted_iota(jnp.int32, (size, size), 0)
    column = lax.broadcasted_iota(jnp.int32, (size, size), 1)
    identity = jnp.where(row == column, 1.0, 0.0).astype(bf16)
    return dot_columns(identity, value)


def turn_kernel(in_ref, out_ref):
    out_ref[...] = turned(in_ref[...])


def turn(value):
    rows, size = value.shape
    chunk = 384
    return pl.pallas_call(
        turn_kernel,
        out_shape=jax.ShapeDtypeStruct((size, rows), f32),
        grid=(size // chunk,),
        in_specs=[pl.BlockSpec((rows, chunk), lambda j: (0, j))],
        out_specs=pl.BlockSpec((chunk, rows), lambda j: (j, 0)),
        cost_estimate=pl.CostEstimate(flops=1, bytes_accessed=1, transcendentals=0),
        compiler_params=pltpu.CompilerParams(vmem_limit_bytes=5 * 2**20),
        name="turn",
    )(value)


def row_kernel(part, ranges, pair, ids_ref, *refs):
    near = [refs[i][0].astype(bf16) for i in range(pair)]
    far = [refs[pair + i][0].astype(bf16) for i in range(pair)]
    right_ref, right_far_ref = refs[2 * pair : 2 * pair + 2]
    out_refs = refs[2 * pair + 2 :]
    size = near[0].shape[0]
    cut = slice(256, right_ref.shape[1]) if part else slice(0, 256)
    res = dot_rows(jnp.concatenate(near, axis=0), right_ref[:, cut])
    res = res + dot_rows(jnp.concatenate(far, axis=0), right_far_ref[:, cut].astype(bf16))
    rows = size // 4
    step = pl.program_id(0) * pair + ranges[0][0]

    def write(ref, place, base):
        for c in range(2):
            for h in range(4):
                top = base + h * rows
                ref[place, 4 * c + h] = res[top : top + rows, c * 128 : (c + 1) * 128]
        if part:
            for h in range(2):
                top = base + h * rows
                ref[place, 8 + h, :, :64] = res[top : top + rows, 256:]
                top = base + (h + 2) * rows
                ref[place, 8 + h, :, 64:] = res[top : top + rows, 256:]

    for ref, (low, high) in zip(out_refs, ranges):
        block = min(high - low, pair)

        def body(ref=ref, low=low, block=block):
            for i in range(block):
                write(ref, i, (i + (low % pair)) * size)

        pl.when((step + pair > low) & (step < high))(body)


def row_unit(ids, left, left_far, rights, part, ranges):
    _, rows, near = left.shape
    pieces = 8 + 2 * part
    pair = 2
    first, number = ranges[0][0], ranges[-1][1] - ranges[0][0]

    def place(low, high):
        block = min(high - low, pair)
        last = (high - low) // block - 1
        return lambda k, ids: (jnp.clip((k * pair + first - low) // block, 0, last), 0, 0, 0)

    def source(i):
        return pl.BlockSpec((1, rows, near), lambda k, ids: (ids[first + k * pair + i], 0, 0))

    return pl.pallas_call(
        functools.partial(row_kernel, part, ranges, pair),
        out_shape=tuple(
            jax.ShapeDtypeStruct((high - low, pieces, rows // 4, 128), f32) for low, high in ranges
        ),
        grid_spec=pltpu.PrefetchScalarGridSpec(
            num_scalar_prefetch=1,
            grid=(number // pair,),
            in_specs=[source(i % pair) for i in range(2 * pair)]
            + [
                pl.BlockSpec((near, item.shape[1]), lambda k, ids: (0, 0)) for item in rights
            ],
            out_specs=tuple(
                pl.BlockSpec((min(high - low, pair), pieces, rows // 4, 128), place(low, high))
                for low, high in ranges
            ),
        ),
        cost_estimate=pl.CostEstimate(flops=1, bytes_accessed=1, transcendentals=0),
        compiler_params=pltpu.CompilerParams(vmem_limit_bytes=14 * 2**20),
        name="row_unit",
    )(ids, *[left] * pair, *[left_far] * pair, *rights)


def column_kernel(border, first_tile, ranges, number, ids_ref, *refs):
    lefts, (right_ref, right_far_ref) = refs[: 2 * number], refs[2 * number : 2 * number + 2]
    out_refs, stack_ref = refs[2 * number + 2 : -1], refs[-1]
    count, rows, near = lefts[0].shape
    half = count // 2 * rows
    step = pl.program_id(0)

    @pl.when(step == 0)
    def _():
        for i in range(number):
            for r in range(count):
                place = pl.ds(r * rows, rows)
                stack_ref[i, place, :near] = lefts[2 * i][ids_ref[r]].astype(bf16)
                stack_ref[i, place, near:] = lefts[2 * i + 1][ids_ref[r]].astype(bf16)

    right = jnp.concatenate([right_ref[...], right_far_ref[...].astype(bf16)], axis=0)

    def write(kind):
        for base in (half, 0):
            stack = [stack_ref[i, base : base + half] for i in range(number)]
            if kind == "first":
                res = dot_rows(stack[0], right)
            elif kind == "last":
                res = dot_rows(stack[1], right)
            else:
                start = (step * CHUNK + first_tile) * 128
                column = lax.broadcasted_iota(jnp.int32, (half, CHUNK * 128), 1) + start
                res = jnp.where(
                    column < border, dot_rows(stack[0], right), dot_rows(stack[1], right)
                )
            for ref, (low, high) in zip(out_refs, ranges):
                if base <= low * rows < base + half:
                    for r in range(low, high):
                        top = r * rows - base
                        for c in range(CHUNK):
                            ref[r - low, c] = res[top : top + rows, c * 128 : (c + 1) * 128]

    if number == 1:
        write("first")
    else:
        begin = (step * CHUNK + first_tile) * 128
        end = begin + CHUNK * 128

        @pl.when(end <= border)
        def _():
            write("first")

        @pl.when(begin >= border)
        def _():
            write("last")

        @pl.when((end > border) & (begin < border))
        def _():
            write("mixed")


def column_unit(ids, lefts, right, right_far, part, border, ranges):
    count, rows, near = lefts[0].shape
    first_tile = part * UNIT
    first_chunk = first_tile // CHUNK
    whole = pl.BlockSpec((count, rows, near), lambda j, ids: (0, 0, 0))
    chunk = pl.BlockSpec((near, CHUNK * 128), lambda j, ids: (0, first_chunk + j))
    number = len(lefts) // 2
    return pl.pallas_call(
        functools.partial(column_kernel, border, first_tile, ranges, number),
        out_shape=tuple(
            jax.ShapeDtypeStruct((high - low, UNIT, rows, 128), f32) for low, high in ranges
        ),
        grid_spec=pltpu.PrefetchScalarGridSpec(
            num_scalar_prefetch=1,
            grid=(UNIT // CHUNK,),
            in_specs=[whole] * len(lefts) + [chunk, chunk],
            out_specs=tuple(
                pl.BlockSpec((high - low, CHUNK, rows, 128), lambda j, ids: (0, j, 0, 0))
                for low, high in ranges
            ),
            scratch_shapes=[pltpu.VMEM((number, count * rows, 2 * near), bf16)],
        ),
        cost_estimate=pl.CostEstimate(flops=1, bytes_accessed=1, transcendentals=0),
        compiler_params=pltpu.CompilerParams(vmem_limit_bytes=(10 + 8 * number) * 2**20),
        name="column_unit",
    )(ids, *lefts, right, right_far)


SENDS = ((8, 16),)
KEEPS = ((0, 1), (1, 2), (2, 4), (4, 8))


PIECE = 512


def in_hbm(value):
    return pltpu.with_memory_space_constraint(value, pltpu.HBM)


def up_kernel(in_ref, weight_ref, bias_ref, act_ref, slope_ref, turned_ref):
    for low in range(0, PIECE, 256):
        place = slice(low, low + 256)
        pre = dot_rows(in_ref[...], weight_ref[:, place]) + bias_ref[:, place]
        value, slope = gelu_parts(pre)
        value = value.astype(bf16)
        act_ref[:, place] = value
        slope_ref[:, place] = slope
        turned_ref[place, :] = value.T.astype(f32)


def feed_up(value, weight, bias):
    rows, width = value.shape
    hidden = weight.shape[1]
    return pl.pallas_call(
        up_kernel,
        out_shape=(
            jax.ShapeDtypeStruct((rows, hidden), bf16),
            jax.ShapeDtypeStruct((rows, hidden), f32),
            jax.ShapeDtypeStruct((hidden, rows), f32),
        ),
        grid=(hidden // PIECE,),
        in_specs=[
            pl.BlockSpec((rows, width), lambda j: (0, 0)),
            pl.BlockSpec((width, PIECE), lambda j: (0, j)),
            pl.BlockSpec((1, PIECE), lambda j: (0, j)),
        ],
        out_specs=(
            pl.BlockSpec((rows, PIECE), lambda j: (0, j)),
            pl.BlockSpec((rows, PIECE), lambda j: (0, j)),
            pl.BlockSpec((PIECE, rows), lambda j: (j, 0)),
        ),
        cost_estimate=pl.CostEstimate(flops=1, bytes_accessed=1, transcendentals=0),
        compiler_params=pltpu.CompilerParams(vmem_limit_bytes=11 * 2**20),
        name="feed_up",
    )(value, weight, bias[None].astype(f32))


def down_back_kernel(grad_ref, weight_ref, slope_ref, out_ref):
    out_ref[...] = (dot_columns(grad_ref[...], weight_ref[...]) * slope_ref[...]).astype(bf16)


def feed_back(grad, weight, slope):
    rows, width = grad.shape
    hidden = weight.shape[0]
    return pl.pallas_call(
        down_back_kernel,
        out_shape=jax.ShapeDtypeStruct((rows, hidden), bf16),
        grid=(hidden // PIECE,),
        in_specs=[
            pl.BlockSpec((rows, width), lambda j: (0, 0)),
            pl.BlockSpec((PIECE, width), lambda j: (j, 0)),
            pl.BlockSpec((rows, PIECE), lambda j: (0, j)),
        ],
        out_specs=pl.BlockSpec((rows, PIECE), lambda j: (0, j)),
        cost_estimate=pl.CostEstimate(flops=1, bytes_accessed=1, transcendentals=0),
        compiler_params=pltpu.CompilerParams(vmem_limit_bytes=8 * 2**20),
        name="feed_back",
    )(grad, in_hbm(weight), slope)


def head_window(head, size, width):
    start = min(head * size // 128 * 128, width - 256)
    return start, head * size - start


def head_mask(low, size):
    lane = lax.broadcasted_iota(jnp.int32, (1, 256), 1)
    return (lane >= low) & (lane < low + size)


def dot_columns(left, right):
    return lax.dot_general(left, right, (((1,), (1,)), ((), ())), preferred_element_type=f32)


def head_probs(queries, keys, mask, live, scaling):
    masked = queries * mask.astype(f32).astype(bf16)
    scores = jnp.where(live > 0.0, dot_columns(masked, keys) * scaling, -1e30)
    powers = jnp.exp(scores - jnp.max(scores, axis=1, keepdims=True))
    return powers / jnp.sum(powers, axis=1, keepdims=True)


def attend_kernel(qkv_ref, live_ref, out_ref, total_ref):
    width = out_ref.shape[1]
    size = width // HEADS
    live = live_ref[0]
    for head in range(HEADS):
        start, low = head_window(head, size, width)
        mask = head_mask(low, size)
        queries, keys, values = [
            qkv_ref[:, part * width + start : part * width + start + 256] for part in range(3)
        ]
        probs = head_probs(queries, keys, mask, live, size ** (-0.5)).astype(bf16)
        mixed = dot_rows(probs, values)
        place = slice(start, start + 256)
        total_ref[:, place] = jnp.where(mask, mixed, total_ref[:, place])
    out_ref[...] = total_ref[...].astype(bf16)


def attend(qkv, live):
    rows, wide = qkv.shape
    images = live.shape[0]
    near = rows // images
    width = wide // 3
    return pl.pallas_call(
        attend_kernel,
        out_shape=jax.ShapeDtypeStruct((rows, width), bf16),
        grid=(images,),
        in_specs=[
            pl.BlockSpec((near, wide), lambda i: (i, 0)),
            pl.BlockSpec((1, 1, near), lambda i: (i, 0, 0)),
        ],
        out_specs=pl.BlockSpec((near, width), lambda i: (i, 0)),
        scratch_shapes=[pltpu.VMEM((near, width), f32)],
        cost_estimate=pl.CostEstimate(flops=1, bytes_accessed=1, transcendentals=0),
        compiler_params=pltpu.CompilerParams(vmem_limit_bytes=8 * 2**20),
        name="attend",
    )(qkv, live)


def attend_back_kernel(qkv_ref, live_ref, grad_ref, out_ref, total_ref):
    width = grad_ref.shape[1]
    size = width // HEADS
    scaling = size ** (-0.5)
    live = live_ref[0]
    for head in range(HEADS):
        start, low = head_window(head, size, width)
        mask = head_mask(low, size)
        queries, keys, values = [
            qkv_ref[:, part * width + start : part * width + start + 256] for part in range(3)
        ]
        grads = grad_ref[:, start : start + 256]
        probs = head_probs(queries, keys, mask, live, scaling)
        d_probs = dot_columns(grads * mask.astype(f32).astype(bf16), values)
        delta = jnp.sum(probs * d_probs, axis=1, keepdims=True)
        d_scores = probs * (d_probs - delta)
        pieces = (
            dot_rows(d_scores.astype(bf16), keys) * scaling,
            dot_rows(d_scores.T.astype(bf16), queries) * scaling,
            dot_rows(probs.T.astype(bf16), grads),
        )
        for part, piece in enumerate(pieces):
            place = slice(part * width + start, part * width + start + 256)
            total_ref[:, place] = jnp.where(mask, piece, total_ref[:, place])
    out_ref[...] = total_ref[...].astype(bf16)


def attend_back(qkv, live, grad):
    rows, wide = qkv.shape
    images = live.shape[0]
    near = rows // images
    width = wide // 3
    return pl.pallas_call(
        attend_back_kernel,
        out_shape=jax.ShapeDtypeStruct((rows, wide), bf16),
        grid=(images,),
        in_specs=[
            pl.BlockSpec((near, wide), lambda i: (i, 0)),
            pl.BlockSpec((1, 1, near), lambda i: (i, 0, 0)),
            pl.BlockSpec((near, width), lambda i: (i, 0)),
        ],
        out_specs=pl.BlockSpec((near, wide), lambda i: (i, 0)),
        scratch_shapes=[pltpu.VMEM((near, wide), f32)],
        cost_estimate=pl.CostEstimate(flops=1, bytes_accessed=1, transcendentals=0),
        compiler_params=pltpu.CompilerParams(vmem_limit_bytes=12 * 2**20),
        name="attend_back",
    )(qkv, live, grad)


def join_kernel(lines, mine_ref, got_ref, out_ref):
    rest = mine_ref.shape[0] - lines
    out_ref[:lines] = mine_ref[:lines] + got_ref[:lines]
    out_ref[lines : lines + rest] = mine_ref[lines:]
    out_ref[lines + rest :] = got_ref[lines:]


def join(mine, got, lines):
    rows, lanes = mine.shape
    return pl.pallas_call(
        functools.partial(join_kernel, lines),
        out_shape=jax.ShapeDtypeStruct((2 * rows - lines, lanes), f32),
        cost_estimate=pl.CostEstimate(flops=1, bytes_accessed=1, transcendentals=0),
        compiler_params=pltpu.CompilerParams(vmem_limit_bytes=8 * 2**20),
        name="join",
    )(mine, got)


class Halving:
    def __init__(self, orders, count):
        self.orders = orders
        self.count = count
        self.stages = len(orders[0])
        self.message = None
        self.keeps = None
        self.received = []

    def lined(self, blocks):
        return blocks.reshape(-1, blocks.shape[1] * blocks.shape[2], 128)

    def sends(self, blocks):
        self.message = self.lined(blocks)
        return blocks

    def holds(self, blocks):
        self.keeps = [self.lined(item) for item in blocks]
        return blocks[-1]

    def step(self, token):
        stage = len(self.received)
        if stage:
            self.received[-1] = after(self.received[-1], token)
        if stage == self.stages:
            message = self.keeps[0][0]
            for piece in self.received:
                message = message + piece[0]
            self.message = message
            return message
        if stage:
            low = 1 << (self.stages - 1 - stage)
            message = self.keeps[self.stages - stage]
            for piece in self.received:
                message = message + piece[low : 2 * low]
        else:
            message = after(self.message, token)
        self.received.append(flip_stage(message, stage, self.orders, self.count))
        return message

    def result(self, rows):
        return self.message.reshape(-1, rows, 128)


def body(
    patches,
    bucket,
    keep_order,
    timesteps,
    labels,
    patch_weight,
    patch_bias,
    class_table,
    ada_weight,
    ada_bias,
    qkv_weight,
    query_bias,
    value_bias,
    proj_weight,
    proj_bias,
    up_weight,
    up_bias,
    down_weight,
    down_bias,
    final_weight,
    final_bias,
    out_grad,
):
    images, tile_slots, patch_width = patches.shape
    slot_total = keep_order.shape[1]
    width = patch_weight.shape[1]
    hidden = up_weight.shape[1]
    class_count = class_table.shape[0]
    count = lax.axis_size("dp")
    bits = count.bit_length() - 1
    tile = lax.axis_index("tile")
    own = images // 2
    half_slots = slot_total // 2
    first = tile * own

    def mine(value):
        return lax.dynamic_slice_in_dim(value, first, own, 0)

    def others(value):
        return lax.dynamic_slice_in_dim(value, own - first, own, 0)

    unit = (bucket[0] >= 0).astype(f32)

    pair = jnp.concatenate([patches, out_grad], axis=2).astype(f32)
    slots_data = jnp.concatenate([mine(pair), swap_tiles(others(pair)) * unit], axis=1).astype(bf16)
    near = jnp.arange(slot_total, dtype=jnp.int32)
    slot_ids = (near + tile * tile_slots) % slot_total

    condition = time_embed(timesteps, width) + jnp.take(class_table, labels, axis=0).astype(f32)
    cond_act = jax.nn.silu(condition).astype(bf16)
    mod_half = mm("id,de->ie", cond_act, ada_weight) + ada_bias.astype(f32)
    mod_mine, mod_recv = mine(mod_half), swap_tiles(others(mod_half))
    modulation = jnp.where(
        tile == 0,
        jnp.concatenate([mod_mine, mod_recv], axis=1),
        jnp.concatenate([mod_recv, mod_mine], axis=1),
    )
    shift_a, scale_a, gate_a, shift_m, scale_m, gate_m = [
        portion[:, None, :] for portion in jnp.split(modulation, 6, axis=1)
    ]

    my_bucket, my_order = mine(bucket), mine(keep_order)
    half_rows = jnp.where(my_bucket == 0, 8, jnp.where(my_bucket == 1, 6, 10))[:, None]
    columns = jnp.where(my_bucket == 0, 16, jnp.where(my_bucket == 1, 20, 12))[:, None]
    area = half_rows * columns
    order_valid = (my_order % tile_slots) < area
    upper = (near[:, None] < near[None, :]).astype(bf16)
    rank = mm("ij,jk->ik", order_valid.astype(bf16), upper).astype(jnp.int32)
    limit = area
    place = jnp.where(rank < limit, rank, rank - limit + half_slots)
    hit = (place[:, None, :] == near[None, :, None]) & order_valid[:, None, :]
    row_slot = jnp.sum(jnp.where(hit, my_order[:, None, :] + 1, 0), axis=2) - 1
    live = row_slot >= 0
    select = (row_slot[:, :, None] == slot_ids[None, None, :]).astype(bf16)
    row_data = mm("irs,isc->irc", select, slots_data).astype(bf16)
    row_patches, row_grads = row_data[:, :, :patch_width], row_data[:, :, patch_width:]
    local = row_slot % tile_slots
    grid_row = (row_slot // tile_slots) * half_rows + local // columns
    grid_col = local % columns
    marks = jnp.arange(GRID_MAX, dtype=jnp.int32)
    mark_row = (grid_row[:, :, None] == marks).astype(bf16)
    mark_col = (grid_col[:, :, None] == marks).astype(bf16)
    table = three_way(axis_table(width // 2))
    blank = jnp.zeros((GRID_MAX, width // 2), bf16)
    wide = jnp.concatenate(
        [patch_weight]
        + [jnp.concatenate([piece, blank], axis=1) for piece in table]
        + [jnp.concatenate([blank, piece], axis=1) for piece in table],
        axis=0,
    )
    features = jnp.concatenate([row_patches] + [mark_row] * 3 + [mark_col] * 3, axis=2)
    embedded = mm("irk,kd->ird", features, wide) + patch_bias.astype(f32)
    key_live = live[:, :half_slots]

    fast = count == 16 and (width // count) % 8 == 0 and images * slot_total == 1024
    index = lax.axis_index("dp")

    def unit_ids(orders):
        masks = [jnp.array(relative_masks(order), jnp.int32) for order in orders]
        return jnp.where(tile == 0, masks[0], masks[1]) ^ index

    def left_blocks(left):
        rows, size = left.shape[0] * left.shape[1], left.shape[2]
        flat = left.reshape(rows, size)
        blocks = turn(flat) if fast else flat.astype(f32).T
        blocks = blocks.reshape(count, size // count, rows)
        return blocks, swap_tiles(blocks)

    def right_half(*rights):
        if fast:
            keep, give = halves(tile, *[right.reshape(-1, right.shape[2]) for right in rights])
            return keep, swap_tiles(give), give
        keep, give = [], []
        for right in rights:
            size = right.shape[2] // 2
            flat = right.reshape(-1, 2 * size)
            low, high = flat[:, :size], flat[:, size:]
            keep.append(jnp.where(tile == 0, low, high))
            give.append(jnp.where(tile == 0, high, low).astype(f32))
        keep, give = jnp.concatenate(keep, axis=1), jnp.concatenate(give, axis=1)
        return keep, swap_tiles(give), give

    def plain(left, right):
        (near_left, far_left), (near_right, far_right) = left, right
        near_left = near_left.astype(bf16)
        far_left, far_right = (far_left * unit).astype(bf16), (far_right * unit).astype(bf16)
        grad = mm("brk,kc->brc", near_left, near_right) + mm("brk,kc->brc", far_left, far_right)
        grad = grad.reshape(-1, grad.shape[2])
        return lax.psum_scatter(grad, "dp", scatter_dimension=0, tiled=True)

    chains, tables = {}, {}
    for name, plan in PLAN.items():
        if fast:
            orders = unit_orders(plan)
            chains[name] = Halving(orders, count)
            if plan not in tables:
                tables[plan] = unit_ids(orders)
    todo = ORDER.split()
    token = [keep_order]
    small = []

    def gate(value):
        return after(value, token[0]) if fast else value

    def passed(value):
        token[0] = value
        return value

    def small_step():
        orders = list(range(2, bits))[::-1]
        orders = (orders + [0, 1], orders + [1, 0])
        stage, message = small[0], small[1]
        if stage:
            got = gate(small[2])
            lines = small[3]
            if fast:
                message = join(message, got, lines)
            else:
                message = jnp.concatenate(
                    [message[:lines] + got[:lines], message[lines:], got[lines:]], axis=0
                )
        else:
            message = gate(message)
        small[0], small[1] = stage + 1, message
        if stage < bits:
            small[2] = flip_stage(message, stage, orders, count)
        passed(message)

    def reach(block):
        while todo[0] != block:
            event = todo.pop(0)
            if event == "s":
                small_step()
            elif event[0] == "k":
                part = int(event[1])
                passed(chains["d%d" % part].holds(down_unit(part, KEEPS)))
            else:
                passed(chains[event].step(token[0]))
        todo.pop(0)

    def table(name):
        return gate(tables[PLAN[name]])

    def down_unit(part, ranges):
        return row_unit(table("d%d" % part), *down_left, down_right, part, ranges)

    def whole_unit(name, lefts, right, part, border):
        send, *keeps = column_unit(table(name), lefts, *right, part, border, SENDS + KEEPS)
        chains[name].holds(keeps)
        return passed(chains[name].sends(send))

    kept_x = embedded[:, :half_slots]
    normed_a, rstd_a = norm_stats(kept_x)
    attn_in = (normed_a * (1.0 + scale_a) + shift_a).astype(bf16)
    qkv_bias = jnp.concatenate([query_bias, jnp.zeros_like(query_bias), value_bias]).astype(f32)
    qkv = (mm("isd,de->ise", attn_in, qkv_weight) + qkv_bias).astype(bf16)
    qkv = qkv.reshape(own * half_slots, -1)
    live_row = key_live.astype(f32)[:, None, :]
    mixed = attend(qkv, live_row).reshape(own, half_slots, width)
    attn_out = mm("iqd,de->iqe", mixed, proj_weight) + proj_bias.astype(f32)
    middle = kept_x + gate_a * attn_out
    normed_m, rstd_m = norm_stats(middle)
    mlp_in = (normed_m * (1.0 + scale_m) + shift_m).astype(bf16)
    rows = own * half_slots
    activated, act_slope, blocks = feed_up(mlp_in.reshape(rows, width), up_weight, up_bias)
    blocks = blocks.reshape(count, hidden // count, rows)
    down_left = (blocks, swap_tiles(blocks))
    activated = activated.reshape(own, half_slots, hidden)
    mlp_out = mm("iqf,fd->iqd", activated, down_weight) + down_bias.astype(f32)
    block_out = middle + gate_m * mlp_out
    merged = jnp.concatenate([block_out, embedded[:, half_slots:]], axis=1)
    normed_f, rstd_f = norm_stats(merged)
    final_in = normed_f.astype(bf16)

    d_final = mm("isp,dp->isd", row_grads, final_weight)
    d_merged = norm_back(normed_f, rstd_f, d_final)
    d_block = d_merged[:, :half_slots]
    d_mlp = (gate_m * d_block).astype(bf16)
    d_gate_m = jnp.sum(d_block * mlp_out, axis=1)

    *down_right, give = right_half(d_mlp)
    d_mlp = after(d_mlp, give)
    if fast:
        passed(give)
        up_left = left_blocks(gate(mlp_in))
        passed(up_left[0])
        reach("Kd0")
        passed(chains["d0"].sends(down_unit(0, SENDS)[0]))
        reach("Kd1")
        passed(chains["d1"].sends(down_unit(1, SENDS)[0]))
        reach("Cp")
    d_pre = feed_back(gate(d_mlp).reshape(rows, width), down_weight, act_slope)
    d_pre = passed(d_pre.reshape(own, half_slots, hidden))
    if fast:
        *up_right, give = right_half(d_pre)
        passed(give)
        reach("Ct")
        proj_left, qkv_left = left_blocks(gate(mixed)), left_blocks(gate(attn_in))
        passed(qkv_left[0])
        reach("Ku0")
        whole_unit("u0", up_left, up_right, 0, None)
        reach("Ku1")
        whole_unit("u1", up_left, up_right, 1, None)
        reach("C1")
    else:
        down_final = plain(down_left, down_right)
        up_final = plain(left_blocks(mlp_in), right_half(d_pre)[:2])
    d_mlp_in = mm("iqf,df->iqd", gate(d_pre), up_weight)
    d_shift_m = jnp.sum(d_mlp_in, axis=1)
    d_scale_m = jnp.sum(d_mlp_in * normed_m, axis=1)
    d_middle = d_block + norm_back(normed_m, rstd_m, d_mlp_in * (1.0 + scale_m))
    d_attn = passed((gate_a * d_middle).astype(bf16))
    d_gate_a = jnp.sum(d_middle * attn_out, axis=1)
    if fast:
        reach("C2")
    else:
        proj_left, qkv_left = left_blocks(mixed), left_blocks(attn_in)
    d_mixed = mm("iqe,de->iqd", gate(d_attn), proj_weight).astype(bf16)
    d_qkv = attend_back(qkv, live_row, d_mixed.reshape(own * half_slots, width))
    d_qkv = passed(d_qkv.reshape(own, half_slots, 3 * width))
    border = d_qkv.shape[2] // 2
    if fast:
        reach("Cq")
        *both_right, give = right_half(gate(d_qkv), d_attn)
        passed(give)
        reach("Kq0")
        whole_unit("q0", qkv_left, both_right, 0, border)
        reach("Kq1")
        whole_unit("q1", qkv_left + proj_left, both_right, 1, border)
        reach("C3")
    else:
        proj_final = plain(proj_left, right_half(d_attn)[:2])
        qkv_final = plain(qkv_left, right_half(d_qkv)[:2])
    d_qkv = gate(d_qkv)
    qkv_bias_sums = jnp.sum(d_qkv.astype(f32), axis=(0, 1))
    d_attn_in = mm("ice,de->icd", d_qkv, qkv_weight)
    d_shift_a = jnp.sum(d_attn_in, axis=1)
    d_scale_a = jnp.sum(d_attn_in * normed_a, axis=1)
    d_kept = passed(d_middle + norm_back(normed_a, rstd_a, d_attn_in * (1.0 + scale_a)))
    if fast:
        reach("C4")
    d_kept, d_merged, final_in = gate(d_kept), gate(d_merged), gate(final_in)
    proj_bias_grad = jnp.sum(gate(d_attn).astype(f32), axis=(0, 1))
    up_bias_grad = jnp.sum(gate(d_pre).astype(f32), axis=(0, 1))
    down_bias_grad = jnp.sum(gate(d_mlp).astype(f32), axis=(0, 1))
    row_denoised = mm("isd,dp->isp", final_in, final_weight) + final_bias.astype(f32)
    final_weight_grad = mm("isd,isp->dp", final_in, row_grads)
    final_bias_grad = jnp.sum(row_grads.astype(f32), axis=(0, 1))
    d_low = jnp.concatenate([d_kept, d_merged[:, half_slots:]], axis=1).astype(bf16)
    row_patch_grad = mm("isd,pd->isp", d_low, patch_weight)
    patch_weight_grad = mm("isp,isd->pd", row_patches, d_low)
    patch_bias_grad = jnp.sum(d_low.astype(f32), axis=(0, 1))

    back = jnp.concatenate([row_denoised, row_patch_grad], axis=2)
    slot_out = jnp.einsum("irs,irc->isc", select.astype(f32), back, precision=highest)
    near_part, far_part = slot_out[:, :tile_slots], swap_tiles(slot_out[:, tile_slots:])
    slot_mine = jnp.where(
        tile == 0,
        jnp.concatenate([near_part, far_part], axis=0),
        jnp.concatenate([far_part, near_part], axis=0),
    )
    denoised, patch_grad = slot_mine[:, :, :patch_width], slot_mine[:, :, patch_width:]

    d_mod = jnp.concatenate(
        [d_shift_a, d_scale_a, d_gate_a, d_shift_m, d_scale_m, d_gate_m], axis=1
    )
    mod_width = d_mod.shape[1] // 2
    keep = lax.dynamic_slice_in_dim(d_mod, tile * mod_width, mod_width, 1)
    give = lax.dynamic_slice_in_dim(d_mod, (1 - tile) * mod_width, mod_width, 1)
    got = swap_tiles(give) * unit
    d_mod_half = jnp.where(
        tile == 0, jnp.concatenate([keep, got], axis=0), jnp.concatenate([got, keep], axis=0)
    ).astype(bf16)
    d_cond_act = mm("ie,de->id", d_mod_half, ada_weight)
    gated = jax.nn.sigmoid(condition)
    d_cond_part = d_cond_act * (gated * (1.0 + condition * (1.0 - gated)))
    d_condition = d_cond_part + swap_tiles(d_cond_part)

    sums_of = [
        patch_weight_grad,
        patch_bias_grad,
        qkv_bias_sums[:width],
        qkv_bias_sums[2 * width :],
        proj_bias_grad,
        up_bias_grad,
        down_bias_grad,
        final_weight_grad,
        final_bias_grad,
    ]
    area_all = jnp.where(bucket == 0, 128, 120)
    counts_local = jnp.stack([jnp.sum(area_all), jnp.sum(2 * area_all)]).astype(f32) * 0.5
    sums_of.append(counts_local)
    flat = jnp.concatenate([leaf.reshape(-1) for leaf in sums_of])
    flat = jnp.pad(flat, (0, (-flat.shape[0]) % 2048)).reshape(2, -1, 128)
    flat_half = lax.dynamic_index_in_dim(flat, tile, 0, keepdims=False) + swap_tiles(
        lax.dynamic_index_in_dim(flat, 1 - tile, 0, keepdims=False)
    )
    lines = flat_half.shape[0]
    marks = jnp.stack([labels, timesteps], axis=1).astype(f32)
    packed = jnp.concatenate(
        [d_mod_half.astype(f32), d_condition, jnp.pad(marks, ((0, 0), (0, 126)))], axis=1
    )
    message = passed(jnp.concatenate([flat_half, packed.reshape(-1, 128)], axis=0))
    small.extend([0, message, None, lines])
    if fast:
        reach("C5")
    else:
        for _ in range(bits + 1):
            small_step()
    message = small[1]

    every = (message[lines:] * unit).reshape(count * images, -1)
    all_mod = every[:, :mod_width].astype(bf16)
    all_cond = every[:, mod_width : mod_width + width]
    all_label = every[:, mod_width + width].astype(jnp.int32)
    all_time = every[:, mod_width + width + 1]
    one_hot = (all_label[:, None] == jnp.arange(class_count, dtype=jnp.int32)[None, :])
    block = width // count
    table_rows = lax.dynamic_slice_in_dim(class_table, index * block, block, 1)
    picked = mm("nc,cd->nd", one_hot.astype(bf16), table_rows)
    act_rows = time_columns(all_time, index * block, block, width) + picked
    act_rows = jax.nn.silu(act_rows).astype(bf16)
    ada_final = mm("nd,ne->de", act_rows, all_mod)
    ada_half = jnp.sum(all_mod.astype(f32), axis=0)
    ending = jnp.concatenate([message[:lines], ada_half.reshape(-1, 128)], axis=0)
    other = swap_tiles(ending)
    first_end = jnp.where(tile == 0, ending, other)
    second_end = jnp.where(tile == 0, other, ending)
    ada_bias_sum = jnp.concatenate(
        [first_end[lines:].reshape(-1), second_end[lines:].reshape(-1)]
    )
    summed = jnp.concatenate([first_end[:lines].reshape(-1), second_end[:lines].reshape(-1)])
    sums = []
    offset = 0
    for leaf in sums_of:
        sums.append(summed[offset : offset + leaf.size].reshape(leaf.shape))
        offset += leaf.size
    class_table_sum = jnp.einsum("nc,nd->cd", one_hot.astype(f32), all_cond, precision=highest)

    if fast:
        todo.append("end")
        reach("end")
        part_rows = width // count
        first_part, second_part = [chains[name].result(part_rows) for name in ("d0", "d1")]
        wide = [
            item[:8].reshape(2, 4, part_rows, 128).transpose(1, 2, 0, 3).reshape(-1, 256)
            for item in (first_part, second_part)
        ]
        rest = second_part[8:]
        rest = jnp.concatenate(
            [rest[0, :, :64], rest[1, :, :64], rest[0, :, 64:], rest[1, :, 64:]], axis=0
        )
        down_final = jnp.concatenate(wide + [rest], axis=1)

        def columns_of(name):
            tiles = [chains[name + part].result(part_rows) for part in "01"]
            tiles = jnp.concatenate(tiles)
            return tiles.transpose(1, 0, 2).reshape(tiles.shape[1], -1)

        up_final = columns_of("u")
        joint = columns_of("q")
        qkv_final, proj_final = joint[:, :border], joint[:, border:]
    (
        patch_weight_sum,
        patch_bias_sum,
        query_bias_sum,
        value_bias_sum,
        proj_bias_sum,
        up_bias_sum,
        down_bias_sum,
        final_weight_sum,
        final_bias_sum,
        token_counts,
    ) = sums
    return (
        denoised,
        patch_grad,
        patch_weight_sum,
        patch_bias_sum,
        class_table_sum,
        ada_final,
        ada_bias_sum,
        qkv_final,
        query_bias_sum,
        value_bias_sum,
        proj_final,
        proj_bias_sum,
        up_final,
        up_bias_sum,
        down_final,
        down_bias_sum,
        final_weight_sum,
        final_bias_sum,
        token_counts,
    )


def solution(mesh):
    in_specs = (
        P("dp", "tile", None),
        P("dp"),
        P("dp", None),
        P("dp"),
        P("dp"),
        P(),
        P(),
        P(),
        P(None, "tile"),
        P("tile"),
        P(),
        P(),
        P(),
        P(),
        P(),
        P(),
        P(),
        P(),
        P(),
        P(),
        P(),
        P("dp", "tile", None),
    )
    out_specs = (
        P("dp", "tile", None),
        P("dp", "tile", None),
        P(),
        P(),
        P(),
        P("dp", "tile"),
        P(),
        P("dp", "tile"),
        P(),
        P(),
        P("dp", "tile"),
        P(),
        P("dp", "tile"),
        P(),
        P("dp", "tile"),
        P(),
        P(),
        P(),
        P(),
    )
    return jax.shard_map(body, mesh=mesh, in_specs=in_specs, out_specs=out_specs, check_vma=False)
```

```python
import functools
import math

import jax
import jax.numpy as jnp
from jax import lax
from jax.experimental import pallas as pl
from jax.experimental.pallas import tpu as pltpu
from jax.sharding import PartitionSpec as P

HEADS = 16
GRID_MAX = 32
epsilon = 1e-06
f32 = jnp.float32
bf16 = jnp.bfloat16


def mm(spec, left, right):
    return jnp.einsum(spec, left, right, preferred_element_type=f32)


def norm_stats(values):
    center = values - jnp.mean(values, axis=-1, keepdims=True)
    rstd = lax.rsqrt(jnp.mean(center * center, axis=-1, keepdims=True) + epsilon)
    return center * rstd, rstd


def norm_back(normed, rstd, grad):
    return rstd * (
        grad
        - jnp.mean(grad, axis=-1, keepdims=True)
        - normed * jnp.mean(grad * normed, axis=-1, keepdims=True)
    )


def gelu_parts(u):
    inner = 0.7978845608028654 * (u + 0.044715 * u * u * u)
    th = jnp.tanh(inner)
    value = 0.5 * u * (1.0 + th)
    slope = 0.5 * (1.0 + th) + 0.5 * u * (1.0 - th * th) * 0.7978845608028654 * (
        1.0 + 3.0 * 0.044715 * u * u
    )
    return value, slope


def three_way(table):
    parts = []
    rest = table
    for _ in range(3):
        piece = lax.reduce_precision(rest, exponent_bits=8, mantissa_bits=7)
        parts.append(piece.astype(bf16))
        rest = rest - piece
    return parts


def axis_table(width):
    quarter = width // 2
    omega = jnp.exp(-math.log(10000.0) * jnp.arange(quarter, dtype=f32) / quarter)
    angles = jnp.arange(GRID_MAX, dtype=f32)[:, None] * omega[None, :]
    return jnp.concatenate([jnp.sin(angles), jnp.cos(angles)], axis=-1)


def time_embed(timesteps, model_width):
    half = model_width // 2
    freqs = jnp.exp(-math.log(10000.0) * jnp.arange(half, dtype=f32) / half)
    angles = timesteps.astype(f32)[:, None] * freqs
    return jnp.concatenate([jnp.cos(angles), jnp.sin(angles)], axis=-1)


def time_columns(timesteps, first, number, model_width):
    half = model_width // 2
    column = first + jnp.arange(number, dtype=jnp.int32)
    freqs = jnp.exp(-math.log(10000.0) * (column % half).astype(f32) / half)
    angles = timesteps[:, None] * freqs
    return jnp.where(column < half, jnp.cos(angles), jnp.sin(angles))


def swap_tiles(value):
    return lax.ppermute(value, "tile", [(0, 1), (1, 0)])


def flip_stage(value, stage, orders, count):
    pairs = []
    for d in range(count):
        for t, order in enumerate(orders):
            pairs.append((2 * d + t, 2 * (d ^ (1 << order[stage])) + t))
    return lax.ppermute(value, ("dp", "tile"), pairs)


def relative_masks(order):
    bits = len(order)
    masks = []
    for rel in range(1 << bits):
        mask = 0
        for stage in range(bits):
            if (rel >> (bits - 1 - stage)) & 1:
                mask |= 1 << order[stage]
        masks.append(mask)
    return masks


def after(value, *others):
    return lax.optimization_barrier((value,) + others)[0]


CHUNK = 3
UNIT = 9
BOTH = {
    "x": (0, 1),
    "y": (1, 0),
    "1": (2, 2),
    "2": (3, 3),
}
PLAN = {
    "d0": "x1y2",
    "d1": "1x2y",
    "u0": "xy12",
    "u1": "xy12",
    "q0": "xy12",
    "q1": "xy12",
}
ORDER = """
Kd0 d0 Kd1 d1 Cp Ct k0 d0 Ku0 u0 Ku1 u1 C1 C2 Cq k1 d1 u0 u1 Kq0 Kq1 u0 q1 C3 d0 d1 u0 q0 u1 C4
q1 s d1 u1 s u0 s q1 q0 u1 d0 d1 s q1 q0 q1 s C5 q0 d0 q0
"""


def unit_orders(plan):
    return tuple([BOTH[c][t] for c in plan] for t in (0, 1))


def dot_rows(left, right):
    return lax.dot_general(left, right, (((1,), (0,)), ((), ())), preferred_element_type=f32)


def halves_kernel(tile_ref, *refs):
    number = len(refs) - 2
    keep_ref, give_ref = refs[-2:]

    def write(own):
        start = 0
        for ref in refs[:number]:
            size = ref.shape[1] // 2
            place = slice(start, start + size)
            keep_ref[:, place] = ref[:, own * size : (own + 1) * size]
            give_ref[:, place] = ref[:, (1 - own) * size : (2 - own) * size].astype(f32)
            start += size
        if start < give_ref.shape[1]:
            rest = give_ref.shape[1] - start
            give_ref[:, start:] = jnp.zeros((give_ref.shape[0], rest), f32)

    for own in (0, 1):
        pl.when(tile_ref[0] == own)(functools.partial(write, own))


def halves(tile, *values):
    rows = values[0].shape[0]
    size = sum(value.shape[1] for value in values) // 2
    padded = -(-size // 128) * 128
    return pl.pallas_call(
        halves_kernel,
        out_shape=(
            jax.ShapeDtypeStruct((rows, size), bf16),
            jax.ShapeDtypeStruct((rows, padded), f32),
        ),
        grid_spec=pltpu.PrefetchScalarGridSpec(
            num_scalar_prefetch=1,
            grid=(1,),
            in_specs=[pl.BlockSpec(value.shape, lambda i, tile: (0, 0)) for value in values],
            out_specs=(
                pl.BlockSpec((rows, size), lambda i, tile: (0, 0)),
                pl.BlockSpec((rows, padded), lambda i, tile: (0, 0)),
            ),
        ),
        cost_estimate=pl.CostEstimate(flops=1, bytes_accessed=1, transcendentals=0),
        compiler_params=pltpu.CompilerParams(vmem_limit_bytes=12 * 2**20),
        name="halves",
    )(tile[None], *values)


def turned(value):
    size = value.shape[1]
    row = lax.broadcasted_iota(jnp.int32, (size, size), 0)
    column = lax.broadcasted_iota(jnp.int32, (size, size), 1)
    identity = jnp.where(row == column, 1.0, 0.0).astype(bf16)
    return dot_columns(identity, value)


def turn_kernel(in_ref, out_ref):
    out_ref[...] = turned(in_ref[...])


def turn(value):
    rows, size = value.shape
    chunk = 384
    return pl.pallas_call(
        turn_kernel,
        out_shape=jax.ShapeDtypeStruct((size, rows), f32),
        grid=(size // chunk,),
        in_specs=[pl.BlockSpec((rows, chunk), lambda j: (0, j))],
        out_specs=pl.BlockSpec((chunk, rows), lambda j: (j, 0)),
        cost_estimate=pl.CostEstimate(flops=1, bytes_accessed=1, transcendentals=0),
        compiler_params=pltpu.CompilerParams(vmem_limit_bytes=5 * 2**20),
        name="turn",
    )(value)


def row_kernel(part, ranges, pair, ids_ref, *refs):
    near = [refs[i][0].astype(bf16) for i in range(pair)]
    far = [refs[pair + i][0].astype(bf16) for i in range(pair)]
    right_ref, right_far_ref = refs[2 * pair : 2 * pair + 2]
    out_refs = refs[2 * pair + 2 :]
    size = near[0].shape[0]
    cut = slice(256, right_ref.shape[1]) if part else slice(0, 256)
    res = dot_rows(jnp.concatenate(near, axis=0), right_ref[:, cut])
    res = res + dot_rows(jnp.concatenate(far, axis=0), right_far_ref[:, cut].astype(bf16))
    rows = size // 4
    step = pl.program_id(0) * pair + ranges[0][0]

    def write(ref, place, base):
        for c in range(2):
            for h in range(4):
                top = base + h * rows
                ref[place, 4 * c + h] = res[top : top + rows, c * 128 : (c + 1) * 128]
        if part:
            for h in range(2):
                top = base + h * rows
                ref[place, 8 + h, :, :64] = res[top : top + rows, 256:]
                top = base + (h + 2) * rows
                ref[place, 8 + h, :, 64:] = res[top : top + rows, 256:]

    for ref, (low, high) in zip(out_refs, ranges):
        block = min(high - low, pair)

        def body(ref=ref, low=low, block=block):
            for i in range(block):
                write(ref, i, (i + (low % pair)) * size)

        pl.when((step + pair > low) & (step < high))(body)


def row_unit(ids, left, left_far, rights, part, ranges):
    _, rows, near = left.shape
    pieces = 8 + 2 * part
    pair = 2
    first, number = ranges[0][0], ranges[-1][1] - ranges[0][0]

    def place(low, high):
        block = min(high - low, pair)
        last = (high - low) // block - 1
        return lambda k, ids: (jnp.clip((k * pair + first - low) // block, 0, last), 0, 0, 0)

    def source(i):
        return pl.BlockSpec((1, rows, near), lambda k, ids: (ids[first + k * pair + i], 0, 0))

    return pl.pallas_call(
        functools.partial(row_kernel, part, ranges, pair),
        out_shape=tuple(
            jax.ShapeDtypeStruct((high - low, pieces, rows // 4, 128), f32) for low, high in ranges
        ),
        grid_spec=pltpu.PrefetchScalarGridSpec(
            num_scalar_prefetch=1,
            grid=(number // pair,),
            in_specs=[source(i % pair) for i in range(2 * pair)]
            + [
                pl.BlockSpec((near, item.shape[1]), lambda k, ids: (0, 0)) for item in rights
            ],
            out_specs=tuple(
                pl.BlockSpec((min(high - low, pair), pieces, rows // 4, 128), place(low, high))
                for low, high in ranges
            ),
        ),
        cost_estimate=pl.CostEstimate(flops=1, bytes_accessed=1, transcendentals=0),
        compiler_params=pltpu.CompilerParams(vmem_limit_bytes=14 * 2**20),
        name="row_unit",
    )(ids, *[left] * pair, *[left_far] * pair, *rights)


def column_kernel(border, first_tile, ranges, number, ids_ref, *refs):
    lefts, (right_ref, right_far_ref) = refs[: 2 * number], refs[2 * number : 2 * number + 2]
    out_refs, stack_ref = refs[2 * number + 2 : -1], refs[-1]
    count, rows, near = lefts[0].shape
    half = count // 2 * rows
    step = pl.program_id(0)

    @pl.when(step == 0)
    def _():
        for i in range(number):
            for r in range(count):
                place = pl.ds(r * rows, rows)
                stack_ref[i, place, :near] = lefts[2 * i][ids_ref[r]].astype(bf16)
                stack_ref[i, place, near:] = lefts[2 * i + 1][ids_ref[r]].astype(bf16)

    right = jnp.concatenate([right_ref[...], right_far_ref[...].astype(bf16)], axis=0)

    def write(kind):
        for base in (half, 0):
            stack = [stack_ref[i, base : base + half] for i in range(number)]
            if kind == "first":
                res = dot_rows(stack[0], right)
            elif kind == "last":
                res = dot_rows(stack[1], right)
            else:
                start = (step * CHUNK + first_tile) * 128
                column = lax.broadcasted_iota(jnp.int32, (half, CHUNK * 128), 1) + start
                res = jnp.where(
                    column < border, dot_rows(stack[0], right), dot_rows(stack[1], right)
                )
            for ref, (low, high) in zip(out_refs, ranges):
                if base <= low * rows < base + half:
                    for r in range(low, high):
                        top = r * rows - base
                        for c in range(CHUNK):
                            ref[r - low, c] = res[top : top + rows, c * 128 : (c + 1) * 128]

    if number == 1:
        write("first")
    else:
        begin = (step * CHUNK + first_tile) * 128
        end = begin + CHUNK * 128

        @pl.when(end <= border)
        def _():
            write("first")

        @pl.when(begin >= border)
        def _():
            write("last")

        @pl.when((end > border) & (begin < border))
        def _():
            write("mixed")


def column_unit(ids, lefts, right, right_far, part, border, ranges):
    count, rows, near = lefts[0].shape
    first_tile = part * UNIT
    first_chunk = first_tile // CHUNK
    whole = pl.BlockSpec((count, rows, near), lambda j, ids: (0, 0, 0))
    chunk = pl.BlockSpec((near, CHUNK * 128), lambda j, ids: (0, first_chunk + j))
    number = len(lefts) // 2
    return pl.pallas_call(
        functools.partial(column_kernel, border, first_tile, ranges, number),
        out_shape=tuple(
            jax.ShapeDtypeStruct((high - low, UNIT, rows, 128), f32) for low, high in ranges
        ),
        grid_spec=pltpu.PrefetchScalarGridSpec(
            num_scalar_prefetch=1,
            grid=(UNIT // CHUNK,),
            in_specs=[whole] * len(lefts) + [chunk, chunk],
            out_specs=tuple(
                pl.BlockSpec((high - low, CHUNK, rows, 128), lambda j, ids: (0, j, 0, 0))
                for low, high in ranges
            ),
            scratch_shapes=[pltpu.VMEM((number, count * rows, 2 * near), bf16)],
        ),
        cost_estimate=pl.CostEstimate(flops=1, bytes_accessed=1, transcendentals=0),
        compiler_params=pltpu.CompilerParams(vmem_limit_bytes=(10 + 8 * number) * 2**20),
        name="column_unit",
    )(ids, *lefts, right, right_far)


SENDS = ((8, 16),)
KEEPS = ((0, 1), (1, 2), (2, 4), (4, 8))


PIECE = 512


def in_hbm(value):
    return pltpu.with_memory_space_constraint(value, pltpu.HBM)


def up_kernel(in_ref, weight_ref, bias_ref, act_ref, slope_ref, turned_ref):
    for low in range(0, PIECE, 256):
        place = slice(low, low + 256)
        pre = dot_rows(in_ref[...], weight_ref[:, place]) + bias_ref[:, place]
        value, slope = gelu_parts(pre)
        value = value.astype(bf16)
        act_ref[:, place] = value
        slope_ref[:, place] = slope
        turned_ref[place, :] = value.T.astype(f32)


def feed_up(value, weight, bias):
    rows, width = value.shape
    hidden = weight.shape[1]
    return pl.pallas_call(
        up_kernel,
        out_shape=(
            jax.ShapeDtypeStruct((rows, hidden), bf16),
            jax.ShapeDtypeStruct((rows, hidden), f32),
            jax.ShapeDtypeStruct((hidden, rows), f32),
        ),
        grid=(hidden // PIECE,),
        in_specs=[
            pl.BlockSpec((rows, width), lambda j: (0, 0)),
            pl.BlockSpec((width, PIECE), lambda j: (0, j)),
            pl.BlockSpec((1, PIECE), lambda j: (0, j)),
        ],
        out_specs=(
            pl.BlockSpec((rows, PIECE), lambda j: (0, j)),
            pl.BlockSpec((rows, PIECE), lambda j: (0, j)),
            pl.BlockSpec((PIECE, rows), lambda j: (j, 0)),
        ),
        cost_estimate=pl.CostEstimate(flops=1, bytes_accessed=1, transcendentals=0),
        compiler_params=pltpu.CompilerParams(vmem_limit_bytes=11 * 2**20),
        name="feed_up",
    )(value, weight, bias[None].astype(f32))


def down_back_kernel(grad_ref, weight_ref, slope_ref, out_ref):
    out_ref[...] = (dot_columns(grad_ref[...], weight_ref[...]) * slope_ref[...]).astype(bf16)


def feed_back(grad, weight, slope):
    rows, width = grad.shape
    hidden = weight.shape[0]
    return pl.pallas_call(
        down_back_kernel,
        out_shape=jax.ShapeDtypeStruct((rows, hidden), bf16),
        grid=(hidden // PIECE,),
        in_specs=[
            pl.BlockSpec((rows, width), lambda j: (0, 0)),
            pl.BlockSpec((PIECE, width), lambda j: (j, 0)),
            pl.BlockSpec((rows, PIECE), lambda j: (0, j)),
        ],
        out_specs=pl.BlockSpec((rows, PIECE), lambda j: (0, j)),
        cost_estimate=pl.CostEstimate(flops=1, bytes_accessed=1, transcendentals=0),
        compiler_params=pltpu.CompilerParams(vmem_limit_bytes=8 * 2**20),
        name="feed_back",
    )(grad, in_hbm(weight), slope)


def head_window(head, size, width):
    start = jnp.minimum(head * size // 128 * 128, width - 256)
    return pl.multiple_of(start, 128), head * size - start


def each_head(body):
    def group(step, carry):
        for i in range(4):
            body(4 * step + i)
        return carry

    lax.fori_loop(0, HEADS // 4, group, 0)


def head_mask(low, size):
    lane = lax.broadcasted_iota(jnp.int32, (1, 256), 1)
    return (lane >= low) & (lane < low + size)


def dot_columns(left, right):
    return lax.dot_general(left, right, (((1,), (1,)), ((), ())), preferred_element_type=f32)


def head_probs(queries, keys, mask, live, scaling):
    masked = queries * mask.astype(f32).astype(bf16)
    scores = jnp.where(live > 0.0, dot_columns(masked, keys) * scaling, -1e30)
    powers = jnp.exp(scores - jnp.max(scores, axis=1, keepdims=True))
    return powers / jnp.sum(powers, axis=1, keepdims=True)


def attend_kernel(qkv_ref, live_ref, out_ref, total_ref):
    width = out_ref.shape[1]
    size = width // HEADS
    live = live_ref[0]

    def one(head):
        start, low = head_window(head, size, width)
        mask = head_mask(low, size)
        queries, keys, values = [
            qkv_ref[:, pl.ds(part * width + start, 256)] for part in range(3)
        ]
        probs = head_probs(queries, keys, mask, live, size ** (-0.5)).astype(bf16)
        mixed = dot_rows(probs, values)
        place = pl.ds(start, 256)
        total_ref[:, place] = jnp.where(mask, mixed, total_ref[:, place])

    each_head(one)
    out_ref[...] = total_ref[...].astype(bf16)


def attend(qkv, live):
    rows, wide = qkv.shape
    images = live.shape[0]
    near = rows // images
    width = wide // 3
    return pl.pallas_call(
        attend_kernel,
        out_shape=jax.ShapeDtypeStruct((rows, width), bf16),
        grid=(images,),
        in_specs=[
            pl.BlockSpec((near, wide), lambda i: (i, 0)),
            pl.BlockSpec((1, 1, near), lambda i: (i, 0, 0)),
        ],
        out_specs=pl.BlockSpec((near, width), lambda i: (i, 0)),
        scratch_shapes=[pltpu.VMEM((near, width), f32)],
        cost_estimate=pl.CostEstimate(flops=1, bytes_accessed=1, transcendentals=0),
        compiler_params=pltpu.CompilerParams(vmem_limit_bytes=8 * 2**20),
        name="attend",
    )(qkv, live)


def attend_back_kernel(qkv_ref, live_ref, grad_ref, out_ref, total_ref):
    width = grad_ref.shape[1]
    size = width // HEADS
    scaling = size ** (-0.5)
    live = live_ref[0]

    def one(head):
        start, low = head_window(head, size, width)
        mask = head_mask(low, size)
        queries, keys, values = [
            qkv_ref[:, pl.ds(part * width + start, 256)] for part in range(3)
        ]
        grads = grad_ref[:, pl.ds(start, 256)]
        probs = head_probs(queries, keys, mask, live, scaling)
        d_probs = dot_columns(grads * mask.astype(f32).astype(bf16), values)
        delta = jnp.sum(probs * d_probs, axis=1, keepdims=True)
        d_scores = probs * (d_probs - delta)
        pieces = (
            dot_rows(d_scores.astype(bf16), keys) * scaling,
            dot_rows(d_scores.T.astype(bf16), queries) * scaling,
            dot_rows(probs.T.astype(bf16), grads),
        )
        for part, piece in enumerate(pieces):
            place = pl.ds(part * width + start, 256)
            total_ref[:, place] = jnp.where(mask, piece, total_ref[:, place])

    each_head(one)
    out_ref[...] = total_ref[...].astype(bf16)


def attend_back(qkv, live, grad):
    rows, wide = qkv.shape
    images = live.shape[0]
    near = rows // images
    width = wide // 3
    return pl.pallas_call(
        attend_back_kernel,
        out_shape=jax.ShapeDtypeStruct((rows, wide), bf16),
        grid=(images,),
        in_specs=[
            pl.BlockSpec((near, wide), lambda i: (i, 0)),
            pl.BlockSpec((1, 1, near), lambda i: (i, 0, 0)),
            pl.BlockSpec((near, width), lambda i: (i, 0)),
        ],
        out_specs=pl.BlockSpec((near, wide), lambda i: (i, 0)),
        scratch_shapes=[pltpu.VMEM((near, wide), f32)],
        cost_estimate=pl.CostEstimate(flops=1, bytes_accessed=1, transcendentals=0),
        compiler_params=pltpu.CompilerParams(vmem_limit_bytes=12 * 2**20),
        name="attend_back",
    )(qkv, live, grad)


def join_kernel(lines, mine_ref, got_ref, out_ref):
    rest = mine_ref.shape[0] - lines
    out_ref[:lines] = mine_ref[:lines] + got_ref[:lines]
    out_ref[lines : lines + rest] = mine_ref[lines:]
    out_ref[lines + rest :] = got_ref[lines:]


def join(mine, got, lines):
    rows, lanes = mine.shape
    return pl.pallas_call(
        functools.partial(join_kernel, lines),
        out_shape=jax.ShapeDtypeStruct((2 * rows - lines, lanes), f32),
        cost_estimate=pl.CostEstimate(flops=1, bytes_accessed=1, transcendentals=0),
        compiler_params=pltpu.CompilerParams(vmem_limit_bytes=8 * 2**20),
        name="join",
    )(mine, got)


class Halving:
    def __init__(self, orders, count):
        self.orders = orders
        self.count = count
        self.stages = len(orders[0])
        self.message = None
        self.keeps = None
        self.received = []

    def lined(self, blocks):
        return blocks.reshape(-1, blocks.shape[1] * blocks.shape[2], 128)

    def sends(self, blocks):
        self.message = self.lined(blocks)
        return blocks

    def holds(self, blocks):
        self.keeps = [self.lined(item) for item in blocks]
        return blocks[-1]

    def step(self, token):
        stage = len(self.received)
        if stage:
            self.received[-1] = after(self.received[-1], token)
        if stage == self.stages:
            message = self.keeps[0][0]
            for piece in self.received:
                message = message + piece[0]
            self.message = message
            return message
        if stage:
            low = 1 << (self.stages - 1 - stage)
            message = self.keeps[self.stages - stage]
            for piece in self.received:
                message = message + piece[low : 2 * low]
        else:
            message = after(self.message, token)
        self.received.append(flip_stage(message, stage, self.orders, self.count))
        return message

    def result(self, rows):
        return self.message.reshape(-1, rows, 128)


def body(
    patches,
    bucket,
    keep_order,
    timesteps,
    labels,
    patch_weight,
    patch_bias,
    class_table,
    ada_weight,
    ada_bias,
    qkv_weight,
    query_bias,
    value_bias,
    proj_weight,
    proj_bias,
    up_weight,
    up_bias,
    down_weight,
    down_bias,
    final_weight,
    final_bias,
    out_grad,
):
    images, tile_slots, patch_width = patches.shape
    slot_total = keep_order.shape[1]
    width = patch_weight.shape[1]
    hidden = up_weight.shape[1]
    class_count = class_table.shape[0]
    count = lax.axis_size("dp")
    bits = count.bit_length() - 1
    tile = lax.axis_index("tile")
    own = images // 2
    half_slots = slot_total // 2
    first = tile * own

    def mine(value):
        return lax.dynamic_slice_in_dim(value, first, own, 0)

    def others(value):
        return lax.dynamic_slice_in_dim(value, own - first, own, 0)

    unit = (bucket[0] >= 0).astype(f32)

    pair = jnp.concatenate([patches, out_grad], axis=2).astype(f32)
    slots_data = jnp.concatenate([mine(pair), swap_tiles(others(pair)) * unit], axis=1).astype(bf16)
    near = jnp.arange(slot_total, dtype=jnp.int32)
    slot_ids = (near + tile * tile_slots) % slot_total

    condition = time_embed(timesteps, width) + jnp.take(class_table, labels, axis=0).astype(f32)
    cond_act = jax.nn.silu(condition).astype(bf16)
    mod_half = mm("id,de->ie", cond_act, ada_weight) + ada_bias.astype(f32)
    mod_mine, mod_recv = mine(mod_half), swap_tiles(others(mod_half))
    modulation = jnp.where(
        tile == 0,
        jnp.concatenate([mod_mine, mod_recv], axis=1),
        jnp.concatenate([mod_recv, mod_mine], axis=1),
    )
    shift_a, scale_a, gate_a, shift_m, scale_m, gate_m = [
        portion[:, None, :] for portion in jnp.split(modulation, 6, axis=1)
    ]

    my_bucket, my_order = mine(bucket), mine(keep_order)
    half_rows = jnp.where(my_bucket == 0, 8, jnp.where(my_bucket == 1, 6, 10))[:, None]
    columns = jnp.where(my_bucket == 0, 16, jnp.where(my_bucket == 1, 20, 12))[:, None]
    area = half_rows * columns
    order_valid = (my_order % tile_slots) < area
    upper = (near[:, None] < near[None, :]).astype(bf16)
    rank = mm("ij,jk->ik", order_valid.astype(bf16), upper).astype(jnp.int32)
    limit = area
    place = jnp.where(rank < limit, rank, rank - limit + half_slots)
    hit = (place[:, None, :] == near[None, :, None]) & order_valid[:, None, :]
    row_slot = jnp.sum(jnp.where(hit, my_order[:, None, :] + 1, 0), axis=2) - 1
    live = row_slot >= 0
    select = (row_slot[:, :, None] == slot_ids[None, None, :]).astype(bf16)
    row_data = mm("irs,isc->irc", select, slots_data).astype(bf16)
    row_patches, row_grads = row_data[:, :, :patch_width], row_data[:, :, patch_width:]
    local = row_slot % tile_slots
    grid_row = (row_slot // tile_slots) * half_rows + local // columns
    grid_col = local % columns
    marks = jnp.arange(GRID_MAX, dtype=jnp.int32)
    mark_row = (grid_row[:, :, None] == marks).astype(bf16)
    mark_col = (grid_col[:, :, None] == marks).astype(bf16)
    table = three_way(axis_table(width // 2))
    blank = jnp.zeros((GRID_MAX, width // 2), bf16)
    wide = jnp.concatenate(
        [patch_weight]
        + [jnp.concatenate([piece, blank], axis=1) for piece in table]
        + [jnp.concatenate([blank, piece], axis=1) for piece in table],
        axis=0,
    )
    features = jnp.concatenate([row_patches] + [mark_row] * 3 + [mark_col] * 3, axis=2)
    embedded = mm("irk,kd->ird", features, wide) + patch_bias.astype(f32)
    key_live = live[:, :half_slots]

    fast = count == 16 and (width // count) % 8 == 0 and images * slot_total == 1024
    index = lax.axis_index("dp")

    def unit_ids(orders):
        masks = [jnp.array(relative_masks(order), jnp.int32) for order in orders]
        return jnp.where(tile == 0, masks[0], masks[1]) ^ index

    def left_blocks(left):
        rows, size = left.shape[0] * left.shape[1], left.shape[2]
        flat = left.reshape(rows, size)
        blocks = turn(flat) if fast else flat.astype(f32).T
        blocks = blocks.reshape(count, size // count, rows)
        return blocks, swap_tiles(blocks)

    def right_half(*rights):
        if fast:
            keep, give = halves(tile, *[right.reshape(-1, right.shape[2]) for right in rights])
            return keep, swap_tiles(give), give
        keep, give = [], []
        for right in rights:
            size = right.shape[2] // 2
            flat = right.reshape(-1, 2 * size)
            low, high = flat[:, :size], flat[:, size:]
            keep.append(jnp.where(tile == 0, low, high))
            give.append(jnp.where(tile == 0, high, low).astype(f32))
        keep, give = jnp.concatenate(keep, axis=1), jnp.concatenate(give, axis=1)
        return keep, swap_tiles(give), give

    def plain(left, right):
        (near_left, far_left), (near_right, far_right) = left, right
        near_left = near_left.astype(bf16)
        far_left, far_right = (far_left * unit).astype(bf16), (far_right * unit).astype(bf16)
        grad = mm("brk,kc->brc", near_left, near_right) + mm("brk,kc->brc", far_left, far_right)
        grad = grad.reshape(-1, grad.shape[2])
        return lax.psum_scatter(grad, "dp", scatter_dimension=0, tiled=True)

    chains, tables = {}, {}
    for name, plan in PLAN.items():
        if fast:
            orders = unit_orders(plan)
            chains[name] = Halving(orders, count)
            if plan not in tables:
                tables[plan] = unit_ids(orders)
    todo = ORDER.split()
    token = [keep_order]
    small = []

    def gate(value):
        return after(value, token[0]) if fast else value

    def passed(value):
        token[0] = value
        return value

    def small_step():
        orders = list(range(2, bits))[::-1]
        orders = (orders + [0, 1], orders + [1, 0])
        stage, message = small[0], small[1]
        if stage:
            got = gate(small[2])
            lines = small[3]
            if fast:
                message = join(message, got, lines)
            else:
                message = jnp.concatenate(
                    [message[:lines] + got[:lines], message[lines:], got[lines:]], axis=0
                )
        else:
            message = gate(message)
        small[0], small[1] = stage + 1, message
        if stage < bits:
            small[2] = flip_stage(message, stage, orders, count)
        passed(message)

    def reach(block):
        while todo[0] != block:
            event = todo.pop(0)
            if event == "s":
                small_step()
            elif event[0] == "k":
                part = int(event[1])
                passed(chains["d%d" % part].holds(down_unit(part, KEEPS)))
            else:
                passed(chains[event].step(token[0]))
        todo.pop(0)

    def table(name):
        return gate(tables[PLAN[name]])

    def down_unit(part, ranges):
        return row_unit(table("d%d" % part), *down_left, down_right, part, ranges)

    def whole_unit(name, lefts, right, part, border):
        send, *keeps = column_unit(table(name), lefts, *right, part, border, SENDS + KEEPS)
        chains[name].holds(keeps)
        return passed(chains[name].sends(send))

    kept_x = embedded[:, :half_slots]
    normed_a, rstd_a = norm_stats(kept_x)
    attn_in = (normed_a * (1.0 + scale_a) + shift_a).astype(bf16)
    qkv_bias = jnp.concatenate([query_bias, jnp.zeros_like(query_bias), value_bias]).astype(f32)
    qkv = (mm("isd,de->ise", attn_in, qkv_weight) + qkv_bias).astype(bf16)
    qkv = qkv.reshape(own * half_slots, -1)
    live_row = key_live.astype(f32)[:, None, :]
    mixed = attend(qkv, live_row).reshape(own, half_slots, width)
    attn_out = mm("iqd,de->iqe", mixed, proj_weight) + proj_bias.astype(f32)
    middle = kept_x + gate_a * attn_out
    normed_m, rstd_m = norm_stats(middle)
    mlp_in = (normed_m * (1.0 + scale_m) + shift_m).astype(bf16)
    rows = own * half_slots
    activated, act_slope, blocks = feed_up(mlp_in.reshape(rows, width), up_weight, up_bias)
    blocks = blocks.reshape(count, hidden // count, rows)
    down_left = (blocks, swap_tiles(blocks))
    activated = activated.reshape(own, half_slots, hidden)
    mlp_out = mm("iqf,fd->iqd", activated, down_weight) + down_bias.astype(f32)
    block_out = middle + gate_m * mlp_out
    merged = jnp.concatenate([block_out, embedded[:, half_slots:]], axis=1)
    normed_f, rstd_f = norm_stats(merged)
    final_in = normed_f.astype(bf16)

    d_final = mm("isp,dp->isd", row_grads, final_weight)
    d_merged = norm_back(normed_f, rstd_f, d_final)
    d_block = d_merged[:, :half_slots]
    d_mlp = (gate_m * d_block).astype(bf16)
    d_gate_m = jnp.sum(d_block * mlp_out, axis=1)

    *down_right, give = right_half(d_mlp)
    d_mlp = after(d_mlp, give)
    if fast:
        passed(give)
        up_left = left_blocks(gate(mlp_in))
        passed(up_left[0])
        reach("Kd0")
        passed(chains["d0"].sends(down_unit(0, SENDS)[0]))
        reach("Kd1")
        passed(chains["d1"].sends(down_unit(1, SENDS)[0]))
        reach("Cp")
    d_pre = feed_back(gate(d_mlp).reshape(rows, width), down_weight, act_slope)
    d_pre = passed(d_pre.reshape(own, half_slots, hidden))
    if fast:
        *up_right, give = right_half(d_pre)
        passed(give)
        reach("Ct")
        proj_left, qkv_left = left_blocks(gate(mixed)), left_blocks(gate(attn_in))
        passed(qkv_left[0])
        reach("Ku0")
        whole_unit("u0", up_left, up_right, 0, None)
        reach("Ku1")
        whole_unit("u1", up_left, up_right, 1, None)
        reach("C1")
    else:
        down_final = plain(down_left, down_right)
        up_final = plain(left_blocks(mlp_in), right_half(d_pre)[:2])
    d_mlp_in = mm("iqf,df->iqd", gate(d_pre), up_weight)
    d_shift_m = jnp.sum(d_mlp_in, axis=1)
    d_scale_m = jnp.sum(d_mlp_in * normed_m, axis=1)
    d_middle = d_block + norm_back(normed_m, rstd_m, d_mlp_in * (1.0 + scale_m))
    d_attn = passed((gate_a * d_middle).astype(bf16))
    d_gate_a = jnp.sum(d_middle * attn_out, axis=1)
    if fast:
        reach("C2")
    else:
        proj_left, qkv_left = left_blocks(mixed), left_blocks(attn_in)
    d_mixed = mm("iqe,de->iqd", gate(d_attn), proj_weight).astype(bf16)
    d_qkv = attend_back(qkv, live_row, d_mixed.reshape(own * half_slots, width))
    d_qkv = passed(d_qkv.reshape(own, half_slots, 3 * width))
    border = d_qkv.shape[2] // 2
    if fast:
        reach("Cq")
        *both_right, give = right_half(gate(d_qkv), d_attn)
        passed(give)
        reach("Kq0")
        whole_unit("q0", qkv_left, both_right, 0, border)
        reach("Kq1")
        whole_unit("q1", qkv_left + proj_left, both_right, 1, border)
        reach("C3")
    else:
        proj_final = plain(proj_left, right_half(d_attn)[:2])
        qkv_final = plain(qkv_left, right_half(d_qkv)[:2])
    d_qkv = gate(d_qkv)
    qkv_bias_sums = jnp.sum(d_qkv.astype(f32), axis=(0, 1))
    d_attn_in = mm("ice,de->icd", d_qkv, qkv_weight)
    d_shift_a = jnp.sum(d_attn_in, axis=1)
    d_scale_a = jnp.sum(d_attn_in * normed_a, axis=1)
    d_kept = passed(d_middle + norm_back(normed_a, rstd_a, d_attn_in * (1.0 + scale_a)))
    if fast:
        reach("C4")
    d_kept, d_merged, final_in = gate(d_kept), gate(d_merged), gate(final_in)
    proj_bias_grad = jnp.sum(gate(d_attn).astype(f32), axis=(0, 1))
    up_bias_grad = jnp.sum(gate(d_pre).astype(f32), axis=(0, 1))
    down_bias_grad = jnp.sum(gate(d_mlp).astype(f32), axis=(0, 1))
    row_denoised = mm("isd,dp->isp", final_in, final_weight) + final_bias.astype(f32)
    final_weight_grad = mm("isd,isp->dp", final_in, row_grads)
    final_bias_grad = jnp.sum(row_grads.astype(f32), axis=(0, 1))
    d_low = jnp.concatenate([d_kept, d_merged[:, half_slots:]], axis=1).astype(bf16)
    row_patch_grad = mm("isd,pd->isp", d_low, patch_weight)
    patch_weight_grad = mm("isp,isd->pd", row_patches, d_low)
    patch_bias_grad = jnp.sum(d_low.astype(f32), axis=(0, 1))

    back = jnp.concatenate([row_denoised, row_patch_grad], axis=2)
    slot_out = mm("irs,irc->isc", select, jnp.concatenate(three_way(back), axis=2))
    slot_out = sum(jnp.split(slot_out, 3, axis=2))
    near_part, far_part = slot_out[:, :tile_slots], swap_tiles(slot_out[:, tile_slots:])
    slot_mine = jnp.where(
        tile == 0,
        jnp.concatenate([near_part, far_part], axis=0),
        jnp.concatenate([far_part, near_part], axis=0),
    )
    denoised, patch_grad = slot_mine[:, :, :patch_width], slot_mine[:, :, patch_width:]

    d_mod = jnp.concatenate(
        [d_shift_a, d_scale_a, d_gate_a, d_shift_m, d_scale_m, d_gate_m], axis=1
    )
    mod_width = d_mod.shape[1] // 2
    keep = lax.dynamic_slice_in_dim(d_mod, tile * mod_width, mod_width, 1)
    give = lax.dynamic_slice_in_dim(d_mod, (1 - tile) * mod_width, mod_width, 1)
    got = swap_tiles(give) * unit
    d_mod_half = jnp.where(
        tile == 0, jnp.concatenate([keep, got], axis=0), jnp.concatenate([got, keep], axis=0)
    ).astype(bf16)
    d_cond_act = mm("ie,de->id", d_mod_half, ada_weight)
    gated = jax.nn.sigmoid(condition)
    d_cond_part = d_cond_act * (gated * (1.0 + condition * (1.0 - gated)))
    d_condition = d_cond_part + swap_tiles(d_cond_part)

    sums_of = [
        patch_weight_grad,
        patch_bias_grad,
        qkv_bias_sums[:width],
        qkv_bias_sums[2 * width :],
        proj_bias_grad,
        up_bias_grad,
        down_bias_grad,
        final_weight_grad,
        final_bias_grad,
    ]
    area_all = jnp.where(bucket == 0, 128, 120)
    counts_local = jnp.stack([jnp.sum(area_all), jnp.sum(2 * area_all)]).astype(f32) * 0.5
    sums_of.append(counts_local)
    flat = jnp.concatenate([leaf.reshape(-1) for leaf in sums_of])
    flat = jnp.pad(flat, (0, (-flat.shape[0]) % 2048)).reshape(2, -1, 128)
    flat_half = lax.dynamic_index_in_dim(flat, tile, 0, keepdims=False) + swap_tiles(
        lax.dynamic_index_in_dim(flat, 1 - tile, 0, keepdims=False)
    )
    lines = flat_half.shape[0]
    marks = jnp.stack([labels, timesteps], axis=1).astype(f32)
    packed = jnp.concatenate(
        [d_mod_half.astype(f32), d_condition, jnp.pad(marks, ((0, 0), (0, 126)))], axis=1
    )
    message = passed(jnp.concatenate([flat_half, packed.reshape(-1, 128)], axis=0))
    small.extend([0, message, None, lines])
    if fast:
        reach("C5")
    else:
        for _ in range(bits + 1):
            small_step()
    message = small[1]

    every = (message[lines:] * unit).reshape(count * images, -1)
    all_mod = every[:, :mod_width].astype(bf16)
    all_cond = every[:, mod_width : mod_width + width]
    all_label = every[:, mod_width + width].astype(jnp.int32)
    all_time = every[:, mod_width + width + 1]
    one_hot = (all_label[:, None] == jnp.arange(class_count, dtype=jnp.int32)[None, :])
    block = width // count
    table_rows = lax.dynamic_slice_in_dim(class_table, index * block, block, 1)
    picked = mm("nc,cd->nd", one_hot.astype(bf16), table_rows)
    act_rows = time_columns(all_time, index * block, block, width) + picked
    act_rows = jax.nn.silu(act_rows).astype(bf16)
    ada_final = mm("nd,ne->de", act_rows, all_mod)
    ada_half = jnp.sum(all_mod.astype(f32), axis=0)
    ending = jnp.concatenate([message[:lines], ada_half.reshape(-1, 128)], axis=0)
    other = swap_tiles(ending)
    first_end = jnp.where(tile == 0, ending, other)
    second_end = jnp.where(tile == 0, other, ending)
    ada_bias_sum = jnp.concatenate(
        [first_end[lines:].reshape(-1), second_end[lines:].reshape(-1)]
    )
    summed = jnp.concatenate([first_end[:lines].reshape(-1), second_end[:lines].reshape(-1)])
    sums = []
    offset = 0
    for leaf in sums_of:
        sums.append(summed[offset : offset + leaf.size].reshape(leaf.shape))
        offset += leaf.size
    class_table_sum = mm(
        "nc,nd->cd",
        jnp.concatenate([one_hot.astype(bf16)] * 3, axis=0),
        jnp.concatenate(three_way(all_cond), axis=0),
    )

    if fast:
        todo.append("end")
        reach("end")
        part_rows = width // count
        first_part, second_part = [chains[name].result(part_rows) for name in ("d0", "d1")]
        wide = [
            item[:8].reshape(2, 4, part_rows, 128).transpose(1, 2, 0, 3).reshape(-1, 256)
            for item in (first_part, second_part)
        ]
        rest = second_part[8:]
        rest = jnp.concatenate(
            [rest[0, :, :64], rest[1, :, :64], rest[0, :, 64:], rest[1, :, 64:]], axis=0
        )
        down_final = jnp.concatenate(wide + [rest], axis=1)

        def columns_of(name):
            tiles = [chains[name + part].result(part_rows) for part in "01"]
            tiles = jnp.concatenate(tiles)
            return tiles.transpose(1, 0, 2).reshape(tiles.shape[1], -1)

        up_final = columns_of("u")
        joint = columns_of("q")
        qkv_final, proj_final = joint[:, :border], joint[:, border:]
    (
        patch_weight_sum,
        patch_bias_sum,
        query_bias_sum,
        value_bias_sum,
        proj_bias_sum,
        up_bias_sum,
        down_bias_sum,
        final_weight_sum,
        final_bias_sum,
        token_counts,
    ) = sums
    return (
        denoised,
        patch_grad,
        patch_weight_sum,
        patch_bias_sum,
        class_table_sum,
        ada_final,
        ada_bias_sum,
        qkv_final,
        query_bias_sum,
        value_bias_sum,
        proj_final,
        proj_bias_sum,
        up_final,
        up_bias_sum,
        down_final,
        down_bias_sum,
        final_weight_sum,
        final_bias_sum,
        token_counts,
    )


def solution(mesh):
    in_specs = (
        P("dp", "tile", None),
        P("dp"),
        P("dp", None),
        P("dp"),
        P("dp"),
        P(),
        P(),
        P(),
        P(None, "tile"),
        P("tile"),
        P(),
        P(),
        P(),
        P(),
        P(),
        P(),
        P(),
        P(),
        P(),
        P(),
        P(),
        P("dp", "tile", None),
    )
    out_specs = (
        P("dp", "tile", None),
        P("dp", "tile", None),
        P(),
        P(),
        P(),
        P("dp", "tile"),
        P(),
        P("dp", "tile"),
        P(),
        P(),
        P("dp", "tile"),
        P(),
        P("dp", "tile"),
        P(),
        P("dp", "tile"),
        P(),
        P(),
        P(),
        P(),
    )
    return jax.shard_map(body, mesh=mesh, in_specs=in_specs, out_specs=out_specs, check_vma=False)
```

```python
import functools
import math

import jax
import jax.numpy as jnp
from jax import lax
from jax.experimental import pallas as pl
from jax.experimental.pallas import tpu as pltpu
from jax.sharding import PartitionSpec as P

HEADS = 16
GRID_MAX = 32
epsilon = 1e-06
f32 = jnp.float32
bf16 = jnp.bfloat16


def mm(spec, left, right):
    return jnp.einsum(spec, left, right, preferred_element_type=f32)


def norm_stats(values):
    center = values - jnp.mean(values, axis=-1, keepdims=True)
    rstd = lax.rsqrt(jnp.mean(center * center, axis=-1, keepdims=True) + epsilon)
    return center * rstd, rstd


def norm_back(normed, rstd, grad):
    return rstd * (
        grad
        - jnp.mean(grad, axis=-1, keepdims=True)
        - normed * jnp.mean(grad * normed, axis=-1, keepdims=True)
    )


def gelu_parts(u):
    inner = 0.7978845608028654 * (u + 0.044715 * u * u * u)
    th = jnp.tanh(inner)
    value = 0.5 * u * (1.0 + th)
    slope = 0.5 * (1.0 + th) + 0.5 * u * (1.0 - th * th) * 0.7978845608028654 * (
        1.0 + 3.0 * 0.044715 * u * u
    )
    return value, slope


def three_way(table):
    parts = []
    rest = table
    for _ in range(3):
        piece = lax.reduce_precision(rest, exponent_bits=8, mantissa_bits=7)
        parts.append(piece.astype(bf16))
        rest = rest - piece
    return parts


def axis_table(width):
    quarter = width // 2
    omega = jnp.exp(-math.log(10000.0) * jnp.arange(quarter, dtype=f32) / quarter)
    angles = jnp.arange(GRID_MAX, dtype=f32)[:, None] * omega[None, :]
    return jnp.concatenate([jnp.sin(angles), jnp.cos(angles)], axis=-1)


def time_embed(timesteps, model_width):
    half = model_width // 2
    freqs = jnp.exp(-math.log(10000.0) * jnp.arange(half, dtype=f32) / half)
    angles = timesteps.astype(f32)[:, None] * freqs
    return jnp.concatenate([jnp.cos(angles), jnp.sin(angles)], axis=-1)


def time_columns(timesteps, first, number, model_width):
    half = model_width // 2
    column = first + jnp.arange(number, dtype=jnp.int32)
    freqs = jnp.exp(-math.log(10000.0) * (column % half).astype(f32) / half)
    angles = timesteps[:, None] * freqs
    return jnp.where(column < half, jnp.cos(angles), jnp.sin(angles))


def swap_tiles(value):
    return lax.ppermute(value, "tile", [(0, 1), (1, 0)])


def flip_stage(value, stage, orders, count):
    pairs = []
    for d in range(count):
        for t, order in enumerate(orders):
            pairs.append((2 * d + t, 2 * (d ^ (1 << order[stage])) + t))
    return lax.ppermute(value, ("dp", "tile"), pairs)


def relative_masks(order):
    bits = len(order)
    masks = []
    for rel in range(1 << bits):
        mask = 0
        for stage in range(bits):
            if (rel >> (bits - 1 - stage)) & 1:
                mask |= 1 << order[stage]
        masks.append(mask)
    return masks


def after(value, *others):
    return lax.optimization_barrier((value,) + others)[0]


CHUNK = 3
UNIT = 9
BOTH = {
    "x": (0, 1),
    "y": (1, 0),
    "1": (2, 2),
    "2": (3, 3),
}
PLAN = {
    "d0": "x1y2",
    "d1": "1x2y",
    "u0": "xy12",
    "u1": "xy12",
    "q0": "xy12",
    "q1": "xy12",
}
ORDER = """
Kd0 d0 Kd1 d1 Cp Ct k0 d0 Ku0 u0 Ku1 u1 C1 C2 Cq k1 d1 u0 u1 Kq0 Kq1 u0 q1 C3 d0 d1 u0 q0 u1 C4
q1 s d1 u1 s u0 s q0 q1 u1 d0 d1 s q1 q0 q1 s C5 q0 d0 q0
"""


def unit_orders(plan):
    return tuple([BOTH[c][t] for c in plan] for t in (0, 1))


def dot_rows(left, right):
    return lax.dot_general(left, right, (((1,), (0,)), ((), ())), preferred_element_type=f32)


def halves_kernel(tile_ref, *refs):
    number = len(refs) - 2
    keep_ref, give_ref = refs[-2:]

    def write(own):
        start = 0
        for ref in refs[:number]:
            size = ref.shape[1] // 2
            place = slice(start, start + size)
            keep_ref[:, place] = ref[:, own * size : (own + 1) * size]
            give_ref[:, place] = ref[:, (1 - own) * size : (2 - own) * size].astype(f32)
            start += size
        if start < give_ref.shape[1]:
            rest = give_ref.shape[1] - start
            give_ref[:, start:] = jnp.zeros((give_ref.shape[0], rest), f32)

    for own in (0, 1):
        pl.when(tile_ref[0] == own)(functools.partial(write, own))


def halves(tile, *values):
    rows = values[0].shape[0]
    size = sum(value.shape[1] for value in values) // 2
    padded = -(-size // 128) * 128
    return pl.pallas_call(
        halves_kernel,
        out_shape=(
            jax.ShapeDtypeStruct((rows, size), bf16),
            jax.ShapeDtypeStruct((rows, padded), f32),
        ),
        grid_spec=pltpu.PrefetchScalarGridSpec(
            num_scalar_prefetch=1,
            grid=(1,),
            in_specs=[pl.BlockSpec(value.shape, lambda i, tile: (0, 0)) for value in values],
            out_specs=(
                pl.BlockSpec((rows, size), lambda i, tile: (0, 0)),
                pl.BlockSpec((rows, padded), lambda i, tile: (0, 0)),
            ),
        ),
        cost_estimate=pl.CostEstimate(flops=1, bytes_accessed=1, transcendentals=0),
        compiler_params=pltpu.CompilerParams(vmem_limit_bytes=12 * 2**20),
        name="halves",
    )(tile[None], *values)


def turned(value):
    size = value.shape[1]
    row = lax.broadcasted_iota(jnp.int32, (size, size), 0)
    column = lax.broadcasted_iota(jnp.int32, (size, size), 1)
    identity = jnp.where(row == column, 1.0, 0.0).astype(bf16)
    return dot_columns(identity, value)


def turn_kernel(in_ref, out_ref):
    out_ref[...] = turned(in_ref[...])


def turn(value):
    rows, size = value.shape
    chunk = 384
    return pl.pallas_call(
        turn_kernel,
        out_shape=jax.ShapeDtypeStruct((size, rows), f32),
        grid=(size // chunk,),
        in_specs=[pl.BlockSpec((rows, chunk), lambda j: (0, j))],
        out_specs=pl.BlockSpec((chunk, rows), lambda j: (j, 0)),
        cost_estimate=pl.CostEstimate(flops=1, bytes_accessed=1, transcendentals=0),
        compiler_params=pltpu.CompilerParams(vmem_limit_bytes=5 * 2**20),
        name="turn",
    )(value)


def row_kernel(part, ranges, pair, ids_ref, *refs):
    near = [refs[i][0].astype(bf16) for i in range(pair)]
    far = [refs[pair + i][0].astype(bf16) for i in range(pair)]
    right_ref, right_far_ref = refs[2 * pair : 2 * pair + 2]
    out_refs = refs[2 * pair + 2 :]
    size = near[0].shape[0]
    cut = slice(256, right_ref.shape[1]) if part else slice(0, 256)
    res = dot_rows(jnp.concatenate(near, axis=0), right_ref[:, cut])
    res = res + dot_rows(jnp.concatenate(far, axis=0), right_far_ref[:, cut].astype(bf16))
    rows = size // 4
    step = pl.program_id(0) * pair + ranges[0][0]

    def write(ref, place, base):
        for c in range(2):
            for h in range(4):
                top = base + h * rows
                ref[place, 4 * c + h] = res[top : top + rows, c * 128 : (c + 1) * 128]
        if part:
            for h in range(2):
                top = base + h * rows
                ref[place, 8 + h, :, :64] = res[top : top + rows, 256:]
                top = base + (h + 2) * rows
                ref[place, 8 + h, :, 64:] = res[top : top + rows, 256:]

    for ref, (low, high) in zip(out_refs, ranges):
        block = min(high - low, pair)

        def body(ref=ref, low=low, block=block):
            for i in range(block):
                write(ref, i, (i + (low % pair)) * size)

        pl.when((step + pair > low) & (step < high))(body)


def row_unit(ids, left, left_far, rights, part, ranges):
    _, rows, near = left.shape
    pieces = 8 + 2 * part
    pair = 2
    first, number = ranges[0][0], ranges[-1][1] - ranges[0][0]

    def place(low, high):
        block = min(high - low, pair)
        last = (high - low) // block - 1
        return lambda k, ids: (jnp.clip((k * pair + first - low) // block, 0, last), 0, 0, 0)

    def source(i):
        return pl.BlockSpec((1, rows, near), lambda k, ids: (ids[first + k * pair + i], 0, 0))

    return pl.pallas_call(
        functools.partial(row_kernel, part, ranges, pair),
        out_shape=tuple(
            jax.ShapeDtypeStruct((high - low, pieces, rows // 4, 128), f32) for low, high in ranges
        ),
        grid_spec=pltpu.PrefetchScalarGridSpec(
            num_scalar_prefetch=1,
            grid=(number // pair,),
            in_specs=[source(i % pair) for i in range(2 * pair)]
            + [
                pl.BlockSpec((near, item.shape[1]), lambda k, ids: (0, 0)) for item in rights
            ],
            out_specs=tuple(
                pl.BlockSpec((min(high - low, pair), pieces, rows // 4, 128), place(low, high))
                for low, high in ranges
            ),
        ),
        cost_estimate=pl.CostEstimate(flops=1, bytes_accessed=1, transcendentals=0),
        compiler_params=pltpu.CompilerParams(vmem_limit_bytes=14 * 2**20),
        name="row_unit",
    )(ids, *[left] * pair, *[left_far] * pair, *rights)


def column_kernel(border, first_tile, ranges, number, ids_ref, *refs):
    lefts, (right_ref, right_far_ref) = refs[: 2 * number], refs[2 * number : 2 * number + 2]
    out_refs, stack_ref = refs[2 * number + 2 : -1], refs[-1]
    count, rows, near = lefts[0].shape
    half = count // 2 * rows
    step = pl.program_id(0)

    @pl.when(step == 0)
    def _():
        for i in range(number):
            for r in range(count):
                place = pl.ds(r * rows, rows)
                stack_ref[i, place, :near] = lefts[2 * i][ids_ref[r]].astype(bf16)
                stack_ref[i, place, near:] = lefts[2 * i + 1][ids_ref[r]].astype(bf16)

    right = jnp.concatenate([right_ref[...], right_far_ref[...].astype(bf16)], axis=0)

    def write(kind):
        for base in (half, 0):
            stack = [stack_ref[i, base : base + half] for i in range(number)]
            if kind == "first":
                res = dot_rows(stack[0], right)
            elif kind == "last":
                res = dot_rows(stack[1], right)
            else:
                start = (step * CHUNK + first_tile) * 128
                column = lax.broadcasted_iota(jnp.int32, (half, CHUNK * 128), 1) + start
                res = jnp.where(
                    column < border, dot_rows(stack[0], right), dot_rows(stack[1], right)
                )
            for ref, (low, high) in zip(out_refs, ranges):
                if base <= low * rows < base + half:
                    for r in range(low, high):
                        top = r * rows - base
                        for c in range(CHUNK):
                            ref[r - low, c] = res[top : top + rows, c * 128 : (c + 1) * 128]

    if number == 1:
        write("first")
    else:
        begin = (step * CHUNK + first_tile) * 128
        end = begin + CHUNK * 128

        @pl.when(end <= border)
        def _():
            write("first")

        @pl.when(begin >= border)
        def _():
            write("last")

        @pl.when((end > border) & (begin < border))
        def _():
            write("mixed")


def column_unit(ids, lefts, right, right_far, part, border, ranges):
    count, rows, near = lefts[0].shape
    first_tile = part * UNIT
    first_chunk = first_tile // CHUNK
    whole = pl.BlockSpec((count, rows, near), lambda j, ids: (0, 0, 0))
    chunk = pl.BlockSpec((near, CHUNK * 128), lambda j, ids: (0, first_chunk + j))
    number = len(lefts) // 2
    return pl.pallas_call(
        functools.partial(column_kernel, border, first_tile, ranges, number),
        out_shape=tuple(
            pltpu.HBM((high - low, UNIT, rows, 128), f32) for low, high in ranges
        ),
        grid_spec=pltpu.PrefetchScalarGridSpec(
            num_scalar_prefetch=1,
            grid=(UNIT // CHUNK,),
            in_specs=[whole] * len(lefts) + [chunk, chunk],
            out_specs=tuple(
                pl.BlockSpec((high - low, CHUNK, rows, 128), lambda j, ids: (0, j, 0, 0))
                for low, high in ranges
            ),
            scratch_shapes=[pltpu.VMEM((number, count * rows, 2 * near), bf16)],
        ),
        cost_estimate=pl.CostEstimate(flops=1, bytes_accessed=1, transcendentals=0),
        compiler_params=pltpu.CompilerParams(vmem_limit_bytes=(10 + 8 * number) * 2**20),
        name="column_unit",
    )(ids, *lefts, right, right_far)


SENDS = ((8, 16),)
KEEPS = ((0, 1), (1, 2), (2, 4), (4, 8))


PIECE = 512


def in_hbm(value):
    return pltpu.with_memory_space_constraint(value, pltpu.HBM)


def up_kernel(in_ref, weight_ref, bias_ref, act_ref, slope_ref, turned_ref):
    for low in range(0, PIECE, 256):
        place = slice(low, low + 256)
        pre = dot_rows(in_ref[...], weight_ref[:, place]) + bias_ref[:, place]
        value, slope = gelu_parts(pre)
        value = value.astype(bf16)
        act_ref[:, place] = value
        slope_ref[:, place] = slope
        turned_ref[place, :] = value.T.astype(f32)


def feed_up(value, weight, bias):
    rows, width = value.shape
    hidden = weight.shape[1]
    return pl.pallas_call(
        up_kernel,
        out_shape=(
            jax.ShapeDtypeStruct((rows, hidden), bf16),
            jax.ShapeDtypeStruct((rows, hidden), f32),
            jax.ShapeDtypeStruct((hidden, rows), f32),
        ),
        grid=(hidden // PIECE,),
        in_specs=[
            pl.BlockSpec((rows, width), lambda j: (0, 0)),
            pl.BlockSpec((width, PIECE), lambda j: (0, j)),
            pl.BlockSpec((1, PIECE), lambda j: (0, j)),
        ],
        out_specs=(
            pl.BlockSpec((rows, PIECE), lambda j: (0, j)),
            pl.BlockSpec((rows, PIECE), lambda j: (0, j)),
            pl.BlockSpec((PIECE, rows), lambda j: (j, 0)),
        ),
        cost_estimate=pl.CostEstimate(flops=1, bytes_accessed=1, transcendentals=0),
        compiler_params=pltpu.CompilerParams(vmem_limit_bytes=11 * 2**20),
        name="feed_up",
    )(value, weight, bias[None].astype(f32))


def down_back_kernel(grad_ref, weight_ref, slope_ref, out_ref):
    out_ref[...] = (dot_columns(grad_ref[...], weight_ref[...]) * slope_ref[...]).astype(bf16)


def feed_back(grad, weight, slope):
    rows, width = grad.shape
    hidden = weight.shape[0]
    return pl.pallas_call(
        down_back_kernel,
        out_shape=jax.ShapeDtypeStruct((rows, hidden), bf16),
        grid=(hidden // PIECE,),
        in_specs=[
            pl.BlockSpec((rows, width), lambda j: (0, 0)),
            pl.BlockSpec((PIECE, width), lambda j: (j, 0)),
            pl.BlockSpec((rows, PIECE), lambda j: (0, j)),
        ],
        out_specs=pl.BlockSpec((rows, PIECE), lambda j: (0, j)),
        cost_estimate=pl.CostEstimate(flops=1, bytes_accessed=1, transcendentals=0),
        compiler_params=pltpu.CompilerParams(vmem_limit_bytes=8 * 2**20),
        name="feed_back",
    )(grad, in_hbm(weight), slope)


def head_window(head, size, width):
    start = jnp.minimum(head * size // 128 * 128, width - 256)
    return pl.multiple_of(start, 128), head * size - start


def each_head(body):
    def group(step, carry):
        for i in range(4):
            body(4 * step + i)
        return carry

    lax.fori_loop(0, HEADS // 4, group, 0)


def head_mask(low, size):
    lane = lax.broadcasted_iota(jnp.int32, (1, 256), 1)
    return (lane >= low) & (lane < low + size)


def dot_columns(left, right):
    return lax.dot_general(left, right, (((1,), (1,)), ((), ())), preferred_element_type=f32)


def head_probs(queries, keys, mask, live, scaling):
    masked = queries * mask.astype(f32).astype(bf16)
    scores = jnp.where(live > 0.0, dot_columns(masked, keys) * scaling, -1e30)
    powers = jnp.exp(scores - jnp.max(scores, axis=1, keepdims=True))
    return powers / jnp.sum(powers, axis=1, keepdims=True)


def attend_kernel(qkv_ref, live_ref, out_ref, total_ref):
    width = out_ref.shape[1]
    size = width // HEADS
    live = live_ref[0]

    def one(head):
        start, low = head_window(head, size, width)
        mask = head_mask(low, size)
        queries, keys, values = [
            qkv_ref[:, pl.ds(part * width + start, 256)] for part in range(3)
        ]
        probs = head_probs(queries, keys, mask, live, size ** (-0.5)).astype(bf16)
        mixed = dot_rows(probs, values)
        place = pl.ds(start, 256)
        total_ref[:, place] = jnp.where(mask, mixed, total_ref[:, place])

    each_head(one)
    out_ref[...] = total_ref[...].astype(bf16)


def attend(qkv, live):
    rows, wide = qkv.shape
    images = live.shape[0]
    near = rows // images
    width = wide // 3
    return pl.pallas_call(
        attend_kernel,
        out_shape=jax.ShapeDtypeStruct((rows, width), bf16),
        grid=(images,),
        in_specs=[
            pl.BlockSpec((near, wide), lambda i: (i, 0)),
            pl.BlockSpec((1, 1, near), lambda i: (i, 0, 0)),
        ],
        out_specs=pl.BlockSpec((near, width), lambda i: (i, 0)),
        scratch_shapes=[pltpu.VMEM((near, width), f32)],
        cost_estimate=pl.CostEstimate(flops=1, bytes_accessed=1, transcendentals=0),
        compiler_params=pltpu.CompilerParams(vmem_limit_bytes=8 * 2**20),
        name="attend",
    )(qkv, live)


def attend_back_kernel(qkv_ref, live_ref, grad_ref, out_ref, total_ref):
    width = grad_ref.shape[1]
    size = width // HEADS
    scaling = size ** (-0.5)
    live = live_ref[0]

    def one(head):
        start, low = head_window(head, size, width)
        mask = head_mask(low, size)
        queries, keys, values = [
            qkv_ref[:, pl.ds(part * width + start, 256)] for part in range(3)
        ]
        grads = grad_ref[:, pl.ds(start, 256)]
        probs = head_probs(queries, keys, mask, live, scaling)
        d_probs = dot_columns(grads * mask.astype(f32).astype(bf16), values)
        delta = jnp.sum(probs * d_probs, axis=1, keepdims=True)
        d_scores = probs * (d_probs - delta)
        pieces = (
            dot_rows(d_scores.astype(bf16), keys) * scaling,
            dot_rows(d_scores.T.astype(bf16), queries) * scaling,
            dot_rows(probs.T.astype(bf16), grads),
        )
        for part, piece in enumerate(pieces):
            place = pl.ds(part * width + start, 256)
            total_ref[:, place] = jnp.where(mask, piece, total_ref[:, place])

    each_head(one)
    out_ref[...] = total_ref[...].astype(bf16)


def attend_back(qkv, live, grad):
    rows, wide = qkv.shape
    images = live.shape[0]
    near = rows // images
    width = wide // 3
    return pl.pallas_call(
        attend_back_kernel,
        out_shape=jax.ShapeDtypeStruct((rows, wide), bf16),
        grid=(images,),
        in_specs=[
            pl.BlockSpec((near, wide), lambda i: (i, 0)),
            pl.BlockSpec((1, 1, near), lambda i: (i, 0, 0)),
            pl.BlockSpec((near, width), lambda i: (i, 0)),
        ],
        out_specs=pl.BlockSpec((near, wide), lambda i: (i, 0)),
        scratch_shapes=[pltpu.VMEM((near, wide), f32)],
        cost_estimate=pl.CostEstimate(flops=1, bytes_accessed=1, transcendentals=0),
        compiler_params=pltpu.CompilerParams(vmem_limit_bytes=12 * 2**20),
        name="attend_back",
    )(qkv, live, grad)


def join_kernel(lines, mine_ref, got_ref, out_ref):
    rest = mine_ref.shape[0] - lines
    out_ref[:lines] = mine_ref[:lines] + got_ref[:lines]
    out_ref[lines : lines + rest] = mine_ref[lines:]
    out_ref[lines + rest :] = got_ref[lines:]


def join(mine, got, lines):
    rows, lanes = mine.shape
    return pl.pallas_call(
        functools.partial(join_kernel, lines),
        out_shape=jax.ShapeDtypeStruct((2 * rows - lines, lanes), f32),
        cost_estimate=pl.CostEstimate(flops=1, bytes_accessed=1, transcendentals=0),
        compiler_params=pltpu.CompilerParams(vmem_limit_bytes=8 * 2**20),
        name="join",
    )(mine, got)


class Halving:
    def __init__(self, orders, count):
        self.orders = orders
        self.count = count
        self.stages = len(orders[0])
        self.message = None
        self.keeps = None
        self.received = []

    def lined(self, blocks):
        return blocks.reshape(-1, blocks.shape[1] * blocks.shape[2], 128)

    def sends(self, blocks):
        self.message = self.lined(blocks)
        return blocks

    def holds(self, blocks):
        self.keeps = [self.lined(item) for item in blocks]
        return blocks[-1]

    def step(self, token):
        stage = len(self.received)
        if stage:
            self.received[-1] = after(self.received[-1], token)
        if stage == self.stages:
            message = self.keeps[0][0]
            for piece in self.received:
                message = message + piece[0]
            self.message = message
            return message
        if stage:
            low = 1 << (self.stages - 1 - stage)
            message = self.keeps[self.stages - stage]
            for piece in self.received:
                message = message + piece[low : 2 * low]
        else:
            message = after(self.message, token)
        self.received.append(flip_stage(message, stage, self.orders, self.count))
        return message

    def result(self, rows):
        return self.message.reshape(-1, rows, 128)


def body(
    patches,
    bucket,
    keep_order,
    timesteps,
    labels,
    patch_weight,
    patch_bias,
    class_table,
    ada_weight,
    ada_bias,
    qkv_weight,
    query_bias,
    value_bias,
    proj_weight,
    proj_bias,
    up_weight,
    up_bias,
    down_weight,
    down_bias,
    final_weight,
    final_bias,
    out_grad,
):
    images, tile_slots, patch_width = patches.shape
    slot_total = keep_order.shape[1]
    width = patch_weight.shape[1]
    hidden = up_weight.shape[1]
    class_count = class_table.shape[0]
    count = lax.axis_size("dp")
    bits = count.bit_length() - 1
    tile = lax.axis_index("tile")
    own = images // 2
    half_slots = slot_total // 2
    first = tile * own

    def mine(value):
        return lax.dynamic_slice_in_dim(value, first, own, 0)

    def others(value):
        return lax.dynamic_slice_in_dim(value, own - first, own, 0)

    unit = (bucket[0] >= 0).astype(f32)

    pair = jnp.concatenate([patches, out_grad], axis=2).astype(f32)
    slots_data = jnp.concatenate([mine(pair), swap_tiles(others(pair)) * unit], axis=1).astype(bf16)
    near = jnp.arange(slot_total, dtype=jnp.int32)
    slot_ids = (near + tile * tile_slots) % slot_total

    condition = time_embed(timesteps, width) + jnp.take(class_table, labels, axis=0).astype(f32)
    cond_act = jax.nn.silu(condition).astype(bf16)
    mod_half = mm("id,de->ie", cond_act, ada_weight) + ada_bias.astype(f32)
    mod_mine, mod_recv = mine(mod_half), swap_tiles(others(mod_half))
    modulation = jnp.where(
        tile == 0,
        jnp.concatenate([mod_mine, mod_recv], axis=1),
        jnp.concatenate([mod_recv, mod_mine], axis=1),
    )
    shift_a, scale_a, gate_a, shift_m, scale_m, gate_m = [
        portion[:, None, :] for portion in jnp.split(modulation, 6, axis=1)
    ]

    my_bucket, my_order = mine(bucket), mine(keep_order)
    half_rows = jnp.where(my_bucket == 0, 8, jnp.where(my_bucket == 1, 6, 10))[:, None]
    columns = jnp.where(my_bucket == 0, 16, jnp.where(my_bucket == 1, 20, 12))[:, None]
    area = half_rows * columns
    order_valid = (my_order % tile_slots) < area
    upper = (near[:, None] < near[None, :]).astype(bf16)
    rank = mm("ij,jk->ik", order_valid.astype(bf16), upper).astype(jnp.int32)
    limit = area
    place = jnp.where(rank < limit, rank, rank - limit + half_slots)
    hit = (place[:, None, :] == near[None, :, None]) & order_valid[:, None, :]
    row_slot = jnp.sum(jnp.where(hit, my_order[:, None, :] + 1, 0), axis=2) - 1
    live = row_slot >= 0
    select = (row_slot[:, :, None] == slot_ids[None, None, :]).astype(bf16)
    row_data = mm("irs,isc->irc", select, slots_data).astype(bf16)
    row_patches, row_grads = row_data[:, :, :patch_width], row_data[:, :, patch_width:]
    local = row_slot % tile_slots
    grid_row = (row_slot // tile_slots) * half_rows + local // columns
    grid_col = local % columns
    marks = jnp.arange(GRID_MAX, dtype=jnp.int32)
    mark_row = (grid_row[:, :, None] == marks).astype(bf16)
    mark_col = (grid_col[:, :, None] == marks).astype(bf16)
    table = three_way(axis_table(width // 2))
    blank = jnp.zeros((GRID_MAX, width // 2), bf16)
    wide = jnp.concatenate(
        [patch_weight]
        + [jnp.concatenate([piece, blank], axis=1) for piece in table]
        + [jnp.concatenate([blank, piece], axis=1) for piece in table],
        axis=0,
    )
    features = jnp.concatenate([row_patches] + [mark_row] * 3 + [mark_col] * 3, axis=2)
    embedded = mm("irk,kd->ird", features, wide) + patch_bias.astype(f32)
    key_live = live[:, :half_slots]

    fast = count == 16 and (width // count) % 8 == 0 and images * slot_total == 1024
    index = lax.axis_index("dp")

    def unit_ids(orders):
        masks = [jnp.array(relative_masks(order), jnp.int32) for order in orders]
        return jnp.where(tile == 0, masks[0], masks[1]) ^ index

    def left_blocks(left):
        rows, size = left.shape[0] * left.shape[1], left.shape[2]
        flat = left.reshape(rows, size)
        blocks = turn(flat) if fast else flat.astype(f32).T
        blocks = blocks.reshape(count, size // count, rows)
        return blocks, swap_tiles(blocks)

    def right_half(*rights):
        if fast:
            keep, give = halves(tile, *[right.reshape(-1, right.shape[2]) for right in rights])
            return keep, swap_tiles(give), give
        keep, give = [], []
        for right in rights:
            size = right.shape[2] // 2
            flat = right.reshape(-1, 2 * size)
            low, high = flat[:, :size], flat[:, size:]
            keep.append(jnp.where(tile == 0, low, high))
            give.append(jnp.where(tile == 0, high, low).astype(f32))
        keep, give = jnp.concatenate(keep, axis=1), jnp.concatenate(give, axis=1)
        return keep, swap_tiles(give), give

    def plain(left, right):
        (near_left, far_left), (near_right, far_right) = left, right
        near_left = near_left.astype(bf16)
        far_left, far_right = (far_left * unit).astype(bf16), (far_right * unit).astype(bf16)
        grad = mm("brk,kc->brc", near_left, near_right) + mm("brk,kc->brc", far_left, far_right)
        grad = grad.reshape(-1, grad.shape[2])
        return lax.psum_scatter(grad, "dp", scatter_dimension=0, tiled=True)

    chains, tables = {}, {}
    for name, plan in PLAN.items():
        if fast:
            orders = unit_orders(plan)
            chains[name] = Halving(orders, count)
            if plan not in tables:
                tables[plan] = unit_ids(orders)
    todo = ORDER.split()
    token = [keep_order]
    small = []

    def gate(value):
        return after(value, token[0]) if fast else value

    def passed(value):
        token[0] = value
        return value

    def small_step():
        orders = list(range(2, bits))[::-1]
        orders = (orders + [0, 1], orders + [1, 0])
        stage, message = small[0], small[1]
        if stage:
            got = gate(small[2])
            lines = small[3]
            if fast:
                message = join(message, got, lines)
            else:
                message = jnp.concatenate(
                    [message[:lines] + got[:lines], message[lines:], got[lines:]], axis=0
                )
        else:
            message = gate(message)
        small[0], small[1] = stage + 1, message
        if stage < bits:
            small[2] = flip_stage(message, stage, orders, count)
        passed(message)

    def reach(block):
        while todo[0] != block:
            event = todo.pop(0)
            if event == "s":
                small_step()
            elif event[0] == "k":
                part = int(event[1])
                passed(chains["d%d" % part].holds(down_unit(part, KEEPS)))
            else:
                passed(chains[event].step(token[0]))
        todo.pop(0)

    def table(name):
        return gate(tables[PLAN[name]])

    def down_unit(part, ranges):
        return row_unit(table("d%d" % part), *down_left, down_right, part, ranges)

    def whole_unit(name, lefts, right, part, border):
        send, *keeps = column_unit(table(name), lefts, *right, part, border, SENDS + KEEPS)
        chains[name].holds(keeps)
        return passed(chains[name].sends(send))

    kept_x = embedded[:, :half_slots]
    normed_a, rstd_a = norm_stats(kept_x)
    attn_in = (normed_a * (1.0 + scale_a) + shift_a).astype(bf16)
    qkv_bias = jnp.concatenate([query_bias, jnp.zeros_like(query_bias), value_bias]).astype(f32)
    qkv = (mm("isd,de->ise", attn_in, qkv_weight) + qkv_bias).astype(bf16)
    qkv = qkv.reshape(own * half_slots, -1)
    live_row = key_live.astype(f32)[:, None, :]
    mixed = attend(qkv, live_row).reshape(own, half_slots, width)
    attn_out = mm("iqd,de->iqe", mixed, proj_weight) + proj_bias.astype(f32)
    middle = kept_x + gate_a * attn_out
    normed_m, rstd_m = norm_stats(middle)
    mlp_in = (normed_m * (1.0 + scale_m) + shift_m).astype(bf16)
    rows = own * half_slots
    activated, act_slope, blocks = feed_up(mlp_in.reshape(rows, width), up_weight, up_bias)
    blocks = blocks.reshape(count, hidden // count, rows)
    down_left = (blocks, swap_tiles(blocks))
    activated = activated.reshape(own, half_slots, hidden)
    mlp_out = mm("iqf,fd->iqd", activated, down_weight) + down_bias.astype(f32)
    block_out = middle + gate_m * mlp_out
    merged = jnp.concatenate([block_out, embedded[:, half_slots:]], axis=1)
    normed_f, rstd_f = norm_stats(merged)
    final_in = normed_f.astype(bf16)

    d_final = mm("isp,dp->isd", row_grads, final_weight)
    d_merged = norm_back(normed_f, rstd_f, d_final)
    d_block = d_merged[:, :half_slots]
    d_mlp = (gate_m * d_block).astype(bf16)
    d_gate_m = jnp.sum(d_block * mlp_out, axis=1)

    *down_right, give = right_half(d_mlp)
    d_mlp = after(d_mlp, give)
    if fast:
        passed(give)
        up_left = left_blocks(gate(mlp_in))
        passed(up_left[0])
        reach("Kd0")
        passed(chains["d0"].sends(down_unit(0, SENDS)[0]))
        reach("Kd1")
        passed(chains["d1"].sends(down_unit(1, SENDS)[0]))
        reach("Cp")
    d_pre = feed_back(gate(d_mlp).reshape(rows, width), down_weight, act_slope)
    d_pre = passed(d_pre.reshape(own, half_slots, hidden))
    if fast:
        *up_right, give = right_half(d_pre)
        passed(give)
        reach("Ct")
        proj_left, qkv_left = left_blocks(gate(mixed)), left_blocks(gate(attn_in))
        passed(qkv_left[0])
        reach("Ku0")
        whole_unit("u0", up_left, up_right, 0, None)
        reach("Ku1")
        whole_unit("u1", up_left, up_right, 1, None)
        reach("C1")
    else:
        down_final = plain(down_left, down_right)
        up_final = plain(left_blocks(mlp_in), right_half(d_pre)[:2])
    d_mlp_in = mm("iqf,df->iqd", gate(d_pre), up_weight)
    d_shift_m = jnp.sum(d_mlp_in, axis=1)
    d_scale_m = jnp.sum(d_mlp_in * normed_m, axis=1)
    d_middle = d_block + norm_back(normed_m, rstd_m, d_mlp_in * (1.0 + scale_m))
    d_attn = passed((gate_a * d_middle).astype(bf16))
    d_gate_a = jnp.sum(d_middle * attn_out, axis=1)
    if fast:
        reach("C2")
    else:
        proj_left, qkv_left = left_blocks(mixed), left_blocks(attn_in)
    d_mixed = mm("iqe,de->iqd", gate(d_attn), proj_weight).astype(bf16)
    d_qkv = attend_back(qkv, live_row, d_mixed.reshape(own * half_slots, width))
    d_qkv = passed(d_qkv.reshape(own, half_slots, 3 * width))
    border = d_qkv.shape[2] // 2
    if fast:
        reach("Cq")
        *both_right, give = right_half(gate(d_qkv), d_attn)
        passed(give)
        reach("Kq0")
        whole_unit("q0", qkv_left, both_right, 0, border)
        reach("Kq1")
        whole_unit("q1", qkv_left + proj_left, both_right, 1, border)
        reach("C3")
    else:
        proj_final = plain(proj_left, right_half(d_attn)[:2])
        qkv_final = plain(qkv_left, right_half(d_qkv)[:2])
    d_qkv = gate(d_qkv)
    qkv_bias_sums = jnp.sum(d_qkv.astype(f32), axis=(0, 1))
    d_attn_in = mm("ice,de->icd", d_qkv, qkv_weight)
    d_shift_a = jnp.sum(d_attn_in, axis=1)
    d_scale_a = jnp.sum(d_attn_in * normed_a, axis=1)
    d_kept = passed(d_middle + norm_back(normed_a, rstd_a, d_attn_in * (1.0 + scale_a)))
    if fast:
        reach("C4")
    d_kept, d_merged, final_in = gate(d_kept), gate(d_merged), gate(final_in)
    proj_bias_grad = jnp.sum(gate(d_attn).astype(f32), axis=(0, 1))
    up_bias_grad = jnp.sum(gate(d_pre).astype(f32), axis=(0, 1))
    down_bias_grad = jnp.sum(gate(d_mlp).astype(f32), axis=(0, 1))
    row_denoised = mm("isd,dp->isp", final_in, final_weight) + final_bias.astype(f32)
    final_weight_grad = mm("isd,isp->dp", final_in, row_grads)
    final_bias_grad = jnp.sum(row_grads.astype(f32), axis=(0, 1))
    d_low = jnp.concatenate([d_kept, d_merged[:, half_slots:]], axis=1).astype(bf16)
    row_patch_grad = mm("isd,pd->isp", d_low, patch_weight)
    patch_weight_grad = mm("isp,isd->pd", row_patches, d_low)
    patch_bias_grad = jnp.sum(d_low.astype(f32), axis=(0, 1))

    back = jnp.concatenate([row_denoised, row_patch_grad], axis=2)
    slot_out = mm("irs,irc->isc", select, jnp.concatenate(three_way(back), axis=2))
    slot_out = sum(jnp.split(slot_out, 3, axis=2))
    near_part, far_part = slot_out[:, :tile_slots], swap_tiles(slot_out[:, tile_slots:])
    slot_mine = jnp.where(
        tile == 0,
        jnp.concatenate([near_part, far_part], axis=0),
        jnp.concatenate([far_part, near_part], axis=0),
    )
    denoised, patch_grad = slot_mine[:, :, :patch_width], slot_mine[:, :, patch_width:]

    d_mod = jnp.concatenate(
        [d_shift_a, d_scale_a, d_gate_a, d_shift_m, d_scale_m, d_gate_m], axis=1
    )
    mod_width = d_mod.shape[1] // 2
    keep = lax.dynamic_slice_in_dim(d_mod, tile * mod_width, mod_width, 1)
    give = lax.dynamic_slice_in_dim(d_mod, (1 - tile) * mod_width, mod_width, 1)
    got = swap_tiles(give) * unit
    d_mod_half = jnp.where(
        tile == 0, jnp.concatenate([keep, got], axis=0), jnp.concatenate([got, keep], axis=0)
    ).astype(bf16)
    d_cond_act = mm("ie,de->id", d_mod_half, ada_weight)
    gated = jax.nn.sigmoid(condition)
    d_cond_part = d_cond_act * (gated * (1.0 + condition * (1.0 - gated)))
    d_condition = d_cond_part + swap_tiles(d_cond_part)

    sums_of = [
        patch_weight_grad,
        patch_bias_grad,
        qkv_bias_sums[:width],
        qkv_bias_sums[2 * width :],
        proj_bias_grad,
        up_bias_grad,
        down_bias_grad,
        final_weight_grad,
        final_bias_grad,
    ]
    area_all = jnp.where(bucket == 0, 128, 120)
    counts_local = jnp.stack([jnp.sum(area_all), jnp.sum(2 * area_all)]).astype(f32) * 0.5
    sums_of.append(counts_local)
    flat = jnp.concatenate([leaf.reshape(-1) for leaf in sums_of])
    flat = jnp.pad(flat, (0, (-flat.shape[0]) % 2048)).reshape(2, -1, 128)
    flat_half = lax.dynamic_index_in_dim(flat, tile, 0, keepdims=False) + swap_tiles(
        lax.dynamic_index_in_dim(flat, 1 - tile, 0, keepdims=False)
    )
    lines = flat_half.shape[0]
    marks = jnp.stack([labels, timesteps], axis=1).astype(f32)
    packed = jnp.concatenate(
        [d_mod_half.astype(f32), d_condition, jnp.pad(marks, ((0, 0), (0, 126)))], axis=1
    )
    message = passed(jnp.concatenate([flat_half, packed.reshape(-1, 128)], axis=0))
    small.extend([0, message, None, lines])
    if fast:
        reach("C5")
    else:
        for _ in range(bits + 1):
            small_step()
    message = small[1]

    every = (message[lines:] * unit).reshape(count * images, -1)
    all_mod = every[:, :mod_width].astype(bf16)
    all_cond = every[:, mod_width : mod_width + width]
    all_label = every[:, mod_width + width].astype(jnp.int32)
    all_time = every[:, mod_width + width + 1]
    one_hot = (all_label[:, None] == jnp.arange(class_count, dtype=jnp.int32)[None, :])
    block = width // count
    table_rows = lax.dynamic_slice_in_dim(class_table, index * block, block, 1)
    picked = mm("nc,cd->nd", one_hot.astype(bf16), table_rows)
    act_rows = time_columns(all_time, index * block, block, width) + picked
    act_rows = jax.nn.silu(act_rows).astype(bf16)
    ada_final = mm("nd,ne->de", act_rows, all_mod)
    ada_half = jnp.sum(all_mod.astype(f32), axis=0)
    ending = jnp.concatenate([message[:lines], ada_half.reshape(-1, 128)], axis=0)
    other = swap_tiles(ending)
    first_end = jnp.where(tile == 0, ending, other)
    second_end = jnp.where(tile == 0, other, ending)
    ada_bias_sum = jnp.concatenate(
        [first_end[lines:].reshape(-1), second_end[lines:].reshape(-1)]
    )
    summed = jnp.concatenate([first_end[:lines].reshape(-1), second_end[:lines].reshape(-1)])
    sums = []
    offset = 0
    for leaf in sums_of:
        sums.append(summed[offset : offset + leaf.size].reshape(leaf.shape))
        offset += leaf.size
    class_table_sum = mm(
        "nc,nd->cd",
        jnp.concatenate([one_hot.astype(bf16)] * 3, axis=0),
        jnp.concatenate(three_way(all_cond), axis=0),
    )

    if fast:
        todo.append("end")
        reach("end")
        part_rows = width // count
        first_part, second_part = [chains[name].result(part_rows) for name in ("d0", "d1")]
        wide = [
            item[:8].reshape(2, 4, part_rows, 128).transpose(1, 2, 0, 3).reshape(-1, 256)
            for item in (first_part, second_part)
        ]
        rest = second_part[8:]
        rest = jnp.concatenate(
            [rest[0, :, :64], rest[1, :, :64], rest[0, :, 64:], rest[1, :, 64:]], axis=0
        )
        down_final = jnp.concatenate(wide + [rest], axis=1)

        def columns_of(name):
            tiles = [chains[name + part].result(part_rows) for part in "01"]
            tiles = jnp.concatenate(tiles)
            return tiles.transpose(1, 0, 2).reshape(tiles.shape[1], -1)

        up_final = columns_of("u")
        joint = columns_of("q")
        qkv_final, proj_final = joint[:, :border], joint[:, border:]
    (
        patch_weight_sum,
        patch_bias_sum,
        query_bias_sum,
        value_bias_sum,
        proj_bias_sum,
        up_bias_sum,
        down_bias_sum,
        final_weight_sum,
        final_bias_sum,
        token_counts,
    ) = sums
    return (
        denoised,
        patch_grad,
        patch_weight_sum,
        patch_bias_sum,
        class_table_sum,
        ada_final,
        ada_bias_sum,
        qkv_final,
        query_bias_sum,
        value_bias_sum,
        proj_final,
        proj_bias_sum,
        up_final,
        up_bias_sum,
        down_final,
        down_bias_sum,
        final_weight_sum,
        final_bias_sum,
        token_counts,
    )


def solution(mesh):
    in_specs = (
        P("dp", "tile", None),
        P("dp"),
        P("dp", None),
        P("dp"),
        P("dp"),
        P(),
        P(),
        P(),
        P(None, "tile"),
        P("tile"),
        P(),
        P(),
        P(),
        P(),
        P(),
        P(),
        P(),
        P(),
        P(),
        P(),
        P(),
        P("dp", "tile", None),
    )
    out_specs = (
        P("dp", "tile", None),
        P("dp", "tile", None),
        P(),
        P(),
        P(),
        P("dp", "tile"),
        P(),
        P("dp", "tile"),
        P(),
        P(),
        P("dp", "tile"),
        P(),
        P("dp", "tile"),
        P(),
        P("dp", "tile"),
        P(),
        P(),
        P(),
        P(),
    )
    return jax.shard_map(body, mesh=mesh, in_specs=in_specs, out_specs=out_specs, check_vma=False)
```

```python
import functools
import math

import jax
import jax.numpy as jnp
from jax import lax
from jax.experimental import pallas as pl
from jax.experimental.pallas import tpu as pltpu
from jax.sharding import PartitionSpec as P

HEADS = 16
GRID_MAX = 32
epsilon = 1e-06
f32 = jnp.float32
bf16 = jnp.bfloat16


def mm(spec, left, right):
    return jnp.einsum(spec, left, right, preferred_element_type=f32)


def norm_stats(values):
    center = values - jnp.mean(values, axis=-1, keepdims=True)
    rstd = lax.rsqrt(jnp.mean(center * center, axis=-1, keepdims=True) + epsilon)
    return center * rstd, rstd


def norm_back(normed, rstd, grad):
    return rstd * (
        grad
        - jnp.mean(grad, axis=-1, keepdims=True)
        - normed * jnp.mean(grad * normed, axis=-1, keepdims=True)
    )


def gelu_parts(u):
    inner = 0.7978845608028654 * (u + 0.044715 * u * u * u)
    th = jnp.tanh(inner)
    value = 0.5 * u * (1.0 + th)
    slope = 0.5 * (1.0 + th) + 0.5 * u * (1.0 - th * th) * 0.7978845608028654 * (
        1.0 + 3.0 * 0.044715 * u * u
    )
    return value, slope


def three_way(table):
    parts = []
    rest = table
    for _ in range(3):
        piece = lax.reduce_precision(rest, exponent_bits=8, mantissa_bits=7)
        parts.append(piece.astype(bf16))
        rest = rest - piece
    return parts


def axis_table(width):
    quarter = width // 2
    omega = jnp.exp(-math.log(10000.0) * jnp.arange(quarter, dtype=f32) / quarter)
    angles = jnp.arange(GRID_MAX, dtype=f32)[:, None] * omega[None, :]
    return jnp.concatenate([jnp.sin(angles), jnp.cos(angles)], axis=-1)


def time_embed(timesteps, model_width):
    half = model_width // 2
    freqs = jnp.exp(-math.log(10000.0) * jnp.arange(half, dtype=f32) / half)
    angles = timesteps.astype(f32)[:, None] * freqs
    return jnp.concatenate([jnp.cos(angles), jnp.sin(angles)], axis=-1)


def time_columns(timesteps, first, number, model_width):
    half = model_width // 2
    column = first + jnp.arange(number, dtype=jnp.int32)
    freqs = jnp.exp(-math.log(10000.0) * (column % half).astype(f32) / half)
    angles = timesteps[:, None] * freqs
    return jnp.where(column < half, jnp.cos(angles), jnp.sin(angles))


def swap_tiles(value):
    return lax.ppermute(value, "tile", [(0, 1), (1, 0)])


def flip_stage(value, stage, orders, count):
    pairs = []
    for d in range(count):
        for t, order in enumerate(orders):
            pairs.append((2 * d + t, 2 * (d ^ (1 << order[stage])) + t))
    return lax.ppermute(value, ("dp", "tile"), pairs)


def relative_masks(order):
    bits = len(order)
    masks = []
    for rel in range(1 << bits):
        mask = 0
        for stage in range(bits):
            if (rel >> (bits - 1 - stage)) & 1:
                mask |= 1 << order[stage]
        masks.append(mask)
    return masks


def after(value, *others):
    return lax.optimization_barrier((value,) + others)[0]


CHUNK = 3
UNIT = 9
BOTH = {
    "x": (0, 1),
    "y": (1, 0),
    "1": (2, 2),
    "2": (3, 3),
}
PLAN = {
    "d0": "x1y2",
    "d1": "1x2y",
    "u0": "xy12",
    "u1": "xy12",
    "q0": "xy12",
    "q1": "xy12",
}
ORDER = """
Kd0 d0 Kd1 d1 Cp Ct k0 d0 Ku0 u0 Ku1 u1 C1 C2 Cq k1 d1 u0 u1 Kq0 Kq1 u0 q1 C3 d0 d1 u0 q0 u1 C4
q1 s d1 u1 s u0 s q0 q1 u1 d0 d1 s q1 q0 q1 s C5 q0 d0 q0
"""


def unit_orders(plan):
    return tuple([BOTH[c][t] for c in plan] for t in (0, 1))


def dot_rows(left, right):
    return lax.dot_general(left, right, (((1,), (0,)), ((), ())), preferred_element_type=f32)


def halves_kernel(tile_ref, *refs):
    number = len(refs) - 2
    keep_ref, give_ref = refs[-2:]

    def write(own):
        start = 0
        for ref in refs[:number]:
            size = ref.shape[1] // 2
            place = slice(start, start + size)
            keep_ref[:, place] = ref[:, own * size : (own + 1) * size]
            give_ref[:, place] = ref[:, (1 - own) * size : (2 - own) * size].astype(f32)
            start += size
        if start < give_ref.shape[1]:
            rest = give_ref.shape[1] - start
            give_ref[:, start:] = jnp.zeros((give_ref.shape[0], rest), f32)

    for own in (0, 1):
        pl.when(tile_ref[0] == own)(functools.partial(write, own))


def halves(tile, *values):
    rows = values[0].shape[0]
    size = sum(value.shape[1] for value in values) // 2
    padded = -(-size // 128) * 128
    return pl.pallas_call(
        halves_kernel,
        out_shape=(
            jax.ShapeDtypeStruct((rows, size), bf16),
            jax.ShapeDtypeStruct((rows, padded), f32),
        ),
        grid_spec=pltpu.PrefetchScalarGridSpec(
            num_scalar_prefetch=1,
            grid=(1,),
            in_specs=[pl.BlockSpec(value.shape, lambda i, tile: (0, 0)) for value in values],
            out_specs=(
                pl.BlockSpec((rows, size), lambda i, tile: (0, 0)),
                pl.BlockSpec((rows, padded), lambda i, tile: (0, 0)),
            ),
        ),
        cost_estimate=pl.CostEstimate(flops=1, bytes_accessed=1, transcendentals=0),
        compiler_params=pltpu.CompilerParams(vmem_limit_bytes=12 * 2**20),
        name="halves",
    )(tile[None], *values)


def turned(value):
    size = value.shape[1]
    row = lax.broadcasted_iota(jnp.int32, (size, size), 0)
    column = lax.broadcasted_iota(jnp.int32, (size, size), 1)
    identity = jnp.where(row == column, 1.0, 0.0).astype(bf16)
    return dot_columns(identity, value)


def turn_kernel(in_ref, out_ref):
    out_ref[...] = turned(in_ref[...])


def turn(value):
    rows, size = value.shape
    chunk = 384
    return pl.pallas_call(
        turn_kernel,
        out_shape=jax.ShapeDtypeStruct((size, rows), f32),
        grid=(size // chunk,),
        in_specs=[pl.BlockSpec((rows, chunk), lambda j: (0, j))],
        out_specs=pl.BlockSpec((chunk, rows), lambda j: (j, 0)),
        cost_estimate=pl.CostEstimate(flops=1, bytes_accessed=1, transcendentals=0),
        compiler_params=pltpu.CompilerParams(vmem_limit_bytes=5 * 2**20),
        name="turn",
    )(value)


def row_kernel(part, ranges, pair, ids_ref, *refs):
    near = [refs[i][0].astype(bf16) for i in range(pair)]
    far = [refs[pair + i][0].astype(bf16) for i in range(pair)]
    right_ref, right_far_ref = refs[2 * pair : 2 * pair + 2]
    out_refs = refs[2 * pair + 2 :]
    size = near[0].shape[0]
    cut = slice(256, right_ref.shape[1]) if part else slice(0, 256)
    res = dot_rows(jnp.concatenate(near, axis=0), right_ref[:, cut])
    res = res + dot_rows(jnp.concatenate(far, axis=0), right_far_ref[:, cut].astype(bf16))
    rows = size // 4
    step = pl.program_id(0) * pair + ranges[0][0]

    def write(ref, place, base):
        for c in range(2):
            for h in range(4):
                top = base + h * rows
                ref[place, 4 * c + h] = res[top : top + rows, c * 128 : (c + 1) * 128]
        if part:
            for h in range(2):
                top = base + h * rows
                ref[place, 8 + h, :, :64] = res[top : top + rows, 256:]
                top = base + (h + 2) * rows
                ref[place, 8 + h, :, 64:] = res[top : top + rows, 256:]

    for ref, (low, high) in zip(out_refs, ranges):
        block = min(high - low, pair)

        def body(ref=ref, low=low, block=block):
            for i in range(block):
                write(ref, i, (i + (low % pair)) * size)

        pl.when((step + pair > low) & (step < high))(body)


def row_unit(ids, left, left_far, rights, part, ranges):
    _, rows, near = left.shape
    pieces = 8 + 2 * part
    pair = 2
    first, number = ranges[0][0], ranges[-1][1] - ranges[0][0]

    def place(low, high):
        block = min(high - low, pair)
        last = (high - low) // block - 1
        return lambda k, ids: (jnp.clip((k * pair + first - low) // block, 0, last), 0, 0, 0)

    def source(i):
        return pl.BlockSpec((1, rows, near), lambda k, ids: (ids[first + k * pair + i], 0, 0))

    return pl.pallas_call(
        functools.partial(row_kernel, part, ranges, pair),
        out_shape=tuple(
            jax.ShapeDtypeStruct((high - low, pieces, rows // 4, 128), f32) for low, high in ranges
        ),
        grid_spec=pltpu.PrefetchScalarGridSpec(
            num_scalar_prefetch=1,
            grid=(number // pair,),
            in_specs=[source(i % pair) for i in range(2 * pair)]
            + [
                pl.BlockSpec((near, item.shape[1]), lambda k, ids: (0, 0)) for item in rights
            ],
            out_specs=tuple(
                pl.BlockSpec((min(high - low, pair), pieces, rows // 4, 128), place(low, high))
                for low, high in ranges
            ),
        ),
        cost_estimate=pl.CostEstimate(flops=1, bytes_accessed=1, transcendentals=0),
        compiler_params=pltpu.CompilerParams(vmem_limit_bytes=14 * 2**20),
        name="row_unit",
    )(ids, *[left] * pair, *[left_far] * pair, *rights)


def column_kernel(border, first_tile, ranges, number, ids_ref, *refs):
    lefts, (right_ref, right_far_ref) = refs[: 2 * number], refs[2 * number : 2 * number + 2]
    out_refs, stack_ref = refs[2 * number + 2 : -1], refs[-1]
    count, rows, near = lefts[0].shape
    half = count // 2 * rows
    step = pl.program_id(0)

    @pl.when(step == 0)
    def _():
        for i in range(number):
            for r in range(count):
                place = pl.ds(r * rows, rows)
                stack_ref[i, place, :near] = lefts[2 * i][ids_ref[r]].astype(bf16)
                stack_ref[i, place, near:] = lefts[2 * i + 1][ids_ref[r]].astype(bf16)

    right = jnp.concatenate([right_ref[...], right_far_ref[...].astype(bf16)], axis=0)

    def write(kind):
        for base in (half, 0):
            stack = [stack_ref[i, base : base + half] for i in range(number)]
            if kind == "first":
                res = dot_rows(stack[0], right)
            elif kind == "last":
                res = dot_rows(stack[1], right)
            else:
                start = (step * CHUNK + first_tile) * 128
                column = lax.broadcasted_iota(jnp.int32, (half, CHUNK * 128), 1) + start
                res = jnp.where(
                    column < border, dot_rows(stack[0], right), dot_rows(stack[1], right)
                )
            for ref, (low, high) in zip(out_refs, ranges):
                if base <= low * rows < base + half:
                    for r in range(low, high):
                        top = r * rows - base
                        for c in range(CHUNK):
                            ref[r - low, c] = res[top : top + rows, c * 128 : (c + 1) * 128]

    if number == 1:
        write("first")
    else:
        begin = (step * CHUNK + first_tile) * 128
        end = begin + CHUNK * 128

        @pl.when(end <= border)
        def _():
            write("first")

        @pl.when(begin >= border)
        def _():
            write("last")

        @pl.when((end > border) & (begin < border))
        def _():
            write("mixed")


def column_unit(ids, lefts, right, right_far, part, border, ranges):
    count, rows, near = lefts[0].shape
    first_tile = part * UNIT
    first_chunk = first_tile // CHUNK
    whole = pl.BlockSpec((count, rows, near), lambda j, ids: (0, 0, 0))
    chunk = pl.BlockSpec((near, CHUNK * 128), lambda j, ids: (0, first_chunk + j))
    number = len(lefts) // 2
    return pl.pallas_call(
        functools.partial(column_kernel, border, first_tile, ranges, number),
        out_shape=tuple(
            pltpu.HBM((high - low, UNIT, rows, 128), f32) for low, high in ranges
        ),
        grid_spec=pltpu.PrefetchScalarGridSpec(
            num_scalar_prefetch=1,
            grid=(UNIT // CHUNK,),
            in_specs=[whole] * len(lefts) + [chunk, chunk],
            out_specs=tuple(
                pl.BlockSpec((high - low, CHUNK, rows, 128), lambda j, ids: (0, j, 0, 0))
                for low, high in ranges
            ),
            scratch_shapes=[pltpu.VMEM((number, count * rows, 2 * near), bf16)],
        ),
        cost_estimate=pl.CostEstimate(flops=1, bytes_accessed=1, transcendentals=0),
        compiler_params=pltpu.CompilerParams(vmem_limit_bytes=(10 + 8 * number) * 2**20),
        name="column_unit",
    )(ids, *lefts, right, right_far)


SENDS = ((8, 16),)
KEEPS = ((0, 1), (1, 2), (2, 4), (4, 8))


PIECE = 512


def in_hbm(value):
    return pltpu.with_memory_space_constraint(value, pltpu.HBM)


def up_kernel(in_ref, weight_ref, bias_ref, act_ref, slope_ref, turned_ref):
    for low in range(0, PIECE, 256):
        place = slice(low, low + 256)
        pre = dot_rows(in_ref[...], weight_ref[:, place]) + bias_ref[:, place]
        value, slope = gelu_parts(pre)
        value = value.astype(bf16)
        act_ref[:, place] = value
        slope_ref[:, place] = slope
        turned_ref[place, :] = value.T.astype(f32)


def feed_up(value, weight, bias):
    rows, width = value.shape
    hidden = weight.shape[1]
    return pl.pallas_call(
        up_kernel,
        out_shape=(
            jax.ShapeDtypeStruct((rows, hidden), bf16),
            jax.ShapeDtypeStruct((rows, hidden), f32),
            jax.ShapeDtypeStruct((hidden, rows), f32),
        ),
        grid=(hidden // PIECE,),
        in_specs=[
            pl.BlockSpec((rows, width), lambda j: (0, 0)),
            pl.BlockSpec((width, PIECE), lambda j: (0, j)),
            pl.BlockSpec((1, PIECE), lambda j: (0, j)),
        ],
        out_specs=(
            pl.BlockSpec((rows, PIECE), lambda j: (0, j)),
            pl.BlockSpec((rows, PIECE), lambda j: (0, j)),
            pl.BlockSpec((PIECE, rows), lambda j: (j, 0)),
        ),
        cost_estimate=pl.CostEstimate(flops=1, bytes_accessed=1, transcendentals=0),
        compiler_params=pltpu.CompilerParams(vmem_limit_bytes=11 * 2**20),
        name="feed_up",
    )(value, weight, bias[None].astype(f32))


def down_back_kernel(grad_ref, weight_ref, slope_ref, out_ref):
    out_ref[...] = (dot_columns(grad_ref[...], weight_ref[...]) * slope_ref[...]).astype(bf16)


def feed_back(grad, weight, slope):
    rows, width = grad.shape
    hidden = weight.shape[0]
    return pl.pallas_call(
        down_back_kernel,
        out_shape=jax.ShapeDtypeStruct((rows, hidden), bf16),
        grid=(hidden // PIECE,),
        in_specs=[
            pl.BlockSpec((rows, width), lambda j: (0, 0)),
            pl.BlockSpec((PIECE, width), lambda j: (j, 0)),
            pl.BlockSpec((rows, PIECE), lambda j: (0, j)),
        ],
        out_specs=pl.BlockSpec((rows, PIECE), lambda j: (0, j)),
        cost_estimate=pl.CostEstimate(flops=1, bytes_accessed=1, transcendentals=0),
        compiler_params=pltpu.CompilerParams(vmem_limit_bytes=8 * 2**20),
        name="feed_back",
    )(grad, in_hbm(weight), slope)


def head_window(head, size, width):
    start = jnp.minimum(head * size // 128 * 128, width - 256)
    return pl.multiple_of(start, 128), head * size - start


def each_head(body):
    def group(step, carry):
        for i in range(8):
            body(8 * step + i)
        return carry

    lax.fori_loop(0, HEADS // 8, group, 0)


def head_mask(low, size):
    lane = lax.broadcasted_iota(jnp.int32, (1, 256), 1)
    return (lane >= low) & (lane < low + size)


def dot_columns(left, right):
    return lax.dot_general(left, right, (((1,), (1,)), ((), ())), preferred_element_type=f32)


def head_probs(queries, keys, mask, live, scaling):
    masked = queries * mask.astype(f32).astype(bf16)
    scores = jnp.where(live > 0.0, dot_columns(masked, keys) * scaling, -1e30)
    powers = jnp.exp(scores - jnp.max(scores, axis=1, keepdims=True))
    return powers / jnp.sum(powers, axis=1, keepdims=True)


def attend_kernel(qkv_ref, live_ref, out_ref, total_ref):
    width = out_ref.shape[1]
    size = width // HEADS
    live = live_ref[0]

    def one(head):
        start, low = head_window(head, size, width)
        mask = head_mask(low, size)
        queries, keys, values = [
            qkv_ref[:, pl.ds(part * width + start, 256)] for part in range(3)
        ]
        probs = head_probs(queries, keys, mask, live, size ** (-0.5)).astype(bf16)
        mixed = dot_rows(probs, values)
        place = pl.ds(start, 256)
        total_ref[:, place] = jnp.where(mask, mixed, total_ref[:, place])

    each_head(one)
    out_ref[...] = total_ref[...].astype(bf16)


def attend(qkv, live):
    rows, wide = qkv.shape
    images = live.shape[0]
    near = rows // images
    width = wide // 3
    return pl.pallas_call(
        attend_kernel,
        out_shape=jax.ShapeDtypeStruct((rows, width), bf16),
        grid=(images,),
        in_specs=[
            pl.BlockSpec((near, wide), lambda i: (i, 0)),
            pl.BlockSpec((1, 1, near), lambda i: (i, 0, 0)),
        ],
        out_specs=pl.BlockSpec((near, width), lambda i: (i, 0)),
        scratch_shapes=[pltpu.VMEM((near, width), f32)],
        cost_estimate=pl.CostEstimate(flops=1, bytes_accessed=1, transcendentals=0),
        compiler_params=pltpu.CompilerParams(vmem_limit_bytes=8 * 2**20),
        name="attend",
    )(qkv, live)


def attend_back_kernel(qkv_ref, live_ref, grad_ref, out_ref, total_ref):
    width = grad_ref.shape[1]
    size = width // HEADS
    scaling = size ** (-0.5)
    live = live_ref[0]

    def one(head):
        start, low = head_window(head, size, width)
        mask = head_mask(low, size)
        queries, keys, values = [
            qkv_ref[:, pl.ds(part * width + start, 256)] for part in range(3)
        ]
        grads = grad_ref[:, pl.ds(start, 256)]
        probs = head_probs(queries, keys, mask, live, scaling)
        d_probs = dot_columns(grads * mask.astype(f32).astype(bf16), values)
        delta = jnp.sum(probs * d_probs, axis=1, keepdims=True)
        d_scores = probs * (d_probs - delta)
        pieces = (
            dot_rows(d_scores.astype(bf16), keys) * scaling,
            dot_rows(d_scores.T.astype(bf16), queries) * scaling,
            dot_rows(probs.T.astype(bf16), grads),
        )
        for part, piece in enumerate(pieces):
            place = pl.ds(part * width + start, 256)
            total_ref[:, place] = jnp.where(mask, piece, total_ref[:, place])

    each_head(one)
    out_ref[...] = total_ref[...].astype(bf16)


def attend_back(qkv, live, grad):
    rows, wide = qkv.shape
    images = live.shape[0]
    near = rows // images
    width = wide // 3
    return pl.pallas_call(
        attend_back_kernel,
        out_shape=jax.ShapeDtypeStruct((rows, wide), bf16),
        grid=(images,),
        in_specs=[
            pl.BlockSpec((near, wide), lambda i: (i, 0)),
            pl.BlockSpec((1, 1, near), lambda i: (i, 0, 0)),
            pl.BlockSpec((near, width), lambda i: (i, 0)),
        ],
        out_specs=pl.BlockSpec((near, wide), lambda i: (i, 0)),
        scratch_shapes=[pltpu.VMEM((near, wide), f32)],
        cost_estimate=pl.CostEstimate(flops=1, bytes_accessed=1, transcendentals=0),
        compiler_params=pltpu.CompilerParams(vmem_limit_bytes=12 * 2**20),
        name="attend_back",
    )(qkv, live, grad)


def join_kernel(lines, mine_ref, got_ref, out_ref):
    rest = mine_ref.shape[0] - lines
    out_ref[:lines] = mine_ref[:lines] + got_ref[:lines]
    out_ref[lines : lines + rest] = mine_ref[lines:]
    out_ref[lines + rest :] = got_ref[lines:]


def join(mine, got, lines):
    rows, lanes = mine.shape
    return pl.pallas_call(
        functools.partial(join_kernel, lines),
        out_shape=jax.ShapeDtypeStruct((2 * rows - lines, lanes), f32),
        cost_estimate=pl.CostEstimate(flops=1, bytes_accessed=1, transcendentals=0),
        compiler_params=pltpu.CompilerParams(vmem_limit_bytes=8 * 2**20),
        name="join",
    )(mine, got)


class Halving:
    def __init__(self, orders, count):
        self.orders = orders
        self.count = count
        self.stages = len(orders[0])
        self.message = None
        self.keeps = None
        self.received = []

    def lined(self, blocks):
        return blocks.reshape(-1, blocks.shape[1] * blocks.shape[2], 128)

    def sends(self, blocks):
        self.message = self.lined(blocks)
        return blocks

    def holds(self, blocks):
        self.keeps = [self.lined(item) for item in blocks]
        return blocks[-1]

    def step(self, token):
        stage = len(self.received)
        if stage:
            self.received[-1] = after(self.received[-1], token)
        if stage == self.stages:
            message = self.keeps[0][0]
            for piece in self.received:
                message = message + piece[0]
            self.message = message
            return message
        if stage:
            low = 1 << (self.stages - 1 - stage)
            message = self.keeps[self.stages - stage]
            for piece in self.received:
                message = message + piece[low : 2 * low]
        else:
            message = after(self.message, token)
        self.received.append(flip_stage(message, stage, self.orders, self.count))
        return message

    def result(self, rows):
        return self.message.reshape(-1, rows, 128)


def body(
    patches,
    bucket,
    keep_order,
    timesteps,
    labels,
    patch_weight,
    patch_bias,
    class_table,
    ada_weight,
    ada_bias,
    qkv_weight,
    query_bias,
    value_bias,
    proj_weight,
    proj_bias,
    up_weight,
    up_bias,
    down_weight,
    down_bias,
    final_weight,
    final_bias,
    out_grad,
):
    images, tile_slots, patch_width = patches.shape
    slot_total = keep_order.shape[1]
    width = patch_weight.shape[1]
    hidden = up_weight.shape[1]
    class_count = class_table.shape[0]
    count = lax.axis_size("dp")
    bits = count.bit_length() - 1
    tile = lax.axis_index("tile")
    own = images // 2
    half_slots = slot_total // 2
    first = tile * own

    def mine(value):
        return lax.dynamic_slice_in_dim(value, first, own, 0)

    def others(value):
        return lax.dynamic_slice_in_dim(value, own - first, own, 0)

    unit = (bucket[0] >= 0).astype(f32)

    pair = jnp.concatenate([patches, out_grad], axis=2).astype(f32)
    slots_data = jnp.concatenate([mine(pair), swap_tiles(others(pair)) * unit], axis=1).astype(bf16)
    near = jnp.arange(slot_total, dtype=jnp.int32)
    slot_ids = (near + tile * tile_slots) % slot_total

    condition = time_embed(timesteps, width) + jnp.take(class_table, labels, axis=0).astype(f32)
    cond_act = jax.nn.silu(condition).astype(bf16)
    mod_half = mm("id,de->ie", cond_act, ada_weight) + ada_bias.astype(f32)
    mod_mine, mod_recv = mine(mod_half), swap_tiles(others(mod_half))
    modulation = jnp.where(
        tile == 0,
        jnp.concatenate([mod_mine, mod_recv], axis=1),
        jnp.concatenate([mod_recv, mod_mine], axis=1),
    )
    shift_a, scale_a, gate_a, shift_m, scale_m, gate_m = [
        portion[:, None, :] for portion in jnp.split(modulation, 6, axis=1)
    ]

    my_bucket, my_order = mine(bucket), mine(keep_order)
    half_rows = jnp.where(my_bucket == 0, 8, jnp.where(my_bucket == 1, 6, 10))[:, None]
    columns = jnp.where(my_bucket == 0, 16, jnp.where(my_bucket == 1, 20, 12))[:, None]
    area = half_rows * columns
    order_valid = (my_order % tile_slots) < area
    upper = (near[:, None] < near[None, :]).astype(bf16)
    rank = mm("ij,jk->ik", order_valid.astype(bf16), upper).astype(jnp.int32)
    limit = area
    place = jnp.where(rank < limit, rank, rank - limit + half_slots)
    hit = (place[:, None, :] == near[None, :, None]) & order_valid[:, None, :]
    row_slot = jnp.sum(jnp.where(hit, my_order[:, None, :] + 1, 0), axis=2) - 1
    live = row_slot >= 0
    select = (row_slot[:, :, None] == slot_ids[None, None, :]).astype(bf16)
    row_data = mm("irs,isc->irc", select, slots_data).astype(bf16)
    row_patches, row_grads = row_data[:, :, :patch_width], row_data[:, :, patch_width:]
    local = row_slot % tile_slots
    grid_row = (row_slot // tile_slots) * half_rows + local // columns
    grid_col = local % columns
    marks = jnp.arange(GRID_MAX, dtype=jnp.int32)
    mark_row = (grid_row[:, :, None] == marks).astype(bf16)
    mark_col = (grid_col[:, :, None] == marks).astype(bf16)
    table = three_way(axis_table(width // 2))
    blank = jnp.zeros((GRID_MAX, width // 2), bf16)
    wide = jnp.concatenate(
        [patch_weight]
        + [jnp.concatenate([piece, blank], axis=1) for piece in table]
        + [jnp.concatenate([blank, piece], axis=1) for piece in table],
        axis=0,
    )
    features = jnp.concatenate([row_patches] + [mark_row] * 3 + [mark_col] * 3, axis=2)
    embedded = mm("irk,kd->ird", features, wide) + patch_bias.astype(f32)
    key_live = live[:, :half_slots]

    fast = count == 16 and (width // count) % 8 == 0 and images * slot_total == 1024
    index = lax.axis_index("dp")

    def unit_ids(orders):
        masks = [jnp.array(relative_masks(order), jnp.int32) for order in orders]
        return jnp.where(tile == 0, masks[0], masks[1]) ^ index

    def left_blocks(left):
        rows, size = left.shape[0] * left.shape[1], left.shape[2]
        flat = left.reshape(rows, size)
        blocks = turn(flat) if fast else flat.astype(f32).T
        blocks = blocks.reshape(count, size // count, rows)
        return blocks, swap_tiles(blocks)

    def right_half(*rights):
        if fast:
            keep, give = halves(tile, *[right.reshape(-1, right.shape[2]) for right in rights])
            return keep, swap_tiles(give), give
        keep, give = [], []
        for right in rights:
            size = right.shape[2] // 2
            flat = right.reshape(-1, 2 * size)
            low, high = flat[:, :size], flat[:, size:]
            keep.append(jnp.where(tile == 0, low, high))
            give.append(jnp.where(tile == 0, high, low).astype(f32))
        keep, give = jnp.concatenate(keep, axis=1), jnp.concatenate(give, axis=1)
        return keep, swap_tiles(give), give

    def plain(left, right):
        (near_left, far_left), (near_right, far_right) = left, right
        near_left = near_left.astype(bf16)
        far_left, far_right = (far_left * unit).astype(bf16), (far_right * unit).astype(bf16)
        grad = mm("brk,kc->brc", near_left, near_right) + mm("brk,kc->brc", far_left, far_right)
        grad = grad.reshape(-1, grad.shape[2])
        return lax.psum_scatter(grad, "dp", scatter_dimension=0, tiled=True)

    chains, tables = {}, {}
    for name, plan in PLAN.items():
        if fast:
            orders = unit_orders(plan)
            chains[name] = Halving(orders, count)
            if plan not in tables:
                tables[plan] = unit_ids(orders)
    todo = ORDER.split()
    token = [keep_order]
    small = []

    def gate(value):
        return after(value, token[0]) if fast else value

    def passed(value):
        token[0] = value
        return value

    def small_step():
        orders = list(range(2, bits))[::-1]
        orders = (orders + [0, 1], orders + [1, 0])
        stage, message = small[0], small[1]
        if stage:
            got = gate(small[2])
            lines = small[3]
            if fast:
                message = join(message, got, lines)
            else:
                message = jnp.concatenate(
                    [message[:lines] + got[:lines], message[lines:], got[lines:]], axis=0
                )
        else:
            message = gate(message)
        small[0], small[1] = stage + 1, message
        if stage < bits:
            small[2] = flip_stage(message, stage, orders, count)
        passed(message)

    def reach(block):
        while todo[0] != block:
            event = todo.pop(0)
            if event == "s":
                small_step()
            elif event[0] == "k":
                part = int(event[1])
                passed(chains["d%d" % part].holds(down_unit(part, KEEPS)))
            else:
                passed(chains[event].step(token[0]))
        todo.pop(0)

    def table(name):
        return gate(tables[PLAN[name]])

    def down_unit(part, ranges):
        return row_unit(table("d%d" % part), *down_left, down_right, part, ranges)

    def whole_unit(name, lefts, right, part, border):
        send, *keeps = column_unit(table(name), lefts, *right, part, border, SENDS + KEEPS)
        chains[name].holds(keeps)
        return passed(chains[name].sends(send))

    kept_x = embedded[:, :half_slots]
    normed_a, rstd_a = norm_stats(kept_x)
    attn_in = (normed_a * (1.0 + scale_a) + shift_a).astype(bf16)
    qkv_bias = jnp.concatenate([query_bias, jnp.zeros_like(query_bias), value_bias]).astype(f32)
    qkv = (mm("isd,de->ise", attn_in, qkv_weight) + qkv_bias).astype(bf16)
    qkv = qkv.reshape(own * half_slots, -1)
    live_row = key_live.astype(f32)[:, None, :]
    mixed = attend(qkv, live_row).reshape(own, half_slots, width)
    attn_out = mm("iqd,de->iqe", mixed, proj_weight) + proj_bias.astype(f32)
    middle = kept_x + gate_a * attn_out
    normed_m, rstd_m = norm_stats(middle)
    mlp_in = (normed_m * (1.0 + scale_m) + shift_m).astype(bf16)
    rows = own * half_slots
    activated, act_slope, blocks = feed_up(mlp_in.reshape(rows, width), up_weight, up_bias)
    blocks = blocks.reshape(count, hidden // count, rows)
    down_left = (blocks, swap_tiles(blocks))
    activated = activated.reshape(own, half_slots, hidden)
    mlp_out = mm("iqf,fd->iqd", activated, down_weight) + down_bias.astype(f32)
    block_out = middle + gate_m * mlp_out
    merged = jnp.concatenate([block_out, embedded[:, half_slots:]], axis=1)
    normed_f, rstd_f = norm_stats(merged)
    final_in = normed_f.astype(bf16)

    d_final = mm("isp,dp->isd", row_grads, final_weight)
    d_merged = norm_back(normed_f, rstd_f, d_final)
    d_block = d_merged[:, :half_slots]
    d_mlp = (gate_m * d_block).astype(bf16)
    d_gate_m = jnp.sum(d_block * mlp_out, axis=1)

    *down_right, give = right_half(d_mlp)
    d_mlp = after(d_mlp, give)
    if fast:
        passed(give)
        up_left = left_blocks(gate(mlp_in))
        passed(up_left[0])
        reach("Kd0")
        passed(chains["d0"].sends(down_unit(0, SENDS)[0]))
        reach("Kd1")
        passed(chains["d1"].sends(down_unit(1, SENDS)[0]))
        reach("Cp")
    d_pre = feed_back(gate(d_mlp).reshape(rows, width), down_weight, act_slope)
    d_pre = passed(d_pre.reshape(own, half_slots, hidden))
    if fast:
        *up_right, give = right_half(d_pre)
        passed(give)
        reach("Ct")
        proj_left, qkv_left = left_blocks(gate(mixed)), left_blocks(gate(attn_in))
        passed(qkv_left[0])
        reach("Ku0")
        whole_unit("u0", up_left, up_right, 0, None)
        reach("Ku1")
        whole_unit("u1", up_left, up_right, 1, None)
        reach("C1")
    else:
        down_final = plain(down_left, down_right)
        up_final = plain(left_blocks(mlp_in), right_half(d_pre)[:2])
    d_mlp_in = mm("iqf,df->iqd", gate(d_pre), up_weight)
    d_shift_m = jnp.sum(d_mlp_in, axis=1)
    d_scale_m = jnp.sum(d_mlp_in * normed_m, axis=1)
    d_middle = d_block + norm_back(normed_m, rstd_m, d_mlp_in * (1.0 + scale_m))
    d_attn = passed((gate_a * d_middle).astype(bf16))
    d_gate_a = jnp.sum(d_middle * attn_out, axis=1)
    if fast:
        reach("C2")
    else:
        proj_left, qkv_left = left_blocks(mixed), left_blocks(attn_in)
    d_mixed = mm("iqe,de->iqd", gate(d_attn), proj_weight).astype(bf16)
    d_qkv = attend_back(qkv, live_row, d_mixed.reshape(own * half_slots, width))
    d_qkv = passed(d_qkv.reshape(own, half_slots, 3 * width))
    border = d_qkv.shape[2] // 2
    if fast:
        reach("Cq")
        *both_right, give = right_half(gate(d_qkv), d_attn)
        passed(give)
        reach("Kq0")
        whole_unit("q0", qkv_left, both_right, 0, border)
        reach("Kq1")
        whole_unit("q1", qkv_left + proj_left, both_right, 1, border)
        reach("C3")
    else:
        proj_final = plain(proj_left, right_half(d_attn)[:2])
        qkv_final = plain(qkv_left, right_half(d_qkv)[:2])
    d_qkv = gate(d_qkv)
    qkv_bias_sums = jnp.sum(d_qkv.astype(f32), axis=(0, 1))
    d_attn_in = mm("ice,de->icd", d_qkv, qkv_weight)
    d_shift_a = jnp.sum(d_attn_in, axis=1)
    d_scale_a = jnp.sum(d_attn_in * normed_a, axis=1)
    d_kept = passed(d_middle + norm_back(normed_a, rstd_a, d_attn_in * (1.0 + scale_a)))
    if fast:
        reach("C4")
    d_kept, d_merged, final_in = gate(d_kept), gate(d_merged), gate(final_in)
    proj_bias_grad = jnp.sum(gate(d_attn).astype(f32), axis=(0, 1))
    up_bias_grad = jnp.sum(gate(d_pre).astype(f32), axis=(0, 1))
    down_bias_grad = jnp.sum(gate(d_mlp).astype(f32), axis=(0, 1))
    row_denoised = mm("isd,dp->isp", final_in, final_weight) + final_bias.astype(f32)
    final_weight_grad = mm("isd,isp->dp", final_in, row_grads)
    final_bias_grad = jnp.sum(row_grads.astype(f32), axis=(0, 1))
    d_low = jnp.concatenate([d_kept, d_merged[:, half_slots:]], axis=1).astype(bf16)
    row_patch_grad = mm("isd,pd->isp", d_low, patch_weight)
    patch_weight_grad = mm("isp,isd->pd", row_patches, d_low)
    patch_bias_grad = jnp.sum(d_low.astype(f32), axis=(0, 1))

    back = jnp.concatenate([row_denoised, row_patch_grad], axis=2)
    slot_out = mm("irs,irc->isc", select, jnp.concatenate(three_way(back), axis=2))
    slot_out = sum(jnp.split(slot_out, 3, axis=2))
    near_part, far_part = slot_out[:, :tile_slots], swap_tiles(slot_out[:, tile_slots:])
    slot_mine = jnp.where(
        tile == 0,
        jnp.concatenate([near_part, far_part], axis=0),
        jnp.concatenate([far_part, near_part], axis=0),
    )
    denoised, patch_grad = slot_mine[:, :, :patch_width], slot_mine[:, :, patch_width:]

    d_mod = jnp.concatenate(
        [d_shift_a, d_scale_a, d_gate_a, d_shift_m, d_scale_m, d_gate_m], axis=1
    )
    mod_width = d_mod.shape[1] // 2
    keep = lax.dynamic_slice_in_dim(d_mod, tile * mod_width, mod_width, 1)
    give = lax.dynamic_slice_in_dim(d_mod, (1 - tile) * mod_width, mod_width, 1)
    got = swap_tiles(give) * unit
    d_mod_half = jnp.where(
        tile == 0, jnp.concatenate([keep, got], axis=0), jnp.concatenate([got, keep], axis=0)
    ).astype(bf16)
    d_cond_act = mm("ie,de->id", d_mod_half, ada_weight)
    gated = jax.nn.sigmoid(condition)
    d_cond_part = d_cond_act * (gated * (1.0 + condition * (1.0 - gated)))
    d_condition = d_cond_part + swap_tiles(d_cond_part)

    sums_of = [
        patch_weight_grad,
        patch_bias_grad,
        qkv_bias_sums[:width],
        qkv_bias_sums[2 * width :],
        proj_bias_grad,
        up_bias_grad,
        down_bias_grad,
        final_weight_grad,
        final_bias_grad,
    ]
    area_all = jnp.where(bucket == 0, 128, 120)
    counts_local = jnp.stack([jnp.sum(area_all), jnp.sum(2 * area_all)]).astype(f32) * 0.5
    sums_of.append(counts_local)
    flat = jnp.concatenate([leaf.reshape(-1) for leaf in sums_of])
    flat = jnp.pad(flat, (0, (-flat.shape[0]) % 2048)).reshape(2, -1, 128)
    flat_half = lax.dynamic_index_in_dim(flat, tile, 0, keepdims=False) + swap_tiles(
        lax.dynamic_index_in_dim(flat, 1 - tile, 0, keepdims=False)
    )
    lines = flat_half.shape[0]
    marks = jnp.stack([labels, timesteps], axis=1).astype(f32)
    packed = jnp.concatenate(
        [d_mod_half.astype(f32), d_condition, jnp.pad(marks, ((0, 0), (0, 126)))], axis=1
    )
    message = passed(jnp.concatenate([flat_half, packed.reshape(-1, 128)], axis=0))
    small.extend([0, message, None, lines])
    if fast:
        reach("C5")
    else:
        for _ in range(bits + 1):
            small_step()
    message = small[1]

    every = (message[lines:] * unit).reshape(count * images, -1)
    all_mod = every[:, :mod_width].astype(bf16)
    all_cond = every[:, mod_width : mod_width + width]
    all_label = every[:, mod_width + width].astype(jnp.int32)
    all_time = every[:, mod_width + width + 1]
    one_hot = (all_label[:, None] == jnp.arange(class_count, dtype=jnp.int32)[None, :])
    block = width // count
    table_rows = lax.dynamic_slice_in_dim(class_table, index * block, block, 1)
    picked = mm("nc,cd->nd", one_hot.astype(bf16), table_rows)
    act_rows = time_columns(all_time, index * block, block, width) + picked
    act_rows = jax.nn.silu(act_rows).astype(bf16)
    ada_final = mm("nd,ne->de", act_rows, all_mod)
    ada_half = jnp.sum(all_mod.astype(f32), axis=0)
    ending = jnp.concatenate([message[:lines], ada_half.reshape(-1, 128)], axis=0)
    other = swap_tiles(ending)
    first_end = jnp.where(tile == 0, ending, other)
    second_end = jnp.where(tile == 0, other, ending)
    ada_bias_sum = jnp.concatenate(
        [first_end[lines:].reshape(-1), second_end[lines:].reshape(-1)]
    )
    summed = jnp.concatenate([first_end[:lines].reshape(-1), second_end[:lines].reshape(-1)])
    sums = []
    offset = 0
    for leaf in sums_of:
        sums.append(summed[offset : offset + leaf.size].reshape(leaf.shape))
        offset += leaf.size
    class_table_sum = mm(
        "nc,nd->cd",
        jnp.concatenate([one_hot.astype(bf16)] * 3, axis=0),
        jnp.concatenate(three_way(all_cond), axis=0),
    )

    if fast:
        todo.append("end")
        reach("end")
        part_rows = width // count
        first_part, second_part = [chains[name].result(part_rows) for name in ("d0", "d1")]
        wide = [
            item[:8].reshape(2, 4, part_rows, 128).transpose(1, 2, 0, 3).reshape(-1, 256)
            for item in (first_part, second_part)
        ]
        rest = second_part[8:]
        rest = jnp.concatenate(
            [rest[0, :, :64], rest[1, :, :64], rest[0, :, 64:], rest[1, :, 64:]], axis=0
        )
        down_final = jnp.concatenate(wide + [rest], axis=1)

        def columns_of(name):
            tiles = [chains[name + part].result(part_rows) for part in "01"]
            tiles = jnp.concatenate(tiles)
            return tiles.transpose(1, 0, 2).reshape(tiles.shape[1], -1)

        up_final = columns_of("u")
        joint = columns_of("q")
        qkv_final, proj_final = joint[:, :border], joint[:, border:]
    (
        patch_weight_sum,
        patch_bias_sum,
        query_bias_sum,
        value_bias_sum,
        proj_bias_sum,
        up_bias_sum,
        down_bias_sum,
        final_weight_sum,
        final_bias_sum,
        token_counts,
    ) = sums
    return (
        denoised,
        patch_grad,
        patch_weight_sum,
        patch_bias_sum,
        class_table_sum,
        ada_final,
        ada_bias_sum,
        qkv_final,
        query_bias_sum,
        value_bias_sum,
        proj_final,
        proj_bias_sum,
        up_final,
        up_bias_sum,
        down_final,
        down_bias_sum,
        final_weight_sum,
        final_bias_sum,
        token_counts,
    )


def solution(mesh):
    in_specs = (
        P("dp", "tile", None),
        P("dp"),
        P("dp", None),
        P("dp"),
        P("dp"),
        P(),
        P(),
        P(),
        P(None, "tile"),
        P("tile"),
        P(),
        P(),
        P(),
        P(),
        P(),
        P(),
        P(),
        P(),
        P(),
        P(),
        P(),
        P("dp", "tile", None),
    )
    out_specs = (
        P("dp", "tile", None),
        P("dp", "tile", None),
        P(),
        P(),
        P(),
        P("dp", "tile"),
        P(),
        P("dp", "tile"),
        P(),
        P(),
        P("dp", "tile"),
        P(),
        P("dp", "tile"),
        P(),
        P("dp", "tile"),
        P(),
        P(),
        P(),
        P(),
    )
    return jax.shard_map(body, mesh=mesh, in_specs=in_specs, out_specs=out_specs, check_vma=False)
```

```python
import functools
import math

import jax
import jax.numpy as jnp
from jax import lax
from jax.experimental import pallas as pl
from jax.experimental.pallas import tpu as pltpu
from jax.sharding import PartitionSpec as P

HEADS = 16
GRID_MAX = 32
epsilon = 1e-06
f32 = jnp.float32
bf16 = jnp.bfloat16


def mm(spec, left, right):
    return jnp.einsum(spec, left, right, preferred_element_type=f32)


def norm_stats(values):
    center = values - jnp.mean(values, axis=-1, keepdims=True)
    rstd = lax.rsqrt(jnp.mean(center * center, axis=-1, keepdims=True) + epsilon)
    return center * rstd, rstd


def norm_back(normed, rstd, grad):
    return rstd * (
        grad
        - jnp.mean(grad, axis=-1, keepdims=True)
        - normed * jnp.mean(grad * normed, axis=-1, keepdims=True)
    )


def gelu_parts(u):
    inner = 0.7978845608028654 * (u + 0.044715 * u * u * u)
    th = jnp.tanh(inner)
    value = 0.5 * u * (1.0 + th)
    slope = 0.5 * (1.0 + th) + 0.5 * u * (1.0 - th * th) * 0.7978845608028654 * (
        1.0 + 3.0 * 0.044715 * u * u
    )
    return value, slope


def three_way(table):
    parts = []
    rest = table
    for _ in range(3):
        piece = lax.reduce_precision(rest, exponent_bits=8, mantissa_bits=7)
        parts.append(piece.astype(bf16))
        rest = rest - piece
    return parts


def axis_table(width):
    quarter = width // 2
    omega = jnp.exp(-math.log(10000.0) * jnp.arange(quarter, dtype=f32) / quarter)
    angles = jnp.arange(GRID_MAX, dtype=f32)[:, None] * omega[None, :]
    return jnp.concatenate([jnp.sin(angles), jnp.cos(angles)], axis=-1)


def time_embed(timesteps, model_width):
    half = model_width // 2
    freqs = jnp.exp(-math.log(10000.0) * jnp.arange(half, dtype=f32) / half)
    angles = timesteps.astype(f32)[:, None] * freqs
    return jnp.concatenate([jnp.cos(angles), jnp.sin(angles)], axis=-1)


def time_columns(timesteps, first, number, model_width):
    half = model_width // 2
    column = first + jnp.arange(number, dtype=jnp.int32)
    freqs = jnp.exp(-math.log(10000.0) * (column % half).astype(f32) / half)
    angles = timesteps[:, None] * freqs
    return jnp.where(column < half, jnp.cos(angles), jnp.sin(angles))


def swap_tiles(value):
    return lax.ppermute(value, "tile", [(0, 1), (1, 0)])


def flip_stage(value, stage, orders, count):
    pairs = []
    for d in range(count):
        for t, order in enumerate(orders):
            pairs.append((2 * d + t, 2 * (d ^ (1 << order[stage])) + t))
    return lax.ppermute(value, ("dp", "tile"), pairs)


def relative_masks(order):
    bits = len(order)
    masks = []
    for rel in range(1 << bits):
        mask = 0
        for stage in range(bits):
            if (rel >> (bits - 1 - stage)) & 1:
                mask |= 1 << order[stage]
        masks.append(mask)
    return masks


def after(value, *others):
    return lax.optimization_barrier((value,) + others)[0]


CHUNK = 3
UNIT = 9
BOTH = {
    "x": (0, 1),
    "y": (1, 0),
    "1": (2, 2),
    "2": (3, 3),
}
PLAN = {
    "d0": "x1y2",
    "d1": "1x2y",
    "u0": "xy12",
    "u1": "xy12",
    "q0": "xy12",
    "q1": "xy12",
}
ORDER = """
Kd0 d0 Kd1 d1 Cp Ct k0 d0 Ku0 u0 Ku1 u1 C1 C2 Cq k1 d1 u0 u1 Kq0 Kq1 u0 q1 C3 d0 d1 u0 q0 u1 C4
q1 s d1 u1 s u0 s q0 q1 u1 d0 d1 s q1 q0 q1 s C5 q0 d0 q0
"""


def unit_orders(plan):
    return tuple([BOTH[c][t] for c in plan] for t in (0, 1))


def dot_rows(left, right):
    return lax.dot_general(left, right, (((1,), (0,)), ((), ())), preferred_element_type=f32)


def halves_kernel(tile_ref, *refs):
    number = len(refs) - 2
    keep_ref, give_ref = refs[-2:]

    def write(own):
        start = 0
        for ref in refs[:number]:
            size = ref.shape[1] // 2
            place = slice(start, start + size)
            keep_ref[:, place] = ref[:, own * size : (own + 1) * size]
            give_ref[:, place] = ref[:, (1 - own) * size : (2 - own) * size].astype(f32)
            start += size
        if start < give_ref.shape[1]:
            rest = give_ref.shape[1] - start
            give_ref[:, start:] = jnp.zeros((give_ref.shape[0], rest), f32)

    for own in (0, 1):
        pl.when(tile_ref[0] == own)(functools.partial(write, own))


def halves(tile, *values):
    rows = values[0].shape[0]
    size = sum(value.shape[1] for value in values) // 2
    padded = -(-size // 128) * 128
    return pl.pallas_call(
        halves_kernel,
        out_shape=(
            jax.ShapeDtypeStruct((rows, size), bf16),
            jax.ShapeDtypeStruct((rows, padded), f32),
        ),
        grid_spec=pltpu.PrefetchScalarGridSpec(
            num_scalar_prefetch=1,
            grid=(1,),
            in_specs=[pl.BlockSpec(value.shape, lambda i, tile: (0, 0)) for value in values],
            out_specs=(
                pl.BlockSpec((rows, size), lambda i, tile: (0, 0)),
                pl.BlockSpec((rows, padded), lambda i, tile: (0, 0)),
            ),
        ),
        cost_estimate=pl.CostEstimate(flops=1, bytes_accessed=1, transcendentals=0),
        compiler_params=pltpu.CompilerParams(vmem_limit_bytes=12 * 2**20),
        name="halves",
    )(tile[None], *values)


def turned(value):
    size = value.shape[1]
    row = lax.broadcasted_iota(jnp.int32, (size, size), 0)
    column = lax.broadcasted_iota(jnp.int32, (size, size), 1)
    identity = jnp.where(row == column, 1.0, 0.0).astype(bf16)
    return dot_columns(identity, value)


def turn_kernel(in_ref, out_ref):
    out_ref[...] = turned(in_ref[...])


def turn(value):
    rows, size = value.shape
    chunk = 384
    return pl.pallas_call(
        turn_kernel,
        out_shape=jax.ShapeDtypeStruct((size, rows), f32),
        grid=(size // chunk,),
        in_specs=[pl.BlockSpec((rows, chunk), lambda j: (0, j))],
        out_specs=pl.BlockSpec((chunk, rows), lambda j: (j, 0)),
        cost_estimate=pl.CostEstimate(flops=1, bytes_accessed=1, transcendentals=0),
        compiler_params=pltpu.CompilerParams(vmem_limit_bytes=5 * 2**20),
        name="turn",
    )(value)


def row_kernel(part, ranges, pair, ids_ref, *refs):
    near = [refs[i][0].astype(bf16) for i in range(pair)]
    far = [refs[pair + i][0].astype(bf16) for i in range(pair)]
    right_ref, right_far_ref = refs[2 * pair : 2 * pair + 2]
    out_refs = refs[2 * pair + 2 :]
    size = near[0].shape[0]
    cut = slice(256, right_ref.shape[1]) if part else slice(0, 256)
    res = dot_rows(jnp.concatenate(near, axis=0), right_ref[:, cut])
    res = res + dot_rows(jnp.concatenate(far, axis=0), right_far_ref[:, cut].astype(bf16))
    rows = size // 4
    step = pl.program_id(0) * pair + ranges[0][0]

    def write(ref, place, base):
        for c in range(2):
            for h in range(4):
                top = base + h * rows
                ref[place, 4 * c + h] = res[top : top + rows, c * 128 : (c + 1) * 128]
        if part:
            for h in range(2):
                top = base + h * rows
                ref[place, 8 + h, :, :64] = res[top : top + rows, 256:]
                top = base + (h + 2) * rows
                ref[place, 8 + h, :, 64:] = res[top : top + rows, 256:]

    for ref, (low, high) in zip(out_refs, ranges):
        block = min(high - low, pair)

        def body(ref=ref, low=low, block=block):
            for i in range(block):
                write(ref, i, (i + (low % pair)) * size)

        pl.when((step + pair > low) & (step < high))(body)


def row_unit(ids, left, left_far, rights, part, ranges):
    _, rows, near = left.shape
    pieces = 8 + 2 * part
    pair = 2
    first, number = ranges[0][0], ranges[-1][1] - ranges[0][0]

    def place(low, high):
        block = min(high - low, pair)
        last = (high - low) // block - 1
        return lambda k, ids: (jnp.clip((k * pair + first - low) // block, 0, last), 0, 0, 0)

    def source(i):
        return pl.BlockSpec((1, rows, near), lambda k, ids: (ids[first + k * pair + i], 0, 0))

    return pl.pallas_call(
        functools.partial(row_kernel, part, ranges, pair),
        out_shape=tuple(
            jax.ShapeDtypeStruct((high - low, pieces, rows // 4, 128), f32) for low, high in ranges
        ),
        grid_spec=pltpu.PrefetchScalarGridSpec(
            num_scalar_prefetch=1,
            grid=(number // pair,),
            in_specs=[source(i % pair) for i in range(2 * pair)]
            + [
                pl.BlockSpec((near, item.shape[1]), lambda k, ids: (0, 0)) for item in rights
            ],
            out_specs=tuple(
                pl.BlockSpec((min(high - low, pair), pieces, rows // 4, 128), place(low, high))
                for low, high in ranges
            ),
        ),
        cost_estimate=pl.CostEstimate(flops=1, bytes_accessed=1, transcendentals=0),
        compiler_params=pltpu.CompilerParams(vmem_limit_bytes=14 * 2**20),
        name="row_unit",
    )(ids, *[left] * pair, *[left_far] * pair, *rights)


def column_kernel(border, first_tile, ranges, number, ids_ref, *refs):
    lefts, (right_ref, right_far_ref) = refs[: 2 * number], refs[2 * number : 2 * number + 2]
    out_refs, stack_ref = refs[2 * number + 2 : -1], refs[-1]
    count, rows, near = lefts[0].shape
    half = count // 2 * rows
    step = pl.program_id(0)

    @pl.when(step == 0)
    def _():
        for i in range(number):
            for r in range(count):
                place = pl.ds(r * rows, rows)
                stack_ref[i, place, :near] = lefts[2 * i][ids_ref[r]].astype(bf16)
                stack_ref[i, place, near:] = lefts[2 * i + 1][ids_ref[r]].astype(bf16)

    right = jnp.concatenate([right_ref[...], right_far_ref[...].astype(bf16)], axis=0)

    def write(kind):
        for base in (half, 0):
            stack = [stack_ref[i, base : base + half] for i in range(number)]
            if kind == "first":
                res = dot_rows(stack[0], right)
            elif kind == "last":
                res = dot_rows(stack[1], right)
            else:
                start = (step * CHUNK + first_tile) * 128
                column = lax.broadcasted_iota(jnp.int32, (half, CHUNK * 128), 1) + start
                res = jnp.where(
                    column < border, dot_rows(stack[0], right), dot_rows(stack[1], right)
                )
            for ref, (low, high) in zip(out_refs, ranges):
                if base <= low * rows < base + half:
                    for r in range(low, high):
                        top = r * rows - base
                        for c in range(CHUNK):
                            ref[r - low, c] = res[top : top + rows, c * 128 : (c + 1) * 128]

    if number == 1:
        write("first")
    else:
        begin = (step * CHUNK + first_tile) * 128
        end = begin + CHUNK * 128

        @pl.when(end <= border)
        def _():
            write("first")

        @pl.when(begin >= border)
        def _():
            write("last")

        @pl.when((end > border) & (begin < border))
        def _():
            write("mixed")


def column_unit(ids, lefts, right, right_far, part, border, ranges):
    count, rows, near = lefts[0].shape
    first_tile = part * UNIT
    first_chunk = first_tile // CHUNK
    whole = pl.BlockSpec((count, rows, near), lambda j, ids: (0, 0, 0))
    chunk = pl.BlockSpec((near, CHUNK * 128), lambda j, ids: (0, first_chunk + j))
    number = len(lefts) // 2
    return pl.pallas_call(
        functools.partial(column_kernel, border, first_tile, ranges, number),
        out_shape=tuple(
            pltpu.HBM((high - low, UNIT, rows, 128), f32) for low, high in ranges
        ),
        grid_spec=pltpu.PrefetchScalarGridSpec(
            num_scalar_prefetch=1,
            grid=(UNIT // CHUNK,),
            in_specs=[whole] * len(lefts) + [chunk, chunk],
            out_specs=tuple(
                pl.BlockSpec((high - low, CHUNK, rows, 128), lambda j, ids: (0, j, 0, 0))
                for low, high in ranges
            ),
            scratch_shapes=[pltpu.VMEM((number, count * rows, 2 * near), bf16)],
        ),
        cost_estimate=pl.CostEstimate(flops=1, bytes_accessed=1, transcendentals=0),
        compiler_params=pltpu.CompilerParams(vmem_limit_bytes=(10 + 8 * number) * 2**20),
        name="column_unit",
    )(ids, *lefts, right, right_far)


SENDS = ((8, 16),)
KEEPS = ((0, 1), (1, 2), (2, 4), (4, 8))


PIECE = 512


def in_hbm(value):
    return pltpu.with_memory_space_constraint(value, pltpu.HBM)


def up_kernel(in_ref, weight_ref, bias_ref, act_ref, slope_ref, turned_ref):
    for low in range(0, PIECE, 256):
        place = slice(low, low + 256)
        pre = dot_rows(in_ref[...], weight_ref[:, place]) + bias_ref[:, place]
        value, slope = gelu_parts(pre)
        value = value.astype(bf16)
        act_ref[:, place] = value
        slope_ref[:, place] = slope
        turned_ref[place, :] = value.T.astype(f32)


def feed_up(value, weight, bias):
    rows, width = value.shape
    hidden = weight.shape[1]
    return pl.pallas_call(
        up_kernel,
        out_shape=(
            jax.ShapeDtypeStruct((rows, hidden), bf16),
            jax.ShapeDtypeStruct((rows, hidden), f32),
            jax.ShapeDtypeStruct((hidden, rows), f32),
        ),
        grid=(hidden // PIECE,),
        in_specs=[
            pl.BlockSpec((rows, width), lambda j: (0, 0)),
            pl.BlockSpec((width, PIECE), lambda j: (0, j)),
            pl.BlockSpec((1, PIECE), lambda j: (0, j)),
        ],
        out_specs=(
            pl.BlockSpec((rows, PIECE), lambda j: (0, j)),
            pl.BlockSpec((rows, PIECE), lambda j: (0, j)),
            pl.BlockSpec((PIECE, rows), lambda j: (j, 0)),
        ),
        cost_estimate=pl.CostEstimate(flops=1, bytes_accessed=1, transcendentals=0),
        compiler_params=pltpu.CompilerParams(vmem_limit_bytes=11 * 2**20),
        name="feed_up",
    )(value, weight, bias[None].astype(f32))


def down_back_kernel(grad_ref, weight_ref, slope_ref, out_ref):
    out_ref[...] = (dot_columns(grad_ref[...], weight_ref[...]) * slope_ref[...]).astype(bf16)


def feed_back(grad, weight, slope):
    rows, width = grad.shape
    hidden = weight.shape[0]
    return pl.pallas_call(
        down_back_kernel,
        out_shape=jax.ShapeDtypeStruct((rows, hidden), bf16),
        grid=(hidden // PIECE,),
        in_specs=[
            pl.BlockSpec((rows, width), lambda j: (0, 0)),
            pl.BlockSpec((PIECE, width), lambda j: (j, 0)),
            pl.BlockSpec((rows, PIECE), lambda j: (0, j)),
        ],
        out_specs=pl.BlockSpec((rows, PIECE), lambda j: (0, j)),
        cost_estimate=pl.CostEstimate(flops=1, bytes_accessed=1, transcendentals=0),
        compiler_params=pltpu.CompilerParams(vmem_limit_bytes=8 * 2**20),
        name="feed_back",
    )(grad, in_hbm(weight), slope)


def head_window(head, size, width):
    start = jnp.minimum(head * size // 128 * 128, width - 256)
    return pl.multiple_of(start, 128), head * size - start


def each_head(body):
    def group(step, carry):
        for i in range(16):
            body(16 * step + i)
        return carry

    lax.fori_loop(0, HEADS // 16, group, 0)


def head_mask(low, size):
    lane = lax.broadcasted_iota(jnp.int32, (1, 256), 1)
    return (lane >= low) & (lane < low + size)


def dot_columns(left, right):
    return lax.dot_general(left, right, (((1,), (1,)), ((), ())), preferred_element_type=f32)


def head_probs(queries, keys, mask, live, scaling):
    masked = queries * mask.astype(f32).astype(bf16)
    scores = jnp.where(live > 0.0, dot_columns(masked, keys) * scaling, -1e30)
    powers = jnp.exp(scores - jnp.max(scores, axis=1, keepdims=True))
    return powers / jnp.sum(powers, axis=1, keepdims=True)


def attend_kernel(qkv_ref, live_ref, out_ref, total_ref):
    width = out_ref.shape[1]
    size = width // HEADS
    live = live_ref[0]

    def one(head):
        start, low = head_window(head, size, width)
        mask = head_mask(low, size)
        queries, keys, values = [
            qkv_ref[:, pl.ds(part * width + start, 256)] for part in range(3)
        ]
        probs = head_probs(queries, keys, mask, live, size ** (-0.5)).astype(bf16)
        mixed = dot_rows(probs, values)
        place = pl.ds(start, 256)
        total_ref[:, place] = jnp.where(mask, mixed, total_ref[:, place])

    each_head(one)
    out_ref[...] = total_ref[...].astype(bf16)


def attend(qkv, live):
    rows, wide = qkv.shape
    images = live.shape[0]
    near = rows // images
    width = wide // 3
    return pl.pallas_call(
        attend_kernel,
        out_shape=jax.ShapeDtypeStruct((rows, width), bf16),
        grid=(images,),
        in_specs=[
            pl.BlockSpec((near, wide), lambda i: (i, 0)),
            pl.BlockSpec((1, 1, near), lambda i: (i, 0, 0)),
        ],
        out_specs=pl.BlockSpec((near, width), lambda i: (i, 0)),
        scratch_shapes=[pltpu.VMEM((near, width), f32)],
        cost_estimate=pl.CostEstimate(flops=1, bytes_accessed=1, transcendentals=0),
        compiler_params=pltpu.CompilerParams(vmem_limit_bytes=8 * 2**20),
        name="attend",
    )(qkv, live)


def attend_back_kernel(qkv_ref, live_ref, grad_ref, out_ref, total_ref):
    width = grad_ref.shape[1]
    size = width // HEADS
    scaling = size ** (-0.5)
    live = live_ref[0]

    def one(head):
        start, low = head_window(head, size, width)
        mask = head_mask(low, size)
        queries, keys, values = [
            qkv_ref[:, pl.ds(part * width + start, 256)] for part in range(3)
        ]
        grads = grad_ref[:, pl.ds(start, 256)]
        probs = head_probs(queries, keys, mask, live, scaling)
        d_probs = dot_columns(grads * mask.astype(f32).astype(bf16), values)
        delta = jnp.sum(probs * d_probs, axis=1, keepdims=True)
        d_scores = probs * (d_probs - delta)
        pieces = (
            dot_rows(d_scores.astype(bf16), keys) * scaling,
            dot_rows(d_scores.T.astype(bf16), queries) * scaling,
            dot_rows(probs.T.astype(bf16), grads),
        )
        for part, piece in enumerate(pieces):
            place = pl.ds(part * width + start, 256)
            total_ref[:, place] = jnp.where(mask, piece, total_ref[:, place])

    each_head(one)
    out_ref[...] = total_ref[...].astype(bf16)


def attend_back(qkv, live, grad):
    rows, wide = qkv.shape
    images = live.shape[0]
    near = rows // images
    width = wide // 3
    return pl.pallas_call(
        attend_back_kernel,
        out_shape=jax.ShapeDtypeStruct((rows, wide), bf16),
        grid=(images,),
        in_specs=[
            pl.BlockSpec((near, wide), lambda i: (i, 0)),
            pl.BlockSpec((1, 1, near), lambda i: (i, 0, 0)),
            pl.BlockSpec((near, width), lambda i: (i, 0)),
        ],
        out_specs=pl.BlockSpec((near, wide), lambda i: (i, 0)),
        scratch_shapes=[pltpu.VMEM((near, wide), f32)],
        cost_estimate=pl.CostEstimate(flops=1, bytes_accessed=1, transcendentals=0),
        compiler_params=pltpu.CompilerParams(vmem_limit_bytes=12 * 2**20),
        name="attend_back",
    )(qkv, live, grad)


def join_kernel(lines, mine_ref, got_ref, out_ref):
    rest = mine_ref.shape[0] - lines
    out_ref[:lines] = mine_ref[:lines] + got_ref[:lines]
    out_ref[lines : lines + rest] = mine_ref[lines:]
    out_ref[lines + rest :] = got_ref[lines:]


def join(mine, got, lines):
    rows, lanes = mine.shape
    return pl.pallas_call(
        functools.partial(join_kernel, lines),
        out_shape=jax.ShapeDtypeStruct((2 * rows - lines, lanes), f32),
        cost_estimate=pl.CostEstimate(flops=1, bytes_accessed=1, transcendentals=0),
        compiler_params=pltpu.CompilerParams(vmem_limit_bytes=8 * 2**20),
        name="join",
    )(mine, got)


class Halving:
    def __init__(self, orders, count):
        self.orders = orders
        self.count = count
        self.stages = len(orders[0])
        self.message = None
        self.keeps = None
        self.received = []

    def lined(self, blocks):
        return blocks.reshape(-1, blocks.shape[1] * blocks.shape[2], 128)

    def sends(self, blocks):
        self.message = self.lined(blocks)
        return blocks

    def holds(self, blocks):
        self.keeps = [self.lined(item) for item in blocks]
        return blocks[-1]

    def step(self, token):
        stage = len(self.received)
        if stage:
            self.received[-1] = after(self.received[-1], token)
        if stage == self.stages:
            message = self.keeps[0][0]
            for piece in self.received:
                message = message + piece[0]
            self.message = message
            return message
        if stage:
            low = 1 << (self.stages - 1 - stage)
            message = self.keeps[self.stages - stage]
            for piece in self.received:
                message = message + piece[low : 2 * low]
        else:
            message = after(self.message, token)
        self.received.append(flip_stage(message, stage, self.orders, self.count))
        return message

    def result(self, rows):
        return self.message.reshape(-1, rows, 128)


def body(
    patches,
    bucket,
    keep_order,
    timesteps,
    labels,
    patch_weight,
    patch_bias,
    class_table,
    ada_weight,
    ada_bias,
    qkv_weight,
    query_bias,
    value_bias,
    proj_weight,
    proj_bias,
    up_weight,
    up_bias,
    down_weight,
    down_bias,
    final_weight,
    final_bias,
    out_grad,
):
    images, tile_slots, patch_width = patches.shape
    slot_total = keep_order.shape[1]
    width = patch_weight.shape[1]
    hidden = up_weight.shape[1]
    class_count = class_table.shape[0]
    count = lax.axis_size("dp")
    bits = count.bit_length() - 1
    tile = lax.axis_index("tile")
    own = images // 2
    half_slots = slot_total // 2
    first = tile * own

    def mine(value):
        return lax.dynamic_slice_in_dim(value, first, own, 0)

    def others(value):
        return lax.dynamic_slice_in_dim(value, own - first, own, 0)

    unit = (bucket[0] >= 0).astype(f32)

    pair = jnp.concatenate([patches, out_grad], axis=2).astype(f32)
    slots_data = jnp.concatenate([mine(pair), swap_tiles(others(pair)) * unit], axis=1).astype(bf16)
    near = jnp.arange(slot_total, dtype=jnp.int32)
    slot_ids = (near + tile * tile_slots) % slot_total

    condition = time_embed(timesteps, width) + jnp.take(class_table, labels, axis=0).astype(f32)
    cond_act = jax.nn.silu(condition).astype(bf16)
    mod_half = mm("id,de->ie", cond_act, ada_weight) + ada_bias.astype(f32)
    mod_mine, mod_recv = mine(mod_half), swap_tiles(others(mod_half))
    modulation = jnp.where(
        tile == 0,
        jnp.concatenate([mod_mine, mod_recv], axis=1),
        jnp.concatenate([mod_recv, mod_mine], axis=1),
    )
    shift_a, scale_a, gate_a, shift_m, scale_m, gate_m = [
        portion[:, None, :] for portion in jnp.split(modulation, 6, axis=1)
    ]

    my_bucket, my_order = mine(bucket), mine(keep_order)
    half_rows = jnp.where(my_bucket == 0, 8, jnp.where(my_bucket == 1, 6, 10))[:, None]
    columns = jnp.where(my_bucket == 0, 16, jnp.where(my_bucket == 1, 20, 12))[:, None]
    area = half_rows * columns
    order_valid = (my_order % tile_slots) < area
    upper = (near[:, None] < near[None, :]).astype(bf16)
    rank = mm("ij,jk->ik", order_valid.astype(bf16), upper).astype(jnp.int32)
    limit = area
    place = jnp.where(rank < limit, rank, rank - limit + half_slots)
    hit = (place[:, None, :] == near[None, :, None]) & order_valid[:, None, :]
    row_slot = jnp.sum(jnp.where(hit, my_order[:, None, :] + 1, 0), axis=2) - 1
    live = row_slot >= 0
    select = (row_slot[:, :, None] == slot_ids[None, None, :]).astype(bf16)
    row_data = mm("irs,isc->irc", select, slots_data).astype(bf16)
    row_patches, row_grads = row_data[:, :, :patch_width], row_data[:, :, patch_width:]
    local = row_slot % tile_slots
    grid_row = (row_slot // tile_slots) * half_rows + local // columns
    grid_col = local % columns
    marks = jnp.arange(GRID_MAX, dtype=jnp.int32)
    mark_row = (grid_row[:, :, None] == marks).astype(bf16)
    mark_col = (grid_col[:, :, None] == marks).astype(bf16)
    table = three_way(axis_table(width // 2))
    blank = jnp.zeros((GRID_MAX, width // 2), bf16)
    wide = jnp.concatenate(
        [patch_weight]
        + [jnp.concatenate([piece, blank], axis=1) for piece in table]
        + [jnp.concatenate([blank, piece], axis=1) for piece in table],
        axis=0,
    )
    features = jnp.concatenate([row_patches] + [mark_row] * 3 + [mark_col] * 3, axis=2)
    embedded = mm("irk,kd->ird", features, wide) + patch_bias.astype(f32)
    key_live = live[:, :half_slots]

    fast = count == 16 and (width // count) % 8 == 0 and images * slot_total == 1024
    index = lax.axis_index("dp")

    def unit_ids(orders):
        masks = [jnp.array(relative_masks(order), jnp.int32) for order in orders]
        return jnp.where(tile == 0, masks[0], masks[1]) ^ index

    def left_blocks(left):
        rows, size = left.shape[0] * left.shape[1], left.shape[2]
        flat = left.reshape(rows, size)
        blocks = turn(flat) if fast else flat.astype(f32).T
        blocks = blocks.reshape(count, size // count, rows)
        return blocks, swap_tiles(blocks)

    def right_half(*rights):
        if fast:
            keep, give = halves(tile, *[right.reshape(-1, right.shape[2]) for right in rights])
            return keep, swap_tiles(give), give
        keep, give = [], []
        for right in rights:
            size = right.shape[2] // 2
            flat = right.reshape(-1, 2 * size)
            low, high = flat[:, :size], flat[:, size:]
            keep.append(jnp.where(tile == 0, low, high))
            give.append(jnp.where(tile == 0, high, low).astype(f32))
        keep, give = jnp.concatenate(keep, axis=1), jnp.concatenate(give, axis=1)
        return keep, swap_tiles(give), give

    def plain(left, right):
        (near_left, far_left), (near_right, far_right) = left, right
        near_left = near_left.astype(bf16)
        far_left, far_right = (far_left * unit).astype(bf16), (far_right * unit).astype(bf16)
        grad = mm("brk,kc->brc", near_left, near_right) + mm("brk,kc->brc", far_left, far_right)
        grad = grad.reshape(-1, grad.shape[2])
        return lax.psum_scatter(grad, "dp", scatter_dimension=0, tiled=True)

    chains, tables = {}, {}
    for name, plan in PLAN.items():
        if fast:
            orders = unit_orders(plan)
            chains[name] = Halving(orders, count)
            if plan not in tables:
                tables[plan] = unit_ids(orders)
    todo = ORDER.split()
    token = [keep_order]
    small = []

    def gate(value):
        return after(value, token[0]) if fast else value

    def passed(value):
        token[0] = value
        return value

    def small_step():
        orders = list(range(2, bits))[::-1]
        orders = (orders + [0, 1], orders + [1, 0])
        stage, message = small[0], small[1]
        if stage:
            got = gate(small[2])
            lines = small[3]
            if fast:
                message = join(message, got, lines)
            else:
                message = jnp.concatenate(
                    [message[:lines] + got[:lines], message[lines:], got[lines:]], axis=0
                )
        else:
            message = gate(message)
        small[0], small[1] = stage + 1, message
        if stage < bits:
            small[2] = flip_stage(message, stage, orders, count)
        passed(message)

    def reach(block):
        while todo[0] != block:
            event = todo.pop(0)
            if event == "s":
                small_step()
            elif event[0] == "k":
                part = int(event[1])
                passed(chains["d%d" % part].holds(down_unit(part, KEEPS)))
            else:
                passed(chains[event].step(token[0]))
        todo.pop(0)

    def table(name):
        return gate(tables[PLAN[name]])

    def down_unit(part, ranges):
        return row_unit(table("d%d" % part), *down_left, down_right, part, ranges)

    def whole_unit(name, lefts, right, part, border):
        send, *keeps = column_unit(table(name), lefts, *right, part, border, SENDS + KEEPS)
        chains[name].holds(keeps)
        return passed(chains[name].sends(send))

    kept_x = embedded[:, :half_slots]
    normed_a, rstd_a = norm_stats(kept_x)
    attn_in = (normed_a * (1.0 + scale_a) + shift_a).astype(bf16)
    qkv_bias = jnp.concatenate([query_bias, jnp.zeros_like(query_bias), value_bias]).astype(f32)
    qkv = (mm("isd,de->ise", attn_in, qkv_weight) + qkv_bias).astype(bf16)
    qkv = qkv.reshape(own * half_slots, -1)
    live_row = key_live.astype(f32)[:, None, :]
    mixed = attend(qkv, live_row).reshape(own, half_slots, width)
    attn_out = mm("iqd,de->iqe", mixed, proj_weight) + proj_bias.astype(f32)
    middle = kept_x + gate_a * attn_out
    normed_m, rstd_m = norm_stats(middle)
    mlp_in = (normed_m * (1.0 + scale_m) + shift_m).astype(bf16)
    rows = own * half_slots
    activated, act_slope, blocks = feed_up(mlp_in.reshape(rows, width), up_weight, up_bias)
    blocks = blocks.reshape(count, hidden // count, rows)
    down_left = (blocks, swap_tiles(blocks))
    activated = activated.reshape(own, half_slots, hidden)
    mlp_out = mm("iqf,fd->iqd", activated, down_weight) + down_bias.astype(f32)
    block_out = middle + gate_m * mlp_out
    merged = jnp.concatenate([block_out, embedded[:, half_slots:]], axis=1)
    normed_f, rstd_f = norm_stats(merged)
    final_in = normed_f.astype(bf16)

    d_final = mm("isp,dp->isd", row_grads, final_weight)
    d_merged = norm_back(normed_f, rstd_f, d_final)
    d_block = d_merged[:, :half_slots]
    d_mlp = (gate_m * d_block).astype(bf16)
    d_gate_m = jnp.sum(d_block * mlp_out, axis=1)

    *down_right, give = right_half(d_mlp)
    d_mlp = after(d_mlp, give)
    if fast:
        passed(give)
        up_left = left_blocks(gate(mlp_in))
        passed(up_left[0])
        reach("Kd0")
        passed(chains["d0"].sends(down_unit(0, SENDS)[0]))
        reach("Kd1")
        passed(chains["d1"].sends(down_unit(1, SENDS)[0]))
        reach("Cp")
    d_pre = feed_back(gate(d_mlp).reshape(rows, width), down_weight, act_slope)
    d_pre = passed(d_pre.reshape(own, half_slots, hidden))
    if fast:
        *up_right, give = right_half(d_pre)
        passed(give)
        reach("Ct")
        proj_left, qkv_left = left_blocks(gate(mixed)), left_blocks(gate(attn_in))
        passed(qkv_left[0])
        reach("Ku0")
        whole_unit("u0", up_left, up_right, 0, None)
        reach("Ku1")
        whole_unit("u1", up_left, up_right, 1, None)
        reach("C1")
    else:
        down_final = plain(down_left, down_right)
        up_final = plain(left_blocks(mlp_in), right_half(d_pre)[:2])
    d_mlp_in = mm("iqf,df->iqd", gate(d_pre), up_weight)
    d_shift_m = jnp.sum(d_mlp_in, axis=1)
    d_scale_m = jnp.sum(d_mlp_in * normed_m, axis=1)
    d_middle = d_block + norm_back(normed_m, rstd_m, d_mlp_in * (1.0 + scale_m))
    d_attn = passed((gate_a * d_middle).astype(bf16))
    d_gate_a = jnp.sum(d_middle * attn_out, axis=1)
    if fast:
        reach("C2")
    else:
        proj_left, qkv_left = left_blocks(mixed), left_blocks(attn_in)
    d_mixed = mm("iqe,de->iqd", gate(d_attn), proj_weight).astype(bf16)
    d_qkv = attend_back(qkv, live_row, d_mixed.reshape(own * half_slots, width))
    d_qkv = passed(d_qkv.reshape(own, half_slots, 3 * width))
    border = d_qkv.shape[2] // 2
    if fast:
        reach("Cq")
        *both_right, give = right_half(gate(d_qkv), d_attn)
        passed(give)
        reach("Kq0")
        whole_unit("q0", qkv_left, both_right, 0, border)
        reach("Kq1")
        whole_unit("q1", qkv_left + proj_left, both_right, 1, border)
        reach("C3")
    else:
        proj_final = plain(proj_left, right_half(d_attn)[:2])
        qkv_final = plain(qkv_left, right_half(d_qkv)[:2])
    d_qkv = gate(d_qkv)
    qkv_bias_sums = jnp.sum(d_qkv.astype(f32), axis=(0, 1))
    d_attn_in = mm("ice,de->icd", d_qkv, qkv_weight)
    d_shift_a = jnp.sum(d_attn_in, axis=1)
    d_scale_a = jnp.sum(d_attn_in * normed_a, axis=1)
    d_kept = passed(d_middle + norm_back(normed_a, rstd_a, d_attn_in * (1.0 + scale_a)))
    if fast:
        reach("C4")
    d_kept, d_merged, final_in = gate(d_kept), gate(d_merged), gate(final_in)
    proj_bias_grad = jnp.sum(gate(d_attn).astype(f32), axis=(0, 1))
    up_bias_grad = jnp.sum(gate(d_pre).astype(f32), axis=(0, 1))
    down_bias_grad = jnp.sum(gate(d_mlp).astype(f32), axis=(0, 1))
    row_denoised = mm("isd,dp->isp", final_in, final_weight) + final_bias.astype(f32)
    final_weight_grad = mm("isd,isp->dp", final_in, row_grads)
    final_bias_grad = jnp.sum(row_grads.astype(f32), axis=(0, 1))
    d_low = jnp.concatenate([d_kept, d_merged[:, half_slots:]], axis=1).astype(bf16)
    row_patch_grad = mm("isd,pd->isp", d_low, patch_weight)
    patch_weight_grad = mm("isp,isd->pd", row_patches, d_low)
    patch_bias_grad = jnp.sum(d_low.astype(f32), axis=(0, 1))

    back = jnp.concatenate([row_denoised, row_patch_grad], axis=2)
    slot_out = mm("irs,irc->isc", select, jnp.concatenate(three_way(back), axis=2))
    slot_out = sum(jnp.split(slot_out, 3, axis=2))
    near_part, far_part = slot_out[:, :tile_slots], swap_tiles(slot_out[:, tile_slots:])
    slot_mine = jnp.where(
        tile == 0,
        jnp.concatenate([near_part, far_part], axis=0),
        jnp.concatenate([far_part, near_part], axis=0),
    )
    denoised, patch_grad = slot_mine[:, :, :patch_width], slot_mine[:, :, patch_width:]

    d_mod = jnp.concatenate(
        [d_shift_a, d_scale_a, d_gate_a, d_shift_m, d_scale_m, d_gate_m], axis=1
    )
    mod_width = d_mod.shape[1] // 2
    keep = lax.dynamic_slice_in_dim(d_mod, tile * mod_width, mod_width, 1)
    give = lax.dynamic_slice_in_dim(d_mod, (1 - tile) * mod_width, mod_width, 1)
    got = swap_tiles(give) * unit
    d_mod_half = jnp.where(
        tile == 0, jnp.concatenate([keep, got], axis=0), jnp.concatenate([got, keep], axis=0)
    ).astype(bf16)
    d_cond_act = mm("ie,de->id", d_mod_half, ada_weight)
    gated = jax.nn.sigmoid(condition)
    d_cond_part = d_cond_act * (gated * (1.0 + condition * (1.0 - gated)))
    d_condition = d_cond_part + swap_tiles(d_cond_part)

    sums_of = [
        patch_weight_grad,
        patch_bias_grad,
        qkv_bias_sums[:width],
        qkv_bias_sums[2 * width :],
        proj_bias_grad,
        up_bias_grad,
        down_bias_grad,
        final_weight_grad,
        final_bias_grad,
    ]
    area_all = jnp.where(bucket == 0, 128, 120)
    counts_local = jnp.stack([jnp.sum(area_all), jnp.sum(2 * area_all)]).astype(f32) * 0.5
    sums_of.append(counts_local)
    flat = jnp.concatenate([leaf.reshape(-1) for leaf in sums_of])
    flat = jnp.pad(flat, (0, (-flat.shape[0]) % 2048)).reshape(2, -1, 128)
    flat_half = lax.dynamic_index_in_dim(flat, tile, 0, keepdims=False) + swap_tiles(
        lax.dynamic_index_in_dim(flat, 1 - tile, 0, keepdims=False)
    )
    lines = flat_half.shape[0]
    marks = jnp.stack([labels, timesteps], axis=1).astype(f32)
    packed = jnp.concatenate(
        [d_mod_half.astype(f32), d_condition, jnp.pad(marks, ((0, 0), (0, 126)))], axis=1
    )
    message = passed(jnp.concatenate([flat_half, packed.reshape(-1, 128)], axis=0))
    small.extend([0, message, None, lines])
    if fast:
        reach("C5")
    else:
        for _ in range(bits + 1):
            small_step()
    message = small[1]

    every = (message[lines:] * unit).reshape(count * images, -1)
    all_mod = every[:, :mod_width].astype(bf16)
    all_cond = every[:, mod_width : mod_width + width]
    all_label = every[:, mod_width + width].astype(jnp.int32)
    all_time = every[:, mod_width + width + 1]
    one_hot = (all_label[:, None] == jnp.arange(class_count, dtype=jnp.int32)[None, :])
    block = width // count
    table_rows = lax.dynamic_slice_in_dim(class_table, index * block, block, 1)
    picked = mm("nc,cd->nd", one_hot.astype(bf16), table_rows)
    act_rows = time_columns(all_time, index * block, block, width) + picked
    act_rows = jax.nn.silu(act_rows).astype(bf16)
    ada_final = mm("nd,ne->de", act_rows, all_mod)
    ada_half = jnp.sum(all_mod.astype(f32), axis=0)
    ending = jnp.concatenate([message[:lines], ada_half.reshape(-1, 128)], axis=0)
    other = swap_tiles(ending)
    first_end = jnp.where(tile == 0, ending, other)
    second_end = jnp.where(tile == 0, other, ending)
    ada_bias_sum = jnp.concatenate(
        [first_end[lines:].reshape(-1), second_end[lines:].reshape(-1)]
    )
    summed = jnp.concatenate([first_end[:lines].reshape(-1), second_end[:lines].reshape(-1)])
    sums = []
    offset = 0
    for leaf in sums_of:
        sums.append(summed[offset : offset + leaf.size].reshape(leaf.shape))
        offset += leaf.size
    class_table_sum = mm(
        "nc,nd->cd",
        jnp.concatenate([one_hot.astype(bf16)] * 3, axis=0),
        jnp.concatenate(three_way(all_cond), axis=0),
    )

    if fast:
        todo.append("end")
        reach("end")
        part_rows = width // count
        first_part, second_part = [chains[name].result(part_rows) for name in ("d0", "d1")]
        wide = [
            item[:8].reshape(2, 4, part_rows, 128).transpose(1, 2, 0, 3).reshape(-1, 256)
            for item in (first_part, second_part)
        ]
        rest = second_part[8:]
        rest = jnp.concatenate(
            [rest[0, :, :64], rest[1, :, :64], rest[0, :, 64:], rest[1, :, 64:]], axis=0
        )
        down_final = jnp.concatenate(wide + [rest], axis=1)

        def columns_of(name):
            tiles = [chains[name + part].result(part_rows) for part in "01"]
            tiles = jnp.concatenate(tiles)
            return tiles.transpose(1, 0, 2).reshape(tiles.shape[1], -1)

        up_final = columns_of("u")
        joint = columns_of("q")
        qkv_final, proj_final = joint[:, :border], joint[:, border:]
    (
        patch_weight_sum,
        patch_bias_sum,
        query_bias_sum,
        value_bias_sum,
        proj_bias_sum,
        up_bias_sum,
        down_bias_sum,
        final_weight_sum,
        final_bias_sum,
        token_counts,
    ) = sums
    return (
        denoised,
        patch_grad,
        patch_weight_sum,
        patch_bias_sum,
        class_table_sum,
        ada_final,
        ada_bias_sum,
        qkv_final,
        query_bias_sum,
        value_bias_sum,
        proj_final,
        proj_bias_sum,
        up_final,
        up_bias_sum,
        down_final,
        down_bias_sum,
        final_weight_sum,
        final_bias_sum,
        token_counts,
    )


def solution(mesh):
    in_specs = (
        P("dp", "tile", None),
        P("dp"),
        P("dp", None),
        P("dp"),
        P("dp"),
        P(),
        P(),
        P(),
        P(None, "tile"),
        P("tile"),
        P(),
        P(),
        P(),
        P(),
        P(),
        P(),
        P(),
        P(),
        P(),
        P(),
        P(),
        P("dp", "tile", None),
    )
    out_specs = (
        P("dp", "tile", None),
        P("dp", "tile", None),
        P(),
        P(),
        P(),
        P("dp", "tile"),
        P(),
        P("dp", "tile"),
        P(),
        P(),
        P("dp", "tile"),
        P(),
        P("dp", "tile"),
        P(),
        P("dp", "tile"),
        P(),
        P(),
        P(),
        P(),
    )
    return jax.shard_map(body, mesh=mesh, in_specs=in_specs, out_specs=out_specs, check_vma=False)
```
